32 devices in a mesh: dp: 4 (over y, core), ctx: 8 (over z, x).
Axes of the slice: x: 2, y: 2, z: 4, core: 2. Of those that a mesh axis runs over, the one named last changes fastest.
Arguments:
- hidden_in: bfloat16 [8, 1024, 768], P('dp', 'ctx'), may hold values from -6 to 6
- grad_out: bfloat16 [8, 1024, 768], P('dp', 'ctx'), may hold values from -8 to 8
- segment_ids: int32 [8, 1024], P('dp', 'ctx'), may hold values from 0 to 7, never falling along the last dimension, each value on 1 to 768 neighbouring positions
- w_qkv: float32 [768, 2304], P('dp'), may hold values from -0.21875 to 0.21875
- w_out: float32 [768, 768], P('dp'), may hold values from -1.75 to 1.75
- w_in: float32 [768, 2304], P('dp'), may hold values from -0.21875 to 0.21875
- w_down: float32 [1152, 768], P(None, 'dp'), may hold values from -0.1875 to 0.1875
- gain_attn: float32 [768], P('dp'), may hold values from 0.1 to 1.9
- gain_mlp: float32 [768], P('dp'), may hold values from 0.1 to 1.9
Outputs:
- layer_out: bfloat16 [8, 1024, 768], P('dp', 'ctx')
- grad_in: bfloat16 [8, 1024, 768], P('dp', 'ctx')
- g_w_qkv: float32 [768, 2304], P('dp')
- g_w_out: float32 [768, 768], P('dp')
- g_w_in: float32 [768, 2304], P('dp')
- g_w_down: float32 [1152, 768], P(None, 'dp')
- g_gain_attn: float32 [768], P('dp')
- g_gain_mlp: float32 [768], P('dp')
The draws below stay inside these ranges and needn't reach their ends.
Inputs may be any that keep to these rules, and one draw needn't show every extreme that they name: `segment_ids`: ids never fall along a sequence; a document has at most (3072) // 4 tokens, and one document of each sequence has exactly that many.
All inputs are finite; a program needn't handle non-finite values.
Results may differ from the reference program's by a relative error of at most 0.018.
Values may be sent and summed in bfloat16 or wider, within the bound.
No kernel may reach another device: no remote copies, remote signals or barrier semaphores. Data moves between devices by JAX's collectives and lax.ppermute only.
A program may use at most 320 MiB of HBM per device.

```python
import math
import jax
import jax.numpy as jnp
import numpy as np
from jax import lax

D = 768
HEADS = 12
HD = 64
FF = 1152
LEN = 1024
SEQS = 8


def with_spikes(array, key, source, target, shards_of, factor):
    def block_of(axis_at):
        return (jnp.arange(array.shape[axis_at]) // (array.shape[axis_at] // shards_of)).reshape((-1,) + (1,) * (array.ndim - 1 - axis_at))

    one_side = jax.random.permutation(key, shards_of)[block_of(target)]
    other_side = (block_of(target) + shards_of // 2) % shards_of
    return jnp.where((block_of(source) == one_side) | (block_of(source) == other_side), factor * array, array)


def shard_levels(stream_key, dims, split, low, top_value):
    level = 1.0
    for position, shards_of in split:
        steps = jax.random.uniform(jax.random.fold_in(jax.random.fold_in(stream_key, 6), position), (shards_of,), jnp.float32, low / len(split), top_value / len(split))
        level = level * jnp.repeat(jnp.exp(steps), dims[position] // shards_of).reshape((-1,) + (1,) * (len(dims) - 1 - position))
    return level


def profile(count, total, reach, slope):
    portions = [(1 << 20) // math.isqrt(grade ** slope) + 1 for grade in range(2, count + 1)]
    surplus, holding = total - reach - (count - 1), [1] * (count - 1)
    while surplus > 0:
        movable = [i for i in range(count - 1) if holding[i] < reach]
        whole, budget = sum([portions[i] for i in movable]), surplus
        for i in movable:
            more = min(reach - holding[i], max(1, budget * portions[i] // whole), surplus)
            holding[i] = holding[i] + more
            surplus = surplus - more
    return np.array([reach] + holding)


def uneven(rng, number_of, total, reach, skew):
    if number_of == 2:
        one = jax.random.randint(rng, (), max(1, total - reach), min(reach, total - 1) + 1)
        return jnp.stack([one, total - one])
    sizes = jnp.asarray(profile(number_of, total, reach, skew), jnp.int32)
    couples = (number_of - 1) // 2
    donor, taker = sizes[1:1 + 2 * couples:2], sizes[2:2 + 2 * couples:2]
    room = jnp.minimum(donor - 1, reach - taker)
    shifted = jax.random.randint(jax.random.fold_in(rng, 1), (couples,), 0, 1 << 20) % (room + 1)
    sizes = sizes.at[1:1 + 2 * couples:2].set(donor - shifted).at[2:2 + 2 * couples:2].set(taker + shifted)
    return sizes[jax.random.permutation(jax.random.fold_in(rng, 2), number_of)]


def noise(stream_key, dims, width, most, pieces=(), kind=jnp.bfloat16):
    factor_of = shard_levels(stream_key, dims, pieces, -0.22, 0.18) if pieces else 1.0
    values = jax.random.normal(stream_key, dims, jnp.float32) * width * factor_of
    return jnp.minimum(jnp.maximum(values, -most), most).astype(kind)


def gaussian_with(own_key, extent, width, reach, pieces, heavy, kind=jnp.bfloat16):
    values = width * jax.random.normal(own_key, extent, jnp.float32)
    if pieces:
        values = values * shard_levels(own_key, extent, pieces, -0.22, 0.18)
    return jnp.clip(with_spikes(values, jax.random.fold_in(own_key, 3), *heavy), -reach, reach).astype(kind)


def setup_inputs(seed: int = 0) -> dict:
    splits = jax.random.split(jax.random.key(seed), 10)
    return {
        "hidden_in": noise(splits[0], (SEQS, LEN, D), 1.0, 6.0, ((0, 4), (1, 8))),
        "grad_out": gaussian_with(splits[1], (SEQS, LEN, D), 1.0, 8.0, ((0, 4), (1, 8)), (1, 2, 8, 2.0)),
        "segment_ids": jax.vmap(lambda own: jnp.searchsorted(jnp.cumsum(uneven(own, max(LEN // 128, 8), LEN, (3 * LEN) // 4, 2)), jnp.arange(LEN), side="right"))(jax.random.split(splits[2], SEQS)).reshape((SEQS, LEN)).astype(jnp.int32),
        "w_qkv": noise(splits[3], (D, 3 * D), D ** -0.5, 0.21875, ((0, 4),), jnp.float32),
        "w_out": noise(splits[4], (D, D), (D // 64) ** -0.5, 1.75, ((0, 4),), jnp.float32),
        "w_in": noise(splits[5], (D, 2 * FF), D ** -0.5, 0.21875, ((0, 4),), jnp.float32),
        "w_down": noise(splits[6], (FF, D), FF ** -0.5, 0.1875, ((1, 4),), jnp.float32),
        "gain_attn": jnp.clip(1.0 + 0.18 * jax.random.normal(splits[7], (D,), jnp.float32), 0.1, 1.9),
        "gain_mlp": jnp.clip(1.0 + 0.18 * jax.random.normal(splits[8], (D,), jnp.float32), 0.1, 1.9),
    }


@jax.custom_vjp
def low(v):
    return lax.optimization_barrier(v.astype(jnp.bfloat16)).astype(jnp.float32)

@jax.custom_vjp
def low_back(v):
    return v

def low_keep(v):
    return (low(v), None)

def low_pass(kept, grad):
    return (grad,)

def back_keep(v):
    return (v, None)

def back_low(kept, grad):
    return (low(grad),)
low.defvjp(low_keep, low_pass)
low_back.defvjp(back_keep, back_low)
norm_eps = 1e-05
theta_base = 160000.0
highest = lax.Precision.HIGHEST

def layer_norm(values, gain):
    mean_val = lax.optimization_barrier(jnp.mean(values, axis=-1, keepdims=True))
    centred = values - mean_val
    variance = lax.optimization_barrier(jnp.mean(centred * centred, axis=-1, keepdims=True))
    return centred * lax.rsqrt(variance + norm_eps) * gain

def rotary_tables(positions, head_size):
    half_size = head_size // 2
    exponents = jnp.arange(half_size, dtype=jnp.float32) * (2.0 / head_size)
    inv_freq = 1.0 / theta_base ** exponents
    angles = positions.astype(jnp.float32)[:, None] * inv_freq[None, :]
    cosine = jnp.cos(angles)
    sine = jnp.sin(angles)
    return (jnp.concatenate([cosine, cosine], -1), jnp.concatenate([sine, sine], -1))

def rotate(values, cosine, sine):
    half_size = values.shape[-1] // 2
    turned = jnp.concatenate([-values[..., half_size:], values[..., :half_size]], -1)
    return values * cosine[:, None, :] + turned * sine[:, None, :]

def attend_block(block, keys, values, key_segments):
    queries, query_segments = block
    score_scale = HD ** (-0.5)
    scores = low_back(jnp.einsum('qhd,khd->hqk', queries, keys, precision=highest) * score_scale)
    same = query_segments[:, None] == key_segments[None, :]
    expo = jnp.where(same[None], jnp.exp(scores), 0.0)
    total = lax.optimization_barrier(jnp.sum(expo, axis=-1))
    summed = low_back(jnp.einsum('hqk,khd->qhd', low(expo), values, precision=highest))
    return summed / jnp.transpose(total)[:, :, None]

def layer(hidden, w_qkv, w_out, w_in, w_down, gain_attn, gain_mlp, segments):
    length = hidden.shape[0]
    normed_attn = low(layer_norm(hidden, low(gain_attn)))
    qkv = low_back(jnp.dot(normed_attn, low(w_qkv), precision=highest))
    q_lin = qkv[:, :D].reshape(length, HEADS, HD)
    k_lin = qkv[:, D:2 * D].reshape(length, HEADS, HD)
    v_lin = qkv[:, 2 * D:].reshape(length, HEADS, HD)
    cosine, sine = rotary_tables(jnp.arange(length, dtype=jnp.int32), HD)
    queries = low(rotate(q_lin, cosine, sine))
    keys = low(rotate(k_lin, cosine, sine))
    values = low(v_lin)
    block = math.gcd(length, 512)
    count = length // block

    def one_block(blk):
        return attend_block(blk, keys, values, segments)
    attended = lax.map(jax.checkpoint(one_block), (queries.reshape(count, block, HEADS, HD), segments.reshape(count, block)))
    attended = low(attended.reshape(length, D))
    mixed = hidden + low_back(jnp.dot(attended, low(w_out), precision=highest))
    normed_mlp = low(layer_norm(mixed, low(gain_mlp)))
    gate_up = low_back(jnp.dot(normed_mlp, low(w_in), precision=highest))
    activ = low(jax.nn.gelu(gate_up[:, :FF], approximate=False) * gate_up[:, FF:])
    return mixed + jnp.dot(activ, low(w_down), precision=highest)

def reference(hidden_in, grad_out, segment_ids, w_qkv, w_out, w_in, w_down, gain_attn, gain_mlp):
    params = (w_qkv, w_out, w_in, w_down, gain_attn, gain_mlp)

    def one_sequence(totals, inputs):
        seq_input, seq_grad, seq_segments = inputs

        def forward(hidden, weight_a, weight_b, weight_c, weight_d, gain_a, gain_b):
            return layer(hidden, weight_a, weight_b, weight_c, weight_d, gain_a, gain_b, seq_segments)
        result, pull = jax.vjp(forward, seq_input.astype(jnp.float32), w_qkv, w_out, w_in, w_down, gain_attn, gain_mlp)
        grads = pull(seq_grad.astype(jnp.float32))
        totals = tuple((old + new for old, new in zip(totals, grads[1:])))
        return (totals, (result.astype(jnp.bfloat16), grads[0].astype(jnp.bfloat16)))
    start = tuple((jnp.zeros_like(param) for param in params))
    totals, outputs = lax.scan(one_sequence, start, (hidden_in, grad_out, segment_ids))
    return (outputs[0], outputs[1], totals[0], totals[1], totals[2], totals[3], totals[4], totals[5])
```

```python
import math

import jax
import jax.numpy as jnp
from jax import lax
from jax.experimental import pallas as pl
from jax.experimental.pallas import tpu as pltpu
from jax.sharding import PartitionSpec as P

D = 768
HEADS = 12
HD = 64
FF = 1152


norm_eps = 1e-05
theta_base = 160000.0


def layer_norm(values, gain):
    mean_val = jnp.mean(values, axis=-1, keepdims=True)
    centred = values - mean_val
    variance = jnp.mean(centred * centred, axis=-1, keepdims=True)
    return centred * lax.rsqrt(variance + norm_eps) * gain


def rotary_tables(positions, head_size):
    half_size = head_size // 2
    exponents = jnp.arange(half_size, dtype=jnp.float32) * (2.0 / head_size)
    inv_freq = 1.0 / theta_base**exponents
    angles = positions.astype(jnp.float32)[:, None] * inv_freq[None, :]
    cosine = jnp.cos(angles)
    sine = jnp.sin(angles)
    return (jnp.concatenate([cosine, cosine], -1), jnp.concatenate([sine, sine], -1))


def rotate(values, cosine, sine):
    half_size = values.shape[-1] // 2
    turned = jnp.concatenate([-values[..., half_size:], values[..., :half_size]], -1)
    return values * cosine[:, None, :] + turned * sine[:, None, :]


def fold_blocks(carry, pieces, piece_segments, work, rows):
    count = piece_segments.shape[0]
    size = math.gcd(count, 4 * rows)
    number = count // size
    blocks = tuple((part.reshape((number, size) + part.shape[1:]) for part in pieces))
    blocks = blocks + (piece_segments.reshape(number, size),)

    def step(acc, block):
        acc = work(acc, block)
        return (acc, None)

    carry, _ = lax.scan(step, carry, blocks)
    return carry


def on_device(hidden_in, grad_out, segment_ids, w_qkv, w_out, w_in, w_down, gain_attn, gain_mlp):
    rows = hidden_in.shape[1]
    local_seqs = hidden_in.shape[0]
    score_scale = HD ** (-0.5)
    bf16 = jnp.bfloat16
    f32 = jnp.float32
    gathered = (
        lax.all_gather(w_qkv.astype(bf16), "dp", axis=0, tiled=True),
        lax.all_gather(w_out.astype(bf16), "dp", axis=0, tiled=True),
        lax.all_gather(w_in.astype(bf16), "dp", axis=0, tiled=True),
        lax.all_gather(w_down.astype(bf16), "dp", axis=1, tiled=True),
        lax.all_gather(gain_attn.astype(bf16), "dp", axis=0, tiled=True),
        lax.all_gather(gain_mlp.astype(bf16), "dp", axis=0, tiled=True),
    )
    weight_qkv, weight_out, weight_in, weight_down, gain_low_a, gain_low_b = gathered
    gain_first = gain_low_a.astype(f32)
    gain_second = gain_low_b.astype(f32)
    whole_segments = lax.all_gather(segment_ids, "ctx", axis=1, tiled=True)
    positions = lax.axis_index("ctx") * rows + jnp.arange(rows, dtype=jnp.int32)
    cosine, sine = rotary_tables(positions, HD)

    def gated(values_in):
        return jax.nn.gelu(values_in[:, :FF], approximate=False) * values_in[:, FF:]

    def turn(pair):
        return (rotate(pair[0], cosine, sine), rotate(pair[1], cosine, sine))

    def one_sequence(seq_index):
        hidden = hidden_in[seq_index].astype(f32)
        own_segments = segment_ids[seq_index]
        all_segments = whole_segments[seq_index]
        normed_first, first_back = jax.vjp(layer_norm, hidden, gain_first)
        normed_attn = normed_first.astype(bf16)
        qkv = jnp.dot(normed_attn, weight_qkv, preferred_element_type=f32)
        q_lin = qkv[:, :D].reshape(rows, HEADS, HD)
        k_lin = qkv[:, D : 2 * D].reshape(rows, HEADS, HD)
        v_lin = qkv[:, 2 * D :].reshape(rows, HEADS, HD)
        turned, turn_back = jax.vjp(turn, (q_lin, k_lin))
        queries = turned[0].astype(bf16)
        keys = turned[1].astype(bf16)
        values = v_lin.astype(bf16)

        def forward_work(acc, block):
            key_blk, value_blk, seg_blk = block
            total, summed = acc
            scores = (
                jnp.einsum("thd,shd->hts", queries, key_blk, preferred_element_type=f32)
                * score_scale
            )
            same = own_segments[:, None] == seg_blk[None, :]
            expo = jnp.where(same[None], jnp.exp(scores), 0.0)
            total = total + jnp.sum(expo, axis=-1)
            summed = summed + jnp.einsum(
                "hts,shd->thd", expo.astype(bf16), value_blk, preferred_element_type=f32
            )
            return (total, summed)

        start_fwd = (jnp.zeros((HEADS, rows), f32), jnp.zeros((rows, HEADS, HD), f32))
        key_piece = lax.all_gather(keys.reshape(rows, D), "ctx", axis=0, tiled=True)
        value_piece = lax.all_gather(values.reshape(rows, D), "ctx", axis=0, tiled=True)
        count = key_piece.shape[0]
        piece_segments = all_segments
        parts = (key_piece.reshape(count, HEADS, HD), value_piece.reshape(count, HEADS, HD))
        total, summed = fold_blocks(start_fwd, parts, piece_segments, forward_work, rows)
        total_rows = jnp.transpose(total)
        attended = (summed / total_rows[:, :, None]).reshape(rows, D).astype(bf16)
        mixed = hidden + jnp.dot(attended, weight_out, preferred_element_type=f32)
        normed_second, second_back = jax.vjp(layer_norm, mixed, gain_second)
        normed_mlp = normed_second.astype(bf16)
        gate_up = jnp.dot(normed_mlp, weight_in, preferred_element_type=f32)
        activ_f, gated_back = jax.vjp(gated, gate_up)
        activ = activ_f.astype(bf16)
        layer_out = (mixed + jnp.dot(activ, weight_down, preferred_element_type=f32)).astype(bf16)
        grad_low = grad_out[seq_index]
        g_w_down = jnp.einsum("tf,td->fd", activ, grad_low, preferred_element_type=f32)
        g_activ = jnp.einsum("td,fd->tf", grad_low, weight_down, preferred_element_type=f32)
        g_gate_up = gated_back(g_activ)[0].astype(bf16)
        g_w_in = jnp.einsum("ti,tj->ij", normed_mlp, g_gate_up, preferred_element_type=f32)
        g_normed_mlp = jnp.einsum("tj,ij->ti", g_gate_up, weight_in, preferred_element_type=f32)
        g_mixed_norm, g_gain_mlp = second_back(g_normed_mlp)
        g_mixed = grad_low.astype(f32) + g_mixed_norm
        g_mixed_low = g_mixed.astype(bf16)
        g_w_out = jnp.einsum("ti,tj->ij", attended, g_mixed_low, preferred_element_type=f32)
        g_att = jnp.einsum(
            "tj,ij->ti", g_mixed_low, weight_out, preferred_element_type=f32
        ).reshape(rows, HEADS, HD)
        g_summed = (g_att / total_rows[:, :, None]).astype(bf16)
        row_term = jnp.sum(g_att * summed, axis=-1) / (total_rows * total_rows)
        own_rows = jnp.transpose(row_term)
        all_rows = lax.all_gather(row_term, "ctx", axis=0, tiled=True)

        def query_work(acc, block):
            key_blk, value_blk, seg_blk = block
            scores = (
                jnp.einsum("thd,shd->hts", queries, key_blk, preferred_element_type=f32)
                * score_scale
            )
            same = own_segments[:, None] == seg_blk[None, :]
            expo = jnp.where(same[None], jnp.exp(scores), 0.0)
            product = jnp.einsum("thd,shd->hts", g_summed, value_blk, preferred_element_type=f32)
            g_scores = (expo * (product - own_rows[:, :, None])).astype(bf16)
            return acc + jnp.einsum("hts,shd->thd", g_scores, key_blk, preferred_element_type=f32)

        key_piece = lax.all_gather(keys.reshape(rows, D), "ctx", axis=0, tiled=True)
        value_piece = lax.all_gather(values.reshape(rows, D), "ctx", axis=0, tiled=True)
        count = key_piece.shape[0]
        piece_segments = all_segments
        parts = (key_piece.reshape(count, HEADS, HD), value_piece.reshape(count, HEADS, HD))
        g_queries = (
            fold_blocks(jnp.zeros((rows, HEADS, HD), f32), parts, piece_segments, query_work, rows)
            * score_scale
        )

        def key_work(acc, block):
            query_blk, gsum_blk, row_blk, seg_blk = block
            g_keys, g_values = acc
            scores = (
                jnp.einsum("shd,thd->hst", query_blk, keys, preferred_element_type=f32)
                * score_scale
            )
            same = seg_blk[:, None] == own_segments[None, :]
            expo = jnp.where(same[None], jnp.exp(scores), 0.0)
            g_values = g_values + jnp.einsum(
                "hst,shd->thd", expo.astype(bf16), gsum_blk, preferred_element_type=f32
            )
            product = jnp.einsum("shd,thd->hst", gsum_blk, values, preferred_element_type=f32)
            g_scores = (expo * (product - jnp.transpose(row_blk)[:, :, None])).astype(bf16)
            g_keys = g_keys + jnp.einsum(
                "hst,shd->thd", g_scores, query_blk, preferred_element_type=f32
            )
            return (g_keys, g_values)

        start_keys = (jnp.zeros((rows, HEADS, HD), f32), jnp.zeros((rows, HEADS, HD), f32))
        query_piece = lax.all_gather(queries.reshape(rows, D), "ctx", axis=0, tiled=True)
        gsum_piece = lax.all_gather(g_summed.reshape(rows, D), "ctx", axis=0, tiled=True)
        count = query_piece.shape[0]
        piece_segments = all_segments
        parts = (
            query_piece.reshape(count, HEADS, HD),
            gsum_piece.reshape(count, HEADS, HD),
            all_rows,
        )
        g_keys, g_values = fold_blocks(start_keys, parts, piece_segments, key_work, rows)
        g_keys = g_keys * score_scale
        unturned = turn_back((g_queries, g_keys))[0]
        g_qkv = jnp.concatenate(
            [unturned[0].reshape(rows, D), unturned[1].reshape(rows, D), g_values.reshape(rows, D)],
            -1,
        ).astype(bf16)
        g_w_qkv = jnp.einsum("ti,tj->ij", normed_attn, g_qkv, preferred_element_type=f32)
        g_normed_attn = jnp.einsum("tj,ij->ti", g_qkv, weight_qkv, preferred_element_type=f32)
        g_hidden_norm, g_gain_attn = first_back(g_normed_attn)
        grad_in = (g_mixed + g_hidden_norm).astype(bf16)
        terms = (g_w_qkv, g_w_out, g_w_in, g_w_down, g_gain_attn, g_gain_mlp)
        return (layer_out, grad_in, terms)

    outputs_fwd = []
    outputs_back = []
    terms = None
    for seq_index in range(local_seqs):
        layer_out, grad_in, seq_terms = one_sequence(seq_index)
        outputs_fwd.append(layer_out)
        outputs_back.append(grad_in)
        if terms is None:
            terms = seq_terms
        else:
            terms = tuple((old + new for old, new in zip(terms, seq_terms)))
    everywhere = lax.psum(terms, "ctx")
    owned = (
        lax.psum_scatter(
            everywhere[0].astype(jnp.bfloat16), "dp", scatter_dimension=0, tiled=True
        ).astype(jnp.float32),
        lax.psum_scatter(
            everywhere[1].astype(jnp.bfloat16), "dp", scatter_dimension=0, tiled=True
        ).astype(jnp.float32),
        lax.psum_scatter(
            everywhere[2].astype(jnp.bfloat16), "dp", scatter_dimension=0, tiled=True
        ).astype(jnp.float32),
        lax.psum_scatter(
            everywhere[3].astype(jnp.bfloat16), "dp", scatter_dimension=1, tiled=True
        ).astype(jnp.float32),
        lax.psum_scatter(
            everywhere[4].astype(jnp.bfloat16), "dp", scatter_dimension=0, tiled=True
        ).astype(jnp.float32),
        lax.psum_scatter(
            everywhere[5].astype(jnp.bfloat16), "dp", scatter_dimension=0, tiled=True
        ).astype(jnp.float32),
    )
    return (
        jnp.stack(outputs_fwd),
        jnp.stack(outputs_back),
        owned[0],
        owned[1],
        owned[2],
        owned[3],
        owned[4],
        owned[5],
    )


HALF = 384
PIECE = 24


def send(values, mask):
    return lax.ppermute(values, ("dp", "ctx"), [(i, i ^ mask) for i in range(32)])


def send_swapped(values, mask):
    def target(i):
        core, high = (i >> 3) & 1, (i >> 2) & 1
        return (i & ~12) | (high << 3) | (core << 2)

    return lax.ppermute(values, ("dp", "ctx"), [(i, target(i) ^ mask) for i in range(32)])


def pick(flag, first, second):
    return jnp.where(flag == 0, first, second)


def pieces_kernel(order, me_ref, source_ref, out_ref):
    me = me_ref[0]
    for slot, mask in enumerate(order):
        start = pl.multiple_of((me ^ mask) * PIECE, 8)
        out_ref[slot] = source_ref[pl.ds(start, PIECE), :].astype(out_ref.dtype)


def natural_kernel(order, me_ref, source_ref, out_ref):
    me = me_ref[0]
    for slot, mask in enumerate(order):
        start = pl.multiple_of((me ^ mask) * PIECE, 8)
        out_ref[pl.ds(start, PIECE), :] = source_ref[slot].astype(out_ref.dtype)


VM = pl.BlockSpec(memory_space=pltpu.VMEM)
SM = pl.BlockSpec(memory_space=pltpu.SMEM)


def to_pieces(values, me, order):
    return pl.pallas_call(
        lambda *refs: pieces_kernel(order, *refs),
        out_shape=jax.ShapeDtypeStruct((len(order), PIECE, values.shape[1]), jnp.bfloat16),
        in_specs=[SM, VM],
        out_specs=VM,
        compiler_params=pltpu.CompilerParams(vmem_limit_bytes=48 << 20),
    )(me, values)


def to_natural(pieces, me, order, kind):
    return pl.pallas_call(
        lambda *refs: natural_kernel(order, *refs),
        out_shape=jax.ShapeDtypeStruct((len(order) * PIECE, pieces.shape[2]), kind),
        in_specs=[SM, VM],
        out_specs=VM,
        compiler_params=pltpu.CompilerParams(vmem_limit_bytes=48 << 20),
    )(me, pieces)


def plus(first, second):
    return (first.astype(jnp.float32) + second.astype(jnp.float32)).astype(jnp.bfloat16)


XZ = [(dx) | (dz << 1) for dx in range(2) for dz in range(4)]


def reduce_xz(part):
    part = part.reshape((2, 4) + part.shape[1:])
    part = plus(part[0], send(part[1], 1))
    total = part[0].astype(jnp.float32)
    for dz in range(1, 4):
        total = total + send(part[dz], 2 * dz).astype(jnp.float32)
    total = total.astype(jnp.bfloat16)
    near = jnp.stack([total] + [send(total, 2 * dz) for dz in range(1, 4)])
    far = send(near, 1)
    return jnp.concatenate([near, far])


def rows_of(shards, dp):
    count = shards[0].shape[0]
    whole = jnp.zeros((4 * count,) + shards[0].shape[1:], shards[0].dtype)
    for mask, shard in zip((0, 1, 2, 3), shards):
        whole = lax.dynamic_update_slice(
            whole, shard, ((dp ^ mask) * count,) + (0,) * (shard.ndim - 1)
        )
    return whole


def gather_dp(shard, dp):
    return rows_of([shard, send(shard, 8), send(shard, 16), send(shard, 24)], dp)


def norm_parts(values):
    mean_val = jnp.mean(values, axis=-1, keepdims=True)
    centred = values - mean_val
    variance = jnp.mean(centred * centred, axis=-1, keepdims=True)
    scale = lax.rsqrt(variance + norm_eps)
    return centred * scale, scale


def norm_back(xhat, scale, grad, gain):
    e = grad * gain
    return scale * (
        e
        - jnp.mean(e, axis=-1, keepdims=True)
        - xhat * jnp.mean(e * xhat, axis=-1, keepdims=True)
    )


def paired_chips(hidden_in, grad_out, segment_ids, w_qkv, w_out, w_in, w_down, gain_attn, gain_mlp):
    bf16, f32 = jnp.bfloat16, jnp.float32
    dp, ctx = lax.axis_index("dp"), lax.axis_index("ctx")
    me = dp * 8 + ctx
    me_ref = me.reshape(1).astype(jnp.int32)
    y, c = dp // 2, dp % 2
    zl, x = (ctx // 2) % 2, ctx % 2
    rows = hidden_in.shape[1]
    own = 2 * rows
    score_scale = HD ** (-0.5)

    def my_columns(core):
        return jnp.concatenate(
            [lax.dynamic_slice_in_dim(w_qkv, t * D + core * HALF, HALF, 1) for t in range(3)], 1
        ).astype(bf16)

    mine, other = my_columns(c), my_columns(1 - c)
    weight_qkv = rows_of([mine, send(other, 8), send(mine, 16), send(other, 24)], dp)
    gains = jnp.stack([gain_attn, gain_mlp]).astype(bf16).reshape(1, 2, 192)
    gains = gather_dp(gains, dp).transpose(1, 0, 2).reshape(2, D).astype(f32)
    gain_first, gain_second = gains[0], gains[1]

    def to_chips(values):
        return (
            send_swapped(pick(zl, values[0], values[1]), 0),
            send_swapped(pick(zl, values[1], values[0]), 2),
        )

    def from_chips(values):
        block_a, block_b = send_swapped(values[:rows], 0), send_swapped(values[rows:], 2)
        return jnp.stack([pick(zl, block_a, block_b), pick(zl, block_b, block_a)])

    def spread(values):
        peer = send(values, 8)
        across = send(values, 1)
        return jnp.concatenate([values, peer, across, send(across, 8)])

    hidden_own = jnp.concatenate(to_chips(hidden_in))
    segs_own = jnp.concatenate(to_chips(segment_ids))
    grad_low = jnp.concatenate(to_chips(grad_out))
    hidden = spread(hidden_own)
    segs = spread(segs_own)
    within = jnp.arange(rows, dtype=jnp.int32)
    starts = []
    for far in range(2):
        for core in range(2):
            for low in range(2):
                starts.append((2 * (2 * (c ^ core) + (zl ^ low)) + (x ^ far)) * rows + within)
    cosine, sine = rotary_tables(jnp.concatenate(starts), HD)
    count = 4 * own
    near = 2 * own

    xhat, scale = norm_parts(hidden.astype(f32))
    normed = (xhat * gain_first).astype(bf16)
    q_lin = jnp.dot(normed[:near], weight_qkv[:, :HALF], preferred_element_type=f32)
    kv_lin = jnp.dot(normed, weight_qkv[:, HALF:], preferred_element_type=f32)
    heads = HEADS // 2
    queries = rotate(q_lin.reshape(near, heads, HD), cosine[:near], sine[:near]).astype(bf16)
    keys = rotate(kv_lin[:, :HALF].reshape(count, heads, HD), cosine, sine).astype(bf16)
    values = kv_lin[:, HALF:].reshape(count, heads, HD).astype(bf16)
    scores = jnp.einsum("thd,shd->hts", queries, keys, preferred_element_type=f32) * score_scale
    same = segs[:near, None] == segs[None, :]
    expo = jnp.where(same[None], jnp.exp(scores), 0.0)
    total = jnp.sum(expo, axis=-1).T[:, :, None]
    probs = expo.astype(bf16)
    summed = jnp.einsum("hts,shd->thd", probs, values, preferred_element_type=f32)
    attended = (summed / total).reshape(near, HALF).astype(bf16)
    attended = jnp.concatenate([attended[:own], send(attended[own:], 8)], 1)

    weight_out = gather_dp(w_out.astype(bf16), dp)
    weight_out = jnp.concatenate(
        [
            lax.dynamic_slice_in_dim(weight_out, c * HALF, HALF, 0),
            lax.dynamic_slice_in_dim(weight_out, (1 - c) * HALF, HALF, 0),
        ]
    )
    weight_in = gather_dp(w_in.astype(bf16), dp)
    weight_down = gather_dp(w_down.T.astype(bf16), dp)

    mixed = hidden_own.astype(f32) + jnp.dot(attended, weight_out, preferred_element_type=f32)
    xhat_mlp, scale_mlp = norm_parts(mixed)
    normed_mlp = (xhat_mlp * gain_second).astype(bf16)
    gate_up = jnp.dot(normed_mlp, weight_in, preferred_element_type=f32)
    gate, upper = gate_up[:, :FF], gate_up[:, FF:]
    chance = 0.5 * (1.0 + lax.erf(gate * math.sqrt(0.5)))
    bell = jnp.exp(-0.5 * gate * gate) * (1.0 / math.sqrt(2.0 * math.pi))
    activ = (gate * chance * upper).astype(bf16)
    down = jnp.einsum("tf,df->td", activ, weight_down, preferred_element_type=f32)
    layer_out = from_chips((mixed + down).astype(bf16))
    g_activ = jnp.dot(grad_low, weight_down, preferred_element_type=f32)
    g_gate_up = jnp.concatenate(
        [g_activ * upper * (chance + gate * bell), g_activ * gate * chance], 1
    ).astype(bf16)
    g_w_down = jnp.einsum("td,tf->df", grad_low, activ, preferred_element_type=f32)
    g_w_in = jnp.einsum("ti,tj->ij", normed_mlp, g_gate_up, preferred_element_type=f32)
    g_normed_mlp = jnp.einsum("tj,ij->ti", g_gate_up, weight_in, preferred_element_type=f32)
    g_mixed = grad_low.astype(f32) + norm_back(xhat_mlp, scale_mlp, g_normed_mlp, gain_second)
    g_gain_mlp = jnp.sum(xhat_mlp * g_normed_mlp, axis=0)
    g_mixed_low = g_mixed.astype(bf16)
    g_w_out = jnp.einsum("ti,tj->ij", attended, g_mixed_low, preferred_element_type=f32)
    g_att = jnp.einsum("tj,ij->ti", g_mixed_low, weight_out, preferred_element_type=f32)

    g_att = g_att.astype(bf16)
    g_att = jnp.concatenate([g_att[:, :HALF], send(g_att[:, HALF:], 8)]).astype(f32)
    g_att = g_att.reshape(near, heads, HD)
    g_summed = (g_att / total).astype(bf16)
    row_term = (jnp.sum(g_att * summed, axis=-1, keepdims=True) / (total * total))[:, :, 0].T
    product = jnp.einsum("thd,shd->hts", g_summed, values, preferred_element_type=f32)
    g_scores = (probs.astype(f32) * (product - row_term[:, :, None])).astype(bf16)
    g_queries = jnp.einsum("hts,shd->thd", g_scores, keys, preferred_element_type=f32)
    g_keys = jnp.einsum("hts,thd->shd", g_scores, queries, preferred_element_type=f32)
    g_values = jnp.einsum("hts,thd->shd", probs, g_summed, preferred_element_type=f32)

    def turn_back(grad, cos, sin):
        turned = grad * sin[:, None, :]
        turned = jnp.concatenate([turned[..., HD // 2 :], -turned[..., : HD // 2]], -1)
        return grad * cos[:, None, :] + turned

    g_q = turn_back(g_queries * score_scale, cosine[:near], sine[:near])
    g_q = g_q.reshape(near, HALF).astype(bf16)
    g_k = turn_back(g_keys * score_scale, cosine, sine).reshape(count, HALF)
    g_kv = jnp.concatenate([g_k, g_values.reshape(count, HALF)], 1).astype(bf16)
    g_w_qkv = jnp.concatenate(
        [
            jnp.einsum("ti,tj->ij", normed[:near], g_q, preferred_element_type=f32),
            jnp.einsum("ti,tj->ij", normed, g_kv, preferred_element_type=f32),
        ],
        1,
    )
    g_near = jnp.einsum("tj,ij->ti", g_q, weight_qkv[:, :HALF], preferred_element_type=f32)
    g_normed = jnp.einsum("tj,ij->ti", g_kv, weight_qkv[:, HALF:], preferred_element_type=f32)
    g_normed = g_normed + jnp.pad(g_near, ((0, near), (0, 0)))
    g_gain_attn = jnp.sum(xhat * g_normed, axis=0)
    g_normed = g_normed.astype(bf16).reshape(2, 2, own, D)
    g_normed = plus(g_normed[:, 0], send(g_normed[:, 1], 8))
    g_normed = g_normed[0].astype(f32) + send(g_normed[1], 1).astype(f32)
    grad_in = g_mixed + norm_back(xhat[:own], scale[:own], g_normed, gain_first)
    grad_in = from_chips(grad_in.astype(bf16))

    all_masks = [(dc << 3) | (dy << 4) | m for dc in range(2) for dy in range(2) for m in XZ]

    def reduce_all(grad):
        part = to_pieces(grad, me_ref, all_masks).reshape(2, 2, 8, PIECE, grad.shape[1])
        part = plus(part[0], send(part[1], 8))
        part = plus(part[0], send(part[1], 16))
        return to_natural(reduce_xz(part), me_ref % 8, XZ, f32)

    g_w_out = jnp.concatenate(
        [
            lax.dynamic_slice_in_dim(g_w_out, c * HALF, HALF, 0),
            lax.dynamic_slice_in_dim(g_w_out, (1 - c) * HALF, HALF, 0),
        ]
    )
    g_w_down, g_w_in, g_w_out = reduce_all(g_w_down), reduce_all(g_w_in), reduce_all(g_w_out)

    core_last = [(dy << 4) | (dc << 3) | m for dy in range(2) for dc in range(2) for m in XZ]
    part = to_pieces(g_w_qkv, me_ref, core_last).reshape(2, 16, PIECE, 3 * HALF)
    part = plus(part[0], send(part[1], 16)).reshape(2, 8, PIECE, 3 * HALF)
    part = jnp.stack([reduce_xz(part[0]), reduce_xz(part[1])])
    other_half = send(part[1], 8)
    mine = to_natural(part[0], me_ref % 8, XZ, f32)
    other = to_natural(other_half, me_ref % 8, XZ, f32)
    low, high = pick(c, mine, other), pick(c, other, mine)
    g_w_qkv = jnp.concatenate(
        [h[:, t * HALF : (t + 1) * HALF] for t in range(3) for h in (low, high)], 1
    )

    g_gains = jnp.stack([g_gain_attn, g_gain_mlp])
    for mask in (8, 16, 1, 2, 4):
        g_gains = g_gains + send(g_gains, mask)
    g_gains = lax.dynamic_slice_in_dim(g_gains, dp * 192, 192, 1)
    return (layer_out, grad_in, g_w_qkv, g_w_out, g_w_in, g_w_down.T, g_gains[0], g_gains[1])


def solution(mesh):
    whole_fit = mesh.shape["dp"] == 4 and mesh.shape["ctx"] == 8
    return jax.shard_map(
        paired_chips if whole_fit else on_device,
        mesh=mesh,
        in_specs=(
            P("dp", "ctx", None),
            P("dp", "ctx", None),
            P("dp", "ctx"),
            P("dp", None),
            P("dp", None),
            P("dp", None),
            P(None, "dp"),
            P("dp"),
            P("dp"),
        ),
        out_specs=(
            P("dp", "ctx", None),
            P("dp", "ctx", None),
            P("dp", None),
            P("dp", None),
            P("dp", None),
            P(None, "dp"),
            P("dp"),
            P("dp"),
        ),
        check_vma=False,
    )
```

```python
import math

import jax
import jax.numpy as jnp
from jax import lax
from jax.experimental import pallas as pl
from jax.experimental.pallas import tpu as pltpu
from jax.sharding import PartitionSpec as P

D = 768
HEADS = 12
HD = 64
FF = 1152


norm_eps = 1e-05
theta_base = 160000.0


def layer_norm(values, gain):
    mean_val = jnp.mean(values, axis=-1, keepdims=True)
    centred = values - mean_val
    variance = jnp.mean(centred * centred, axis=-1, keepdims=True)
    return centred * lax.rsqrt(variance + norm_eps) * gain


def rotary_tables(positions, head_size):
    half_size = head_size // 2
    exponents = jnp.arange(half_size, dtype=jnp.float32) * (2.0 / head_size)
    inv_freq = 1.0 / theta_base**exponents
    angles = positions.astype(jnp.float32)[:, None] * inv_freq[None, :]
    cosine = jnp.cos(angles)
    sine = jnp.sin(angles)
    return (jnp.concatenate([cosine, cosine], -1), jnp.concatenate([sine, sine], -1))


def rotate(values, cosine, sine):
    half_size = values.shape[-1] // 2
    turned = jnp.concatenate([-values[..., half_size:], values[..., :half_size]], -1)
    return values * cosine[:, None, :] + turned * sine[:, None, :]


def fold_blocks(carry, pieces, piece_segments, work, rows):
    count = piece_segments.shape[0]
    size = math.gcd(count, 4 * rows)
    number = count // size
    blocks = tuple((part.reshape((number, size) + part.shape[1:]) for part in pieces))
    blocks = blocks + (piece_segments.reshape(number, size),)

    def step(acc, block):
        acc = work(acc, block)
        return (acc, None)

    carry, _ = lax.scan(step, carry, blocks)
    return carry


def on_device(hidden_in, grad_out, segment_ids, w_qkv, w_out, w_in, w_down, gain_attn, gain_mlp):
    rows = hidden_in.shape[1]
    local_seqs = hidden_in.shape[0]
    score_scale = HD ** (-0.5)
    bf16 = jnp.bfloat16
    f32 = jnp.float32
    gathered = (
        lax.all_gather(w_qkv.astype(bf16), "dp", axis=0, tiled=True),
        lax.all_gather(w_out.astype(bf16), "dp", axis=0, tiled=True),
        lax.all_gather(w_in.astype(bf16), "dp", axis=0, tiled=True),
        lax.all_gather(w_down.astype(bf16), "dp", axis=1, tiled=True),
        lax.all_gather(gain_attn.astype(bf16), "dp", axis=0, tiled=True),
        lax.all_gather(gain_mlp.astype(bf16), "dp", axis=0, tiled=True),
    )
    weight_qkv, weight_out, weight_in, weight_down, gain_low_a, gain_low_b = gathered
    gain_first = gain_low_a.astype(f32)
    gain_second = gain_low_b.astype(f32)
    whole_segments = lax.all_gather(segment_ids, "ctx", axis=1, tiled=True)
    positions = lax.axis_index("ctx") * rows + jnp.arange(rows, dtype=jnp.int32)
    cosine, sine = rotary_tables(positions, HD)

    def gated(values_in):
        return jax.nn.gelu(values_in[:, :FF], approximate=False) * values_in[:, FF:]

    def turn(pair):
        return (rotate(pair[0], cosine, sine), rotate(pair[1], cosine, sine))

    def one_sequence(seq_index):
        hidden = hidden_in[seq_index].astype(f32)
        own_segments = segment_ids[seq_index]
        all_segments = whole_segments[seq_index]
        normed_first, first_back = jax.vjp(layer_norm, hidden, gain_first)
        normed_attn = normed_first.astype(bf16)
        qkv = jnp.dot(normed_attn, weight_qkv, preferred_element_type=f32)
        q_lin = qkv[:, :D].reshape(rows, HEADS, HD)
        k_lin = qkv[:, D : 2 * D].reshape(rows, HEADS, HD)
        v_lin = qkv[:, 2 * D :].reshape(rows, HEADS, HD)
        turned, turn_back = jax.vjp(turn, (q_lin, k_lin))
        queries = turned[0].astype(bf16)
        keys = turned[1].astype(bf16)
        values = v_lin.astype(bf16)

        def forward_work(acc, block):
            key_blk, value_blk, seg_blk = block
            total, summed = acc
            scores = (
                jnp.einsum("thd,shd->hts", queries, key_blk, preferred_element_type=f32)
                * score_scale
            )
            same = own_segments[:, None] == seg_blk[None, :]
            expo = jnp.where(same[None], jnp.exp(scores), 0.0)
            total = total + jnp.sum(expo, axis=-1)
            summed = summed + jnp.einsum(
                "hts,shd->thd", expo.astype(bf16), value_blk, preferred_element_type=f32
            )
            return (total, summed)

        start_fwd = (jnp.zeros((HEADS, rows), f32), jnp.zeros((rows, HEADS, HD), f32))
        key_piece = lax.all_gather(keys.reshape(rows, D), "ctx", axis=0, tiled=True)
        value_piece = lax.all_gather(values.reshape(rows, D), "ctx", axis=0, tiled=True)
        count = key_piece.shape[0]
        piece_segments = all_segments
        parts = (key_piece.reshape(count, HEADS, HD), value_piece.reshape(count, HEADS, HD))
        total, summed = fold_blocks(start_fwd, parts, piece_segments, forward_work, rows)
        total_rows = jnp.transpose(total)
        attended = (summed / total_rows[:, :, None]).reshape(rows, D).astype(bf16)
        mixed = hidden + jnp.dot(attended, weight_out, preferred_element_type=f32)
        normed_second, second_back = jax.vjp(layer_norm, mixed, gain_second)
        normed_mlp = normed_second.astype(bf16)
        gate_up = jnp.dot(normed_mlp, weight_in, preferred_element_type=f32)
        activ_f, gated_back = jax.vjp(gated, gate_up)
        activ = activ_f.astype(bf16)
        layer_out = (mixed + jnp.dot(activ, weight_down, preferred_element_type=f32)).astype(bf16)
        grad_low = grad_out[seq_index]
        g_w_down = jnp.einsum("tf,td->fd", activ, grad_low, preferred_element_type=f32)
        g_activ = jnp.einsum("td,fd->tf", grad_low, weight_down, preferred_element_type=f32)
        g_gate_up = gated_back(g_activ)[0].astype(bf16)
        g_w_in = jnp.einsum("ti,tj->ij", normed_mlp, g_gate_up, preferred_element_type=f32)
        g_normed_mlp = jnp.einsum("tj,ij->ti", g_gate_up, weight_in, preferred_element_type=f32)
        g_mixed_norm, g_gain_mlp = second_back(g_normed_mlp)
        g_mixed = grad_low.astype(f32) + g_mixed_norm
        g_mixed_low = g_mixed.astype(bf16)
        g_w_out = jnp.einsum("ti,tj->ij", attended, g_mixed_low, preferred_element_type=f32)
        g_att = jnp.einsum(
            "tj,ij->ti", g_mixed_low, weight_out, preferred_element_type=f32
        ).reshape(rows, HEADS, HD)
        g_summed = (g_att / total_rows[:, :, None]).astype(bf16)
        row_term = jnp.sum(g_att * summed, axis=-1) / (total_rows * total_rows)
        own_rows = jnp.transpose(row_term)
        all_rows = lax.all_gather(row_term, "ctx", axis=0, tiled=True)

        def query_work(acc, block):
            key_blk, value_blk, seg_blk = block
            scores = (
                jnp.einsum("thd,shd->hts", queries, key_blk, preferred_element_type=f32)
                * score_scale
            )
            same = own_segments[:, None] == seg_blk[None, :]
            expo = jnp.where(same[None], jnp.exp(scores), 0.0)
            product = jnp.einsum("thd,shd->hts", g_summed, value_blk, preferred_element_type=f32)
            g_scores = (expo * (product - own_rows[:, :, None])).astype(bf16)
            return acc + jnp.einsum("hts,shd->thd", g_scores, key_blk, preferred_element_type=f32)

        key_piece = lax.all_gather(keys.reshape(rows, D), "ctx", axis=0, tiled=True)
        value_piece = lax.all_gather(values.reshape(rows, D), "ctx", axis=0, tiled=True)
        count = key_piece.shape[0]
        piece_segments = all_segments
        parts = (key_piece.reshape(count, HEADS, HD), value_piece.reshape(count, HEADS, HD))
        g_queries = (
            fold_blocks(jnp.zeros((rows, HEADS, HD), f32), parts, piece_segments, query_work, rows)
            * score_scale
        )

        def key_work(acc, block):
            query_blk, gsum_blk, row_blk, seg_blk = block
            g_keys, g_values = acc
            scores = (
                jnp.einsum("shd,thd->hst", query_blk, keys, preferred_element_type=f32)
                * score_scale
            )
            same = seg_blk[:, None] == own_segments[None, :]
            expo = jnp.where(same[None], jnp.exp(scores), 0.0)
            g_values = g_values + jnp.einsum(
                "hst,shd->thd", expo.astype(bf16), gsum_blk, preferred_element_type=f32
            )
            product = jnp.einsum("shd,thd->hst", gsum_blk, values, preferred_element_type=f32)
            g_scores = (expo * (product - jnp.transpose(row_blk)[:, :, None])).astype(bf16)
            g_keys = g_keys + jnp.einsum(
                "hst,shd->thd", g_scores, query_blk, preferred_element_type=f32
            )
            return (g_keys, g_values)

        start_keys = (jnp.zeros((rows, HEADS, HD), f32), jnp.zeros((rows, HEADS, HD), f32))
        query_piece = lax.all_gather(queries.reshape(rows, D), "ctx", axis=0, tiled=True)
        gsum_piece = lax.all_gather(g_summed.reshape(rows, D), "ctx", axis=0, tiled=True)
        count = query_piece.shape[0]
        piece_segments = all_segments
        parts = (
            query_piece.reshape(count, HEADS, HD),
            gsum_piece.reshape(count, HEADS, HD),
            all_rows,
        )
        g_keys, g_values = fold_blocks(start_keys, parts, piece_segments, key_work, rows)
        g_keys = g_keys * score_scale
        unturned = turn_back((g_queries, g_keys))[0]
        g_qkv = jnp.concatenate(
            [unturned[0].reshape(rows, D), unturned[1].reshape(rows, D), g_values.reshape(rows, D)],
            -1,
        ).astype(bf16)
        g_w_qkv = jnp.einsum("ti,tj->ij", normed_attn, g_qkv, preferred_element_type=f32)
        g_normed_attn = jnp.einsum("tj,ij->ti", g_qkv, weight_qkv, preferred_element_type=f32)
        g_hidden_norm, g_gain_attn = first_back(g_normed_attn)
        grad_in = (g_mixed + g_hidden_norm).astype(bf16)
        terms = (g_w_qkv, g_w_out, g_w_in, g_w_down, g_gain_attn, g_gain_mlp)
        return (layer_out, grad_in, terms)

    outputs_fwd = []
    outputs_back = []
    terms = None
    for seq_index in range(local_seqs):
        layer_out, grad_in, seq_terms = one_sequence(seq_index)
        outputs_fwd.append(layer_out)
        outputs_back.append(grad_in)
        if terms is None:
            terms = seq_terms
        else:
            terms = tuple((old + new for old, new in zip(terms, seq_terms)))
    everywhere = lax.psum(terms, "ctx")
    owned = (
        lax.psum_scatter(
            everywhere[0].astype(jnp.bfloat16), "dp", scatter_dimension=0, tiled=True
        ).astype(jnp.float32),
        lax.psum_scatter(
            everywhere[1].astype(jnp.bfloat16), "dp", scatter_dimension=0, tiled=True
        ).astype(jnp.float32),
        lax.psum_scatter(
            everywhere[2].astype(jnp.bfloat16), "dp", scatter_dimension=0, tiled=True
        ).astype(jnp.float32),
        lax.psum_scatter(
            everywhere[3].astype(jnp.bfloat16), "dp", scatter_dimension=1, tiled=True
        ).astype(jnp.float32),
        lax.psum_scatter(
            everywhere[4].astype(jnp.bfloat16), "dp", scatter_dimension=0, tiled=True
        ).astype(jnp.float32),
        lax.psum_scatter(
            everywhere[5].astype(jnp.bfloat16), "dp", scatter_dimension=0, tiled=True
        ).astype(jnp.float32),
    )
    return (
        jnp.stack(outputs_fwd),
        jnp.stack(outputs_back),
        owned[0],
        owned[1],
        owned[2],
        owned[3],
        owned[4],
        owned[5],
    )


HALF = 384
PIECE = 24


def send(values, mask):
    return lax.ppermute(values, ("dp", "ctx"), [(i, i ^ mask) for i in range(32)])


def send_swapped(values, mask):
    def target(i):
        core, high = (i >> 3) & 1, (i >> 2) & 1
        return (i & ~12) | (high << 3) | (core << 2)

    return lax.ppermute(values, ("dp", "ctx"), [(i, target(i) ^ mask) for i in range(32)])


def pick(flag, first, second):
    return jnp.where(flag == 0, first, second)


def pieces_kernel(orders, me_ref, *refs):
    sources, outs = refs[: len(orders[0])], refs[len(orders[0]) :]
    me = me_ref[0]
    for out_ref, wanted in zip(outs, orders):
        first = 0
        for source_ref, order in zip(sources, wanted):
            columns = slice(first, first + source_ref.shape[1])
            first += source_ref.shape[1]
            for slot, mask in enumerate(order):
                start = pl.multiple_of((me ^ mask) * PIECE, 8)
                piece = source_ref[pl.ds(start, PIECE), :]
                out_ref[slot, :, columns] = piece.astype(out_ref.dtype)


def natural_kernel(order, me_ref, source_ref, out_ref):
    me = me_ref[0]
    for slot, mask in enumerate(order):
        start = pl.multiple_of((me ^ mask) * PIECE, 8)
        out_ref[pl.ds(start, PIECE), :] = source_ref[slot].astype(out_ref.dtype)


VM = pl.BlockSpec(memory_space=pltpu.VMEM)
SM = pl.BlockSpec(memory_space=pltpu.SMEM)


def to_pieces(sources, me, orders):
    columns = sum(source.shape[1] for source in sources)
    return pl.pallas_call(
        lambda *refs: pieces_kernel(orders, *refs),
        out_shape=tuple(
            jax.ShapeDtypeStruct((len(wanted[0]), PIECE, columns), jnp.bfloat16)
            for wanted in orders
        ),
        in_specs=[SM] + [VM] * len(sources),
        out_specs=(VM,) * len(orders),
        compiler_params=pltpu.CompilerParams(vmem_limit_bytes=48 << 20),
    )(me, *sources)


def to_natural(pieces, me, order, kind):
    return pl.pallas_call(
        lambda *refs: natural_kernel(order, *refs),
        out_shape=jax.ShapeDtypeStruct((len(order) * PIECE, pieces.shape[2]), kind),
        in_specs=[SM, VM],
        out_specs=VM,
        compiler_params=pltpu.CompilerParams(vmem_limit_bytes=48 << 20),
    )(me, pieces)


def plus(first, second):
    return (first.astype(jnp.float32) + second.astype(jnp.float32)).astype(jnp.bfloat16)


XZ = [dx | (dz << 1) for dx in range(2) for dz in range(4)]


def masks(*bits):
    order = [0]
    for bit in bits:
        choices = (0, bit) if bit != 6 else (0, 2, 4, 6)
        order = [m | choice for m in order for choice in choices]
    return order


def fold_z(part):
    total = part[0].astype(jnp.float32)
    for dz in range(1, 4):
        total = total + send(part[dz], 2 * dz).astype(jnp.float32)
    return total.astype(jnp.bfloat16)


def spread_xz(total):
    near = jnp.stack([total] + [send(total, 2 * dz) for dz in range(1, 4)])
    return jnp.concatenate([near, send(near, 1)])


def rows_of(shards, dp):
    count = shards[0].shape[0]
    whole = jnp.zeros((4 * count,) + shards[0].shape[1:], shards[0].dtype)
    for mask, shard in zip((0, 1, 2, 3), shards):
        whole = lax.dynamic_update_slice(
            whole, shard, ((dp ^ mask) * count,) + (0,) * (shard.ndim - 1)
        )
    return whole


def after(values, *others):
    return lax.optimization_barrier((values,) + others)[0]


def norm_parts(values):
    mean_val = jnp.mean(values, axis=-1, keepdims=True)
    centred = values - mean_val
    variance = jnp.mean(centred * centred, axis=-1, keepdims=True)
    scale = lax.rsqrt(variance + norm_eps)
    return centred * scale, scale


def norm_back(xhat, scale, grad, gain):
    e = grad * gain
    return scale * (
        e
        - jnp.mean(e, axis=-1, keepdims=True)
        - xhat * jnp.mean(e * xhat, axis=-1, keepdims=True)
    )


def paired_chips(hidden_in, grad_out, segment_ids, w_qkv, w_out, w_in, w_down, gain_attn, gain_mlp):
    bf16, f32 = jnp.bfloat16, jnp.float32
    dp, ctx = lax.axis_index("dp"), lax.axis_index("ctx")
    me = dp * 8 + ctx
    me_ref = me.reshape(1).astype(jnp.int32)
    y, c = dp // 2, dp % 2
    zl, x = (ctx // 2) % 2, ctx % 2
    rows = hidden_in.shape[1]
    own = 2 * rows
    score_scale = HD ** (-0.5)

    gains = jnp.pad(jnp.stack([gain_attn, gain_mlp]), ((0, 6), (0, 3 * HALF - 192)))

    def my_columns(core):
        columns = [lax.dynamic_slice_in_dim(w_qkv, t * D + core * HALF, HALF, 1) for t in range(3)]
        return jnp.concatenate([jnp.concatenate(columns, 1), gains]).astype(bf16)

    mine, other = my_columns(c), my_columns(1 - c)
    shards = [mine, send(other, 8), send(mine, 16), send(other, 24)]
    weight_qkv = rows_of([shard[:192] for shard in shards], dp)
    gains = rows_of([shard[None, 192:194, :192] for shard in shards], dp)
    gains = gains.transpose(1, 0, 2).reshape(2, D).astype(f32)
    gain_first, gain_second = gains[0], gains[1]

    def gather_dp(shard, *others):
        pair = jnp.stack([shard, send(after(shard, *others), 16)])
        far = send(pair, 8)
        return rows_of([pair[0], far[0], pair[1], far[1]], dp)

    def to_chips(values):
        return (
            send_swapped(pick(zl, values[0], values[1]), 0),
            send_swapped(pick(zl, values[1], values[0]), 2),
        )

    def from_chips(values):
        block_a, block_b = send_swapped(values[:rows], 0), send_swapped(values[rows:], 2)
        return jnp.stack([pick(zl, block_a, block_b), pick(zl, block_b, block_a)])

    ids = jnp.pad(segment_ids[:, None, :], ((0, 0), (0, 7), (0, D - rows))).astype(bf16)
    tokens = jnp.stack(to_chips(jnp.concatenate([hidden_in, ids], 1)))
    tokens = jnp.stack([tokens, send(tokens, 1)])
    tokens = jnp.stack([tokens, send(tokens, 8)], 1)
    tokens = tokens.reshape(8, rows + 8, D)
    hidden = tokens[:, :rows].reshape(8 * rows, D)
    segs = tokens[:, rows, :rows].reshape(8 * rows)
    hidden_own = hidden[:own]
    weight_mid = gather_dp(jnp.concatenate([w_out, w_in], 1).astype(bf16), shards[2], shards[3])
    weight_out, weight_in = weight_mid[:, :D], weight_mid[:, D:]
    weight_down = gather_dp(w_down.T.astype(bf16), weight_mid)
    grad_low = jnp.concatenate(to_chips(after(grad_out, tokens)))
    within = jnp.arange(rows, dtype=jnp.int32)
    starts = []
    for far in range(2):
        for core in range(2):
            for low in range(2):
                starts.append((2 * (2 * (c ^ core) + (zl ^ low)) + (x ^ far)) * rows + within)
    cosine, sine = rotary_tables(jnp.concatenate(starts), HD)
    count = 4 * own
    near = 2 * own

    xhat, scale = norm_parts(hidden.astype(f32))
    normed = (xhat * gain_first).astype(bf16)
    q_lin = jnp.dot(normed[:near], weight_qkv[:, :HALF], preferred_element_type=f32)
    kv_lin = jnp.dot(normed, weight_qkv[:, HALF:], preferred_element_type=f32)
    heads = HEADS // 2
    queries = rotate(q_lin.reshape(near, heads, HD), cosine[:near], sine[:near]).astype(bf16)
    keys = rotate(kv_lin[:, :HALF].reshape(count, heads, HD), cosine, sine).astype(bf16)
    values = kv_lin[:, HALF:].reshape(count, heads, HD).astype(bf16)
    scores = jnp.einsum("thd,shd->hts", queries, keys, preferred_element_type=f32) * score_scale
    same = segs[:near, None] == segs[None, :]
    expo = jnp.where(same[None], jnp.exp(scores), 0.0)
    total = jnp.sum(expo, axis=-1).T[:, :, None]
    probs = expo.astype(bf16)
    summed = jnp.einsum("hts,shd->thd", probs, values, preferred_element_type=f32)
    attended = (summed / total).reshape(near, HALF).astype(bf16)
    attended = jnp.concatenate([attended[:own], send(attended[own:], 8)], 1)

    weight_out = jnp.concatenate(
        [
            lax.dynamic_slice_in_dim(weight_out, c * HALF, HALF, 0),
            lax.dynamic_slice_in_dim(weight_out, (1 - c) * HALF, HALF, 0),
        ]
    )

    mixed = hidden_own.astype(f32) + jnp.dot(attended, weight_out, preferred_element_type=f32)
    xhat_mlp, scale_mlp = norm_parts(mixed)
    normed_mlp = (xhat_mlp * gain_second).astype(bf16)
    gate_up = jnp.dot(normed_mlp, weight_in, preferred_element_type=f32)
    gate, upper = gate_up[:, :FF], gate_up[:, FF:]
    chance = 0.5 * (1.0 + lax.erf(gate * math.sqrt(0.5)))
    bell = jnp.exp(-0.5 * gate * gate) * (1.0 / math.sqrt(2.0 * math.pi))
    activ = (gate * chance * upper).astype(bf16)
    down = jnp.einsum("tf,df->td", activ, weight_down, preferred_element_type=f32)
    layer_out = from_chips((mixed + down).astype(bf16))
    g_activ = jnp.dot(grad_low, weight_down, preferred_element_type=f32)
    g_gate_up = jnp.concatenate(
        [g_activ * upper * (chance + gate * bell), g_activ * gate * chance], 1
    ).astype(bf16)
    g_w_down = jnp.einsum("td,tf->df", grad_low, activ, preferred_element_type=f32)
    g_w_in = jnp.einsum("ti,tj->ij", normed_mlp, g_gate_up, preferred_element_type=f32)
    g_normed_mlp = jnp.einsum("tj,ij->ti", g_gate_up, weight_in, preferred_element_type=f32)
    g_mixed = grad_low.astype(f32) + norm_back(xhat_mlp, scale_mlp, g_normed_mlp, gain_second)
    g_gain_mlp = jnp.sum(xhat_mlp * g_normed_mlp, axis=0)
    g_mixed_low = g_mixed.astype(bf16)
    g_w_out = jnp.einsum("ti,tj->ij", attended, g_mixed_low, preferred_element_type=f32)
    g_att = jnp.einsum("tj,ij->ti", g_mixed_low, weight_out, preferred_element_type=f32)

    def flip_rows(grad):
        return jnp.concatenate(
            [
                lax.dynamic_slice_in_dim(grad, c * HALF, HALF, 0),
                lax.dynamic_slice_in_dim(grad, (1 - c) * HALF, HALF, 0),
            ]
        )

    def with_core(order):
        return [m | 8 for m in order]

    def halves(values, got, cut):
        count = values.shape[0] // 2
        return [
            plus(values[part, :, columns], got[part, :, columns])
            for columns in (slice(0, cut), slice(cut, None))
            for part in (slice(0, count), slice(count, None))
        ]

    y_first, x_first = masks(16, 1, 6), masks(1, 16, 6)
    cut = FF + D
    away, stay = to_pieces(
        [g_w_down, flip_rows(g_w_out), g_w_in],
        me_ref,
        [[with_core(y_first)] * 2 + [with_core(x_first)], [y_first] * 2 + [x_first]],
    )
    g_att = g_att.astype(bf16)
    g_att = jnp.concatenate([g_att[:, :HALF], send(g_att[:, HALF:], 8)]).astype(f32)
    g_att = after(g_att, away, stay)
    g_att = g_att.reshape(near, heads, HD)
    g_summed = (g_att / total).astype(bf16)
    row_term = (jnp.sum(g_att * summed, axis=-1, keepdims=True) / (total * total))[:, :, 0].T
    product = jnp.einsum("thd,shd->hts", g_summed, values, preferred_element_type=f32)
    stay_a, leave_a, stay_b, leave_b = halves(stay, send(away, 8), cut)
    got_a, got_b = send(leave_a, 16), send(leave_b, 1)
    probs = after(probs, stay_a, leave_a, stay_b, leave_b)
    g_scores = (probs.astype(f32) * (product - row_term[:, :, None])).astype(bf16)
    g_queries = jnp.einsum("hts,shd->thd", g_scores, keys, preferred_element_type=f32)
    g_keys = jnp.einsum("hts,thd->shd", g_scores, queries, preferred_element_type=f32)
    g_values = jnp.einsum("hts,thd->shd", probs, g_summed, preferred_element_type=f32)

    def turn_back(grad, cos, sin):
        turned = grad * sin[:, None, :]
        turned = jnp.concatenate([turned[..., HD // 2 :], -turned[..., : HD // 2]], -1)
        return grad * cos[:, None, :] + turned

    g_q = turn_back(g_queries * score_scale, cosine[:near], sine[:near])
    g_q = g_q.reshape(near, HALF).astype(bf16)
    g_k = turn_back(g_keys * score_scale, cosine, sine).reshape(count, HALF)
    g_kv = jnp.concatenate([g_k, g_values.reshape(count, HALF)], 1).astype(bf16)
    stay_a, leave_a = plus(stay_a[:4], got_a[:4]), plus(stay_a[4:], got_a[4:])
    stay_b, leave_b = plus(stay_b[:4], got_b[:4]), plus(stay_b[4:], got_b[4:])
    g_q, g_kv = after(g_q, leave_a, leave_b), after(g_kv, leave_a, leave_b)
    g_w_qkv = jnp.concatenate(
        [
            jnp.einsum("ti,tj->ij", normed[:near], g_q, preferred_element_type=f32),
            jnp.einsum("ti,tj->ij", normed, g_kv, preferred_element_type=f32),
        ],
        1,
    )
    g_near = jnp.einsum("tj,ij->ti", g_q, weight_qkv[:, :HALF], preferred_element_type=f32)
    g_normed = jnp.einsum("tj,ij->ti", g_kv, weight_qkv[:, HALF:], preferred_element_type=f32)
    g_normed = g_normed + jnp.pad(g_near, ((0, near), (0, 0)))
    g_gain_attn = jnp.sum(xhat * g_normed, axis=0)
    g_normed = g_normed.astype(bf16).reshape(2, 2, own, D)
    g_normed = plus(g_normed[:, 0], send(g_normed[:, 1], 8))
    g_normed = g_normed[0].astype(f32) + send(g_normed[1], 1).astype(f32)
    grad_in = g_mixed + norm_back(xhat[:own], scale[:own], g_normed, gain_first)
    grad_in = from_chips(grad_in.astype(bf16))

    got_a, got_b = send(leave_a, 1), send(leave_b, 16)
    early = jnp.concatenate([plus(stay_a, got_a), plus(stay_b, got_b)], 2)

    order_y, order_x = masks(1, 6), masks(16, 6)
    keep_a, away_a, keep_b, away_b = to_pieces(
        [g_w_qkv],
        me_ref,
        [
            [order_y],
            [[m | 16 for m in order_y]],
            [with_core(order_x)],
            [[m | 9 for m in order_x]],
        ],
    )
    away_a, away_b = after(away_a, early), after(away_b, early)
    got_a, got_b = send(away_a, 16), send(away_b, 1)
    early = fold_z(early)
    stay_a, leave_a = plus(keep_a[:4], got_a[:4]), plus(keep_a[4:], got_a[4:])
    stay_b, leave_b = plus(keep_b[:4], got_b[:4]), plus(keep_b[4:], got_b[4:])
    leave_a, leave_b = after(leave_a, early), after(leave_b, early)
    got_a, got_b = send(leave_a, 1), send(leave_b, 16)
    part = jnp.concatenate([plus(stay_a, got_a), plus(stay_b, got_b)], 2)
    early = jnp.stack([early] + [send(early, 2 * dz) for dz in range(1, 4)])
    part = fold_z(after(part, early))
    early = jnp.concatenate([early, send(early, 1)])
    peer = send(part[:, 3 * HALF :], 8)
    part = part[:, : 3 * HALF]
    low, high = pick(c, part, peer), pick(c, peer, part)
    part = jnp.concatenate(
        [h[:, t * HALF : (t + 1) * HALF] for t in range(3) for h in (low, high)], 1
    )
    g_w_qkv = to_natural(spread_xz(part), me_ref % 8, XZ, f32)
    early = to_natural(early, me_ref % 8, XZ, f32)
    g_w_down, g_w_out, g_w_in = early[:, :FF], early[:, FF : FF + D], early[:, FF + D :]

    g_gains = jnp.stack([g_gain_attn, g_gain_mlp])
    for mask in (8, 16, 1, 2, 4):
        g_gains = g_gains + send(g_gains, mask)
    g_gains = lax.dynamic_slice_in_dim(g_gains, dp * 192, 192, 1)
    return (layer_out, grad_in, g_w_qkv, g_w_out, g_w_in, g_w_down.T, g_gains[0], g_gains[1])


def solution(mesh):
    whole_fit = mesh.shape["dp"] == 4 and mesh.shape["ctx"] == 8
    return jax.shard_map(
        paired_chips if whole_fit else on_device,
        mesh=mesh,
        in_specs=(
            P("dp", "ctx", None),
            P("dp", "ctx", None),
            P("dp", "ctx"),
            P("dp", None),
            P("dp", None),
            P("dp", None),
            P(None, "dp"),
            P("dp"),
            P("dp"),
        ),
        out_specs=(
            P("dp", "ctx", None),
            P("dp", "ctx", None),
            P("dp", None),
            P("dp", None),
            P("dp", None),
            P(None, "dp"),
            P("dp"),
            P("dp"),
        ),
        check_vma=False,
    )
```

```python
import math

import jax
import jax.numpy as jnp
from jax import lax
from jax.experimental import pallas as pl
from jax.experimental.pallas import tpu as pltpu
from jax.sharding import PartitionSpec as P

D = 768
HEADS = 12
HD = 64
FF = 1152


norm_eps = 1e-05
theta_base = 160000.0


def layer_norm(values, gain):
    mean_val = jnp.mean(values, axis=-1, keepdims=True)
    centred = values - mean_val
    variance = jnp.mean(centred * centred, axis=-1, keepdims=True)
    return centred * lax.rsqrt(variance + norm_eps) * gain


def rotary_tables(positions, head_size):
    half_size = head_size // 2
    exponents = jnp.arange(half_size, dtype=jnp.float32) * (2.0 / head_size)
    inv_freq = 1.0 / theta_base**exponents
    angles = positions.astype(jnp.float32)[:, None] * inv_freq[None, :]
    cosine = jnp.cos(angles)
    sine = jnp.sin(angles)
    return (jnp.concatenate([cosine, cosine], -1), jnp.concatenate([sine, sine], -1))


def rotate(values, cosine, sine):
    half_size = values.shape[-1] // 2
    turned = jnp.concatenate([-values[..., half_size:], values[..., :half_size]], -1)
    return values * cosine[:, None, :] + turned * sine[:, None, :]


def fold_blocks(carry, pieces, piece_segments, work, rows):
    count = piece_segments.shape[0]
    size = math.gcd(count, 4 * rows)
    number = count // size
    blocks = tuple((part.reshape((number, size) + part.shape[1:]) for part in pieces))
    blocks = blocks + (piece_segments.reshape(number, size),)

    def step(acc, block):
        acc = work(acc, block)
        return (acc, None)

    carry, _ = lax.scan(step, carry, blocks)
    return carry


def on_device(hidden_in, grad_out, segment_ids, w_qkv, w_out, w_in, w_down, gain_attn, gain_mlp):
    rows = hidden_in.shape[1]
    local_seqs = hidden_in.shape[0]
    score_scale = HD ** (-0.5)
    bf16 = jnp.bfloat16
    f32 = jnp.float32
    gathered = (
        lax.all_gather(w_qkv.astype(bf16), "dp", axis=0, tiled=True),
        lax.all_gather(w_out.astype(bf16), "dp", axis=0, tiled=True),
        lax.all_gather(w_in.astype(bf16), "dp", axis=0, tiled=True),
        lax.all_gather(w_down.astype(bf16), "dp", axis=1, tiled=True),
        lax.all_gather(gain_attn.astype(bf16), "dp", axis=0, tiled=True),
        lax.all_gather(gain_mlp.astype(bf16), "dp", axis=0, tiled=True),
    )
    weight_qkv, weight_out, weight_in, weight_down, gain_low_a, gain_low_b = gathered
    gain_first = gain_low_a.astype(f32)
    gain_second = gain_low_b.astype(f32)
    whole_segments = lax.all_gather(segment_ids, "ctx", axis=1, tiled=True)
    positions = lax.axis_index("ctx") * rows + jnp.arange(rows, dtype=jnp.int32)
    cosine, sine = rotary_tables(positions, HD)

    def gated(values_in):
        return jax.nn.gelu(values_in[:, :FF], approximate=False) * values_in[:, FF:]

    def turn(pair):
        return (rotate(pair[0], cosine, sine), rotate(pair[1], cosine, sine))

    def one_sequence(seq_index):
        hidden = hidden_in[seq_index].astype(f32)
        own_segments = segment_ids[seq_index]
        all_segments = whole_segments[seq_index]
        normed_first, first_back = jax.vjp(layer_norm, hidden, gain_first)
        normed_attn = normed_first.astype(bf16)
        qkv = jnp.dot(normed_attn, weight_qkv, preferred_element_type=f32)
        q_lin = qkv[:, :D].reshape(rows, HEADS, HD)
        k_lin = qkv[:, D : 2 * D].reshape(rows, HEADS, HD)
        v_lin = qkv[:, 2 * D :].reshape(rows, HEADS, HD)
        turned, turn_back = jax.vjp(turn, (q_lin, k_lin))
        queries = turned[0].astype(bf16)
        keys = turned[1].astype(bf16)
        values = v_lin.astype(bf16)

        def forward_work(acc, block):
            key_blk, value_blk, seg_blk = block
            total, summed = acc
            scores = (
                jnp.einsum("thd,shd->hts", queries, key_blk, preferred_element_type=f32)
                * score_scale
            )
            same = own_segments[:, None] == seg_blk[None, :]
            expo = jnp.where(same[None], jnp.exp(scores), 0.0)
            total = total + jnp.sum(expo, axis=-1)
            summed = summed + jnp.einsum(
                "hts,shd->thd", expo.astype(bf16), value_blk, preferred_element_type=f32
            )
            return (total, summed)

        start_fwd = (jnp.zeros((HEADS, rows), f32), jnp.zeros((rows, HEADS, HD), f32))
        key_piece = lax.all_gather(keys.reshape(rows, D), "ctx", axis=0, tiled=True)
        value_piece = lax.all_gather(values.reshape(rows, D), "ctx", axis=0, tiled=True)
        count = key_piece.shape[0]
        piece_segments = all_segments
        parts = (key_piece.reshape(count, HEADS, HD), value_piece.reshape(count, HEADS, HD))
        total, summed = fold_blocks(start_fwd, parts, piece_segments, forward_work, rows)
        total_rows = jnp.transpose(total)
        attended = (summed / total_rows[:, :, None]).reshape(rows, D).astype(bf16)
        mixed = hidden + jnp.dot(attended, weight_out, preferred_element_type=f32)
        normed_second, second_back = jax.vjp(layer_norm, mixed, gain_second)
        normed_mlp = normed_second.astype(bf16)
        gate_up = jnp.dot(normed_mlp, weight_in, preferred_element_type=f32)
        activ_f, gated_back = jax.vjp(gated, gate_up)
        activ = activ_f.astype(bf16)
        layer_out = (mixed + jnp.dot(activ, weight_down, preferred_element_type=f32)).astype(bf16)
        grad_low = grad_out[seq_index]
        g_w_down = jnp.einsum("tf,td->fd", activ, grad_low, preferred_element_type=f32)
        g_activ = jnp.einsum("td,fd->tf", grad_low, weight_down, preferred_element_type=f32)
        g_gate_up = gated_back(g_activ)[0].astype(bf16)
        g_w_in = jnp.einsum("ti,tj->ij", normed_mlp, g_gate_up, preferred_element_type=f32)
        g_normed_mlp = jnp.einsum("tj,ij->ti", g_gate_up, weight_in, preferred_element_type=f32)
        g_mixed_norm, g_gain_mlp = second_back(g_normed_mlp)
        g_mixed = grad_low.astype(f32) + g_mixed_norm
        g_mixed_low = g_mixed.astype(bf16)
        g_w_out = jnp.einsum("ti,tj->ij", attended, g_mixed_low, preferred_element_type=f32)
        g_att = jnp.einsum(
            "tj,ij->ti", g_mixed_low, weight_out, preferred_element_type=f32
        ).reshape(rows, HEADS, HD)
        g_summed = (g_att / total_rows[:, :, None]).astype(bf16)
        row_term = jnp.sum(g_att * summed, axis=-1) / (total_rows * total_rows)
        own_rows = jnp.transpose(row_term)
        all_rows = lax.all_gather(row_term, "ctx", axis=0, tiled=True)

        def query_work(acc, block):
            key_blk, value_blk, seg_blk = block
            scores = (
                jnp.einsum("thd,shd->hts", queries, key_blk, preferred_element_type=f32)
                * score_scale
            )
            same = own_segments[:, None] == seg_blk[None, :]
            expo = jnp.where(same[None], jnp.exp(scores), 0.0)
            product = jnp.einsum("thd,shd->hts", g_summed, value_blk, preferred_element_type=f32)
            g_scores = (expo * (product - own_rows[:, :, None])).astype(bf16)
            return acc + jnp.einsum("hts,shd->thd", g_scores, key_blk, preferred_element_type=f32)

        key_piece = lax.all_gather(keys.reshape(rows, D), "ctx", axis=0, tiled=True)
        value_piece = lax.all_gather(values.reshape(rows, D), "ctx", axis=0, tiled=True)
        count = key_piece.shape[0]
        piece_segments = all_segments
        parts = (key_piece.reshape(count, HEADS, HD), value_piece.reshape(count, HEADS, HD))
        g_queries = (
            fold_blocks(jnp.zeros((rows, HEADS, HD), f32), parts, piece_segments, query_work, rows)
            * score_scale
        )

        def key_work(acc, block):
            query_blk, gsum_blk, row_blk, seg_blk = block
            g_keys, g_values = acc
            scores = (
                jnp.einsum("shd,thd->hst", query_blk, keys, preferred_element_type=f32)
                * score_scale
            )
            same = seg_blk[:, None] == own_segments[None, :]
            expo = jnp.where(same[None], jnp.exp(scores), 0.0)
            g_values = g_values + jnp.einsum(
                "hst,shd->thd", expo.astype(bf16), gsum_blk, preferred_element_type=f32
            )
            product = jnp.einsum("shd,thd->hst", gsum_blk, values, preferred_element_type=f32)
            g_scores = (expo * (product - jnp.transpose(row_blk)[:, :, None])).astype(bf16)
            g_keys = g_keys + jnp.einsum(
                "hst,shd->thd", g_scores, query_blk, preferred_element_type=f32
            )
            return (g_keys, g_values)

        start_keys = (jnp.zeros((rows, HEADS, HD), f32), jnp.zeros((rows, HEADS, HD), f32))
        query_piece = lax.all_gather(queries.reshape(rows, D), "ctx", axis=0, tiled=True)
        gsum_piece = lax.all_gather(g_summed.reshape(rows, D), "ctx", axis=0, tiled=True)
        count = query_piece.shape[0]
        piece_segments = all_segments
        parts = (
            query_piece.reshape(count, HEADS, HD),
            gsum_piece.reshape(count, HEADS, HD),
            all_rows,
        )
        g_keys, g_values = fold_blocks(start_keys, parts, piece_segments, key_work, rows)
        g_keys = g_keys * score_scale
        unturned = turn_back((g_queries, g_keys))[0]
        g_qkv = jnp.concatenate(
            [unturned[0].reshape(rows, D), unturned[1].reshape(rows, D), g_values.reshape(rows, D)],
            -1,
        ).astype(bf16)
        g_w_qkv = jnp.einsum("ti,tj->ij", normed_attn, g_qkv, preferred_element_type=f32)
        g_normed_attn = jnp.einsum("tj,ij->ti", g_qkv, weight_qkv, preferred_element_type=f32)
        g_hidden_norm, g_gain_attn = first_back(g_normed_attn)
        grad_in = (g_mixed + g_hidden_norm).astype(bf16)
        terms = (g_w_qkv, g_w_out, g_w_in, g_w_down, g_gain_attn, g_gain_mlp)
        return (layer_out, grad_in, terms)

    outputs_fwd = []
    outputs_back = []
    terms = None
    for seq_index in range(local_seqs):
        layer_out, grad_in, seq_terms = one_sequence(seq_index)
        outputs_fwd.append(layer_out)
        outputs_back.append(grad_in)
        if terms is None:
            terms = seq_terms
        else:
            terms = tuple((old + new for old, new in zip(terms, seq_terms)))
    everywhere = lax.psum(terms, "ctx")
    owned = (
        lax.psum_scatter(
            everywhere[0].astype(jnp.bfloat16), "dp", scatter_dimension=0, tiled=True
        ).astype(jnp.float32),
        lax.psum_scatter(
            everywhere[1].astype(jnp.bfloat16), "dp", scatter_dimension=0, tiled=True
        ).astype(jnp.float32),
        lax.psum_scatter(
            everywhere[2].astype(jnp.bfloat16), "dp", scatter_dimension=0, tiled=True
        ).astype(jnp.float32),
        lax.psum_scatter(
            everywhere[3].astype(jnp.bfloat16), "dp", scatter_dimension=1, tiled=True
        ).astype(jnp.float32),
        lax.psum_scatter(
            everywhere[4].astype(jnp.bfloat16), "dp", scatter_dimension=0, tiled=True
        ).astype(jnp.float32),
        lax.psum_scatter(
            everywhere[5].astype(jnp.bfloat16), "dp", scatter_dimension=0, tiled=True
        ).astype(jnp.float32),
    )
    return (
        jnp.stack(outputs_fwd),
        jnp.stack(outputs_back),
        owned[0],
        owned[1],
        owned[2],
        owned[3],
        owned[4],
        owned[5],
    )


HALF = 384
PIECE = 24


def send(values, mask):
    return lax.ppermute(values, ("dp", "ctx"), [(i, i ^ mask) for i in range(32)])


def send_swapped(values, mask):
    def target(i):
        core, high = (i >> 3) & 1, (i >> 2) & 1
        return (i & ~12) | (high << 3) | (core << 2)

    return lax.ppermute(values, ("dp", "ctx"), [(i, target(i) ^ mask) for i in range(32)])


def pick(flag, first, second):
    return jnp.where(flag == 0, first, second)


def natural_kernel(order, me_ref, source_ref, out_ref):
    me = me_ref[0]
    for slot, mask in enumerate(order):
        start = pl.multiple_of((me ^ mask) * PIECE, 8)
        out_ref[pl.ds(start, PIECE), :] = source_ref[slot].astype(out_ref.dtype)


VM = pl.BlockSpec(memory_space=pltpu.VMEM)
SM = pl.BlockSpec(memory_space=pltpu.SMEM)


def to_natural(pieces, me, order, kind):
    return pl.pallas_call(
        lambda *refs: natural_kernel(order, *refs),
        out_shape=jax.ShapeDtypeStruct((len(order) * PIECE, pieces.shape[2]), kind),
        in_specs=[SM, VM],
        out_specs=VM,
        compiler_params=pltpu.CompilerParams(vmem_limit_bytes=48 << 20),
    )(me, pieces)


def plus(first, second):
    return (first.astype(jnp.float32) + second.astype(jnp.float32)).astype(jnp.bfloat16)


def natural_qkv_kernel(me_ref, near_ref, far_ref, out_ref, gains_ref):
    me = me_ref[0]
    for slot, mask in enumerate(XZ):
        start = pl.multiple_of((me ^ mask) * PIECE, 8)
        piece = (near_ref, far_ref)[slot // 4][slot % 4].astype(jnp.float32)
        out_ref[pl.ds(start, PIECE), :] = piece[:, : 3 * D]
        gains_ref[pl.ds(start, PIECE), :] = piece[:, 3 * D :]


def natural_qkv(near, far, me):
    return pl.pallas_call(
        natural_qkv_kernel,
        out_shape=(
            jax.ShapeDtypeStruct((192, 3 * D), jnp.float32),
            jax.ShapeDtypeStruct((192, 128), jnp.float32),
        ),
        in_specs=[SM, VM, VM],
        out_specs=(VM, VM),
    )(me, near, far)


XZ = [dx | (dz << 1) for dx in range(2) for dz in range(4)]


def masks(*bits):
    order = [0]
    for bit in bits:
        choices = (0, bit) if bit != 6 else (0, 2, 4, 6)
        order = [m | choice for m in order for choice in choices]
    return order


def after(values, *others):
    return lax.optimization_barrier((values,) + others)[0]


def stage(*values):
    return lax.optimization_barrier(values)


def norm_parts(values):
    mean_val = jnp.mean(values, axis=-1, keepdims=True)
    centred = values - mean_val
    variance = jnp.mean(centred * centred, axis=-1, keepdims=True)
    scale = lax.rsqrt(variance + norm_eps)
    return centred * scale, scale


def norm_back(xhat, scale, grad, gain):
    e = grad * gain
    return scale * (
        e
        - jnp.mean(e, axis=-1, keepdims=True)
        - xhat * jnp.mean(e * xhat, axis=-1, keepdims=True)
    )


NT = (((1,), (1,)), ((), ()))
FAR_APART = -1.0e30
MEGA = 1 << 20


def matmul(first, second, dims=None):
    dims = dims or (((1,), (0,)), ((), ()))
    return lax.dot_general(first, second, dims, preferred_element_type=jnp.float32)


def kernel_call(body, outs, scratch, name, flops, moved):
    count = len(outs)
    return lambda *args: pl.pallas_call(
        body,
        out_shape=tuple(jax.ShapeDtypeStruct(shape, kind) for shape, kind in outs),
        in_specs=[SM] + [VM] * (len(args) - 1),
        out_specs=(VM,) * count,
        scratch_shapes=[pltpu.VMEM(shape, kind) for shape, kind in scratch],
        compiler_params=pltpu.CompilerParams(vmem_limit_bytes=56 * MEGA),
        cost_estimate=pl.CostEstimate(flops=flops, bytes_accessed=moved, transcendentals=0),
        name=name,
    )(*args)


def swap_halves(pair):
    lane = lax.broadcasted_iota(jnp.int32, pair.shape, 1) % HD
    return jnp.where(lane < HD // 2, pltpu.roll(pair, 96, 1), pltpu.roll(pair, 32, 1))


def place_rows(me, pieces, whole_ref):
    for mask, piece in pieces:
        start = pl.multiple_of((me // 8 ^ mask) * 192, 16)
        whole_ref[pl.ds(start, 192), :] = piece


def attention_kernel(
    me_ref,
    own_ref,
    across_ref,
    peer_ref,
    mine_ref,
    core_ref,
    up_ref,
    both_ref,
    cos_ref,
    sin_ref,
    normed_ref,
    q_ref,
    k_ref,
    v_ref,
    probs_ref,
    att_own_ref,
    att_peer_ref,
    att_ref,
    inv_ref,
    weight_ref,
    gains_ref,
    q_id_ref,
    keys_ref,
    values_ref,
):
    f32, bf16 = jnp.float32, jnp.bfloat16
    me = me_ref[0]
    shards = (mine_ref, core_ref, up_ref, both_ref)
    place_rows(me, [(mask, ref[:192, :]) for mask, ref in enumerate(shards)], weight_ref)
    gains = sum(ref[192:200, :].astype(f32) for ref in shards)[:, :D]
    gains_ref[...] = gains
    gain = gains[0:1, :]
    row_id = lax.broadcasted_iota(jnp.int32, (128, 128), 0).astype(f32)
    blocks = [own_ref.at[i] for i in range(2)] + [peer_ref.at[0, i] for i in range(2)]
    blocks += [across_ref.at[i] for i in range(2)] + [peer_ref.at[1, i] for i in range(2)]
    for i, block in enumerate(blocks):
        rows = slice(128 * i, 128 * (i + 1))
        hidden = block[:128, :].astype(f32)
        centred = hidden - jnp.mean(hidden, axis=1, keepdims=True)
        variance = jnp.mean(centred * centred, axis=1, keepdims=True)
        normed = (centred * lax.rsqrt(variance + norm_eps) * gain).astype(bf16)
        normed_ref[rows, :] = normed
        ids = block[128:136, :128].astype(f32)[0:1, :]
        hit = jnp.where(row_id == ids, 1.0, 0.0).T
        keys_ref[rows, 128:] = (1.0 - hit).astype(bf16)
        values_ref[rows, 128:] = jnp.ones((128, 128), bf16)
        if i < 4:
            q_id_ref[rows, :] = (hit * FAR_APART).astype(bf16)

    for i in range(4):
        rows = slice(256 * i, 256 * (i + 1))
        normed = normed_ref[rows, :]
        first = 0 if i < 2 else HALF
        qkv = matmul(normed, weight_ref[:, first:])
        for j in range(first // 128, 9):
            part = qkv[:, 128 * j - first : 128 * j - first + 128]
            columns = slice(128 * (j % 3), 128 * (j % 3) + 128)
            if j < 6:
                part = part * cos_ref[rows, :] + swap_halves(part) * sin_ref[rows, :]
            if j < 3:
                q_ref[rows, columns] = (part * HD**-0.5).astype(bf16)
            elif j < 6:
                k_ref[rows, columns] = part.astype(bf16)
            else:
                v_ref[rows, columns] = part.astype(bf16)

    low_head = lax.broadcasted_iota(jnp.int32, (256, 128), 1) < HD
    for pair in range(3):
        columns = slice(128 * pair, 128 * pair + 128)
        keys_ref[:, :128] = k_ref[:, columns]
        values_ref[:, :128] = v_ref[:, columns]
        for i in range(2):
            rows = slice(256 * i, 256 * (i + 1))
            queries = q_ref[rows, columns]
            found = []
            for head in range(2):
                picked = jnp.where(low_head == (head == 0), queries, jnp.zeros_like(queries))
                scores = matmul(
                    jnp.concatenate([picked, q_id_ref[rows, :]], 1), keys_ref[...], NT
                )
                probs = jnp.exp(scores).astype(bf16)
                probs_ref[2 * pair + head, rows, :] = probs
                found.append(matmul(probs, values_ref[...]))
            inverse = 1.0 / jnp.where(low_head, found[0][:, 128:], found[1][:, 128:])
            attended = jnp.where(low_head, found[0][:, :128], found[1][:, :128]) * inverse
            inv_ref[rows, columns] = inverse
            att_ref[rows, columns] = attended
            out_ref = att_own_ref if i == 0 else att_peer_ref
            out_ref[:, columns] = attended.astype(bf16)


def attention_forward(*args):
    f32, bf16 = jnp.float32, jnp.bfloat16
    outs = [
        ((1024, D), bf16),
        ((512, HALF), bf16),
        ((1024, HALF), bf16),
        ((1024, HALF), bf16),
        ((6, 512, 1024), bf16),
        ((256, HALF), bf16),
        ((256, HALF), bf16),
        ((512, HALF), f32),
        ((512, HALF), f32),
        ((D, 3 * HALF), bf16),
        ((8, D), f32),
    ]
    scratch = [((512, 128), bf16), ((1024, 256), bf16), ((1024, 256), bf16)]
    return kernel_call(attention_kernel, outs, scratch, "attention_fwd", 4 * 10**9, 8 * MEGA)(*args)


def put_pieces(me, order, values_ref, out_ref, columns):
    for slot, mask in enumerate(order):
        start = pl.multiple_of((me ^ mask) * PIECE, 8)
        out_ref[slot, :, columns] = values_ref[pl.ds(start, PIECE), :].astype(out_ref.dtype)


def gated_block(normed, grad, gate_rows, upper_rows, down_rows):
    bf16 = jnp.bfloat16
    gate = matmul(normed, gate_rows)
    upper = matmul(normed, upper_rows)
    chance = 0.5 + 0.5 * lax.erf(gate * math.sqrt(0.5))
    bell = jnp.exp(-0.5 * gate * gate) * (1.0 / math.sqrt(2.0 * math.pi))
    gelu = gate * chance
    g_activ = matmul(grad, down_rows)
    g_gate = (g_activ * upper * (chance + gate * bell)).astype(bf16)
    g_upper = (g_activ * gelu).astype(bf16)
    return (gelu * upper).astype(bf16), g_gate, g_upper


WIDTH = 384


def mlp_first_kernel(
    me_ref,
    own_ref,
    att_ref,
    att_peer_ref,
    grad_ref,
    gains_ref,
    near_ref,
    far_ref,
    down_ref,
    g_normed_ref,
    xhat_ref,
    scale_ref,
    w_out_ref,
    away_ref,
    stay_ref,
    w_ref,
    buffer_ref,
):
    f32, bf16 = jnp.float32, jnp.bfloat16
    me = me_ref[0]
    core = (me // 8) % 2
    shards = ((0, near_ref, 0), (2, near_ref, 1), (1, far_ref, 0), (3, far_ref, 1))
    for mask, ref, index in shards:
        shard = me // 8 ^ mask
        head_row = (shard // 2 ^ core) * HALF + (shard % 2) * 192
        w_out_ref[pl.ds(pl.multiple_of(head_row, 16), 192), :] = ref[index, :, :D]
    place_rows(me, [(mask, ref[index, :, D:]) for mask, ref, index in shards], w_ref)

    attended = jnp.concatenate([att_ref[...], att_peer_ref[...]], 1)
    hidden = jnp.concatenate([own_ref[0, :128, :], own_ref[1, :128, :]]).astype(f32)
    mixed = hidden + matmul(attended, w_out_ref[...])
    centred = mixed - jnp.mean(mixed, axis=1, keepdims=True)
    scale = lax.rsqrt(jnp.mean(centred * centred, axis=1, keepdims=True) + norm_eps)
    xhat = centred * scale
    xhat_ref[...] = xhat
    scale_ref[...] = jnp.broadcast_to(scale, (256, 128))
    normed = (xhat * gains_ref[1:2, :]).astype(bf16)
    grad = grad_ref[...]
    normed_t, grad_t = normed.T, grad.T
    y_first, x_first = masks(16, 1, 6), masks(1, 16, 6)

    def emit(values, order, first):
        buffer_ref[...] = values
        columns = slice(first, first + WIDTH)
        put_pieces(me, [m | 8 for m in order], buffer_ref, away_ref, columns)
        put_pieces(me, order, buffer_ref, stay_ref, columns)

    down = mixed
    g_normed = jnp.zeros_like(mixed)
    for i in range(2):
        low, high, last = (slice(first + WIDTH * i, first + WIDTH * (i + 1)) for first in (0, 768, 1536))
        activ, g_gate, g_upper = gated_block(normed, grad, w_ref[:, low], w_ref[:, high], w_ref[:, last])
        down = down + matmul(activ, w_ref[:, last], NT)
        g_normed = g_normed + matmul(g_gate, w_ref[:, low], NT)
        g_normed = g_normed + matmul(g_upper, w_ref[:, high], NT)
        emit(matmul(normed_t, g_gate), y_first, WIDTH * i)
        emit(matmul(normed_t, g_upper), y_first if i == 0 else x_first, 768 + WIDTH * i)
        emit(matmul(grad_t, activ), x_first, 1536 + WIDTH * i)
    down_ref[...] = down
    g_normed_ref[...] = g_normed


def mlp_first(*args):
    f32, bf16 = jnp.float32, jnp.bfloat16
    outs = [
        ((256, D), f32),
        ((256, D), f32),
        ((256, D), f32),
        ((256, 128), f32),
        ((D, D), bf16),
        ((16, PIECE, 6 * WIDTH), bf16),
        ((16, PIECE, 6 * WIDTH), bf16),
    ]
    scratch = [((D, 6 * WIDTH), bf16), ((D, WIDTH), f32)]
    return kernel_call(mlp_first_kernel, outs, scratch, "mlp_first", 3 * 10**9, 16 * MEGA)(*args)


def mlp_second_kernel(
    me_ref,
    att_ref,
    att_peer_ref,
    grad_ref,
    gains_ref,
    near_ref,
    far_ref,
    down_ref,
    g_normed_ref,
    xhat_ref,
    scale_ref,
    w_out_ref,
    out_ref,
    g_mixed_ref,
    g_att_ref,
    g_att_peer_ref,
    away_ref,
    stay_ref,
    g_gain_ref,
    w_ref,
    buffer_ref,
):
    f32, bf16 = jnp.float32, jnp.bfloat16
    me = me_ref[0]
    core = (me // 8) % 2
    shards = ((0, near_ref, 0), (2, near_ref, 1), (1, far_ref, 0), (3, far_ref, 1))
    place_rows(me, [(mask, ref[index]) for mask, ref, index in shards], w_ref)
    gain = gains_ref[1:2, :]
    xhat = xhat_ref[...]
    scale = scale_ref[:, 0:1]
    normed = (xhat * gain).astype(bf16)
    grad = grad_ref[...]
    normed_t, grad_t = normed.T, grad.T
    y_first, x_first = masks(16, 1, 6), masks(1, 16, 6)

    def emit(order, first):
        columns = slice(first, first + WIDTH)
        put_pieces(me, [m | 8 for m in order], buffer_ref, away_ref, columns)
        put_pieces(me, order, buffer_ref, stay_ref, columns)

    low, high, last = (slice(first, first + WIDTH) for first in (0, 384, 768))
    activ, g_gate, g_upper = gated_block(normed, grad, w_ref[:, low], w_ref[:, high], w_ref[:, last])
    g_normed = g_normed_ref[...] + matmul(g_gate, w_ref[:, low], NT)
    g_normed = g_normed + matmul(g_upper, w_ref[:, high], NT)
    e = g_normed * gain
    g_mixed = grad.astype(f32) + scale * (
        e
        - jnp.mean(e, axis=1, keepdims=True)
        - xhat * jnp.mean(e * xhat, axis=1, keepdims=True)
    )
    g_mixed_ref[...] = g_mixed
    g_low = g_mixed.astype(bf16)
    g_att = matmul(g_low, w_out_ref[...], NT).astype(bf16)
    g_att_ref[...] = g_att[:, :HALF]
    g_att_peer_ref[...] = g_att[:, HALF:]
    out_ref[...] = (down_ref[...] + matmul(activ, w_ref[:, last], NT)).astype(bf16)
    g_gain = jnp.broadcast_to(jnp.sum(xhat * g_normed, axis=0, keepdims=True), (128, D))
    row = lax.broadcasted_iota(jnp.int32, (128, D), 0)
    g_gain_ref[...] = jnp.where(row == 1, g_gain, 0.0).T
    buffer_ref[...] = matmul(normed_t, g_gate)
    emit(y_first, 0)
    buffer_ref[...] = matmul(normed_t, g_upper)
    emit(y_first, WIDTH)
    buffer_ref[...] = matmul(grad_t, activ)
    emit(x_first, 3 * WIDTH)
    attended_t = jnp.concatenate([att_ref[...], att_peer_ref[...]], 1).T
    for i in range(2):
        rows_out = matmul(attended_t, g_low[:, WIDTH * i : WIDTH * (i + 1)])
        for half in range(2):
            start = pl.multiple_of((half ^ core) * HALF, HALF)
            buffer_ref[pl.ds(start, HALF), :] = rows_out[HALF * half : HALF * (half + 1), :]
        emit(y_first if i == 0 else x_first, (2 + 2 * i) * WIDTH)


def mlp_second(*args):
    f32, bf16 = jnp.float32, jnp.bfloat16
    outs = [
        ((256, D), bf16),
        ((256, D), f32),
        ((256, HALF), bf16),
        ((256, HALF), bf16),
        ((16, PIECE, 5 * WIDTH), bf16),
        ((16, PIECE, 5 * WIDTH), bf16),
        ((D, 128), f32),
    ]
    scratch = [((D, 3 * WIDTH), bf16), ((D, WIDTH), f32)]
    return kernel_call(mlp_second_kernel, outs, scratch, "mlp_second", 2 * 10**9, 10 * MEGA)(*args)


def attention_back_kernel(
    me_ref,
    g_own_ref,
    g_peer_ref,
    att_ref,
    inv_ref,
    q_ref,
    k_ref,
    v_ref,
    probs_ref,
    cos_ref,
    sin_ref,
    dq_ref,
    dk_ref,
    dv_ref,
    values_ref,
):
    f32, bf16 = jnp.float32, jnp.bfloat16
    low_head = lax.broadcasted_iota(jnp.int32, (1024, 128), 1) < HD
    lane = lax.broadcasted_iota(jnp.int32, (512, 128), 1)
    values_ref[:, 128:] = jnp.ones((1024, 128), bf16)
    for pair in range(3):
        columns = slice(128 * pair, 128 * pair + 128)
        values_ref[:, :128] = v_ref[:, columns]
        queries_t, keys = q_ref[:, columns].T, k_ref[:, columns]
        grad = jnp.concatenate([g_own_ref[:, columns], g_peer_ref[:, columns]]).astype(f32)
        grad = grad * inv_ref[:, columns]
        terms = grad * att_ref[:, columns]
        grad = grad.astype(bf16)
        grad_t = grad.T
        g_queries = jnp.zeros((512, 128), f32)
        g_keys, g_values = [], []
        for head in range(2):
            mine = low_head == (head == 0)
            rows = slice(HD * head, HD * head + HD)
            row = jnp.sum(jnp.where(mine[:512], terms, 0.0), axis=1, keepdims=True)
            high = row.astype(bf16)
            middle = (row - high.astype(f32)).astype(bf16)
            rest = (row - high.astype(f32) - middle.astype(f32)).astype(bf16)
            extra = jnp.where(lane == 0, -high.astype(f32), 0.0)
            extra = jnp.where(lane == 1, -middle.astype(f32), extra)
            extra = jnp.where(lane == 2, -rest.astype(f32), extra).astype(bf16)
            picked = jnp.where(mine[:512], grad, jnp.zeros_like(grad))
            product = matmul(jnp.concatenate([picked, extra], 1), values_ref[...], NT)
            probs = probs_ref[2 * pair + head]
            g_scores = (probs.astype(f32) * product).astype(bf16)
            g_queries = g_queries + matmul(g_scores, jnp.where(mine, keys, jnp.zeros_like(keys)))
            g_keys.append(matmul(queries_t[rows, :], g_scores))
            g_values.append(matmul(grad_t[rows, :], probs))
        g_queries = g_queries * HD**-0.5
        near = slice(0, 512)
        dq_ref[:, columns] = (
            g_queries * cos_ref[near, :] - swap_halves(g_queries) * sin_ref[near, :]
        ).astype(bf16)
        g_keys = jnp.concatenate(g_keys).T
        dk_ref[:, columns] = (
            g_keys * cos_ref[...] - swap_halves(g_keys) * sin_ref[...]
        ).astype(bf16)
        dv_ref[:, columns] = jnp.concatenate(g_values).T.astype(bf16)


def attention_backward(*args):
    bf16 = jnp.bfloat16
    outs = [((512, HALF), bf16), ((1024, HALF), bf16), ((1024, HALF), bf16)]
    scratch = [((1024, 256), bf16)]
    return kernel_call(
        attention_back_kernel, outs, scratch, "attention_bwd", 5 * 10**9, 10 * MEGA
    )(*args)


def qkv_weight_kernel(
    me_ref,
    normed_ref,
    weight_ref,
    g_gain_ref,
    dq_ref,
    dk_ref,
    dv_ref,
    keep_a,
    away_a,
    keep_b,
    away_b,
    buffer_ref,
):
    me = me_ref[0]
    order_a, order_b = masks(1, 6), masks(16, 6)
    normed_t = normed_ref[...].T

    def emit(values_ref, columns):
        put_pieces(me, order_a, values_ref, keep_a, columns)
        put_pieces(me, [m | 16 for m in order_a], values_ref, away_a, columns)
        put_pieces(me, [m | 8 for m in order_b], values_ref, keep_b, columns)
        put_pieces(me, [m | 9 for m in order_b], values_ref, away_b, columns)

    g_gain = jnp.zeros((D, 1), jnp.float32)
    for i, ref in enumerate((dq_ref, dk_ref, dv_ref)):
        columns = slice(HALF * i, HALF * (i + 1))
        values = matmul(normed_t[:, : ref.shape[0]], ref[...])
        weight = weight_ref[:, columns].astype(jnp.float32)
        g_gain = g_gain + jnp.sum(values * weight, axis=1, keepdims=True)
        buffer_ref[...] = values
        emit(buffer_ref, columns)
    lane = lax.broadcasted_iota(jnp.int32, (D, 128), 1)
    buffer_ref[:, :128] = jnp.where(lane == 0, g_gain, g_gain_ref[...])
    emit(buffer_ref.at[:, :128], slice(3 * HALF, 3 * HALF + 128))


def qkv_weight_gradient(*args):
    outs = [((8, PIECE, 3 * HALF + 128), jnp.bfloat16)] * 4
    scratch = [((D, HALF), jnp.float32)]
    return kernel_call(qkv_weight_kernel, outs, scratch, "qkv_weights", 2 * 10**9, 8 * MEGA)(*args)


def qkv_input_kernel(me_ref, weight_ref, dq_ref, dk_ref, dv_ref, own_ref, across_ref, peer_ref):
    targets = (own_ref, peer_ref.at[0], across_ref, peer_ref.at[1])
    for i, target in enumerate(targets):
        rows = slice(256 * i, 256 * (i + 1))
        grad = matmul(dk_ref[rows, :], weight_ref[:, HALF : 2 * HALF], NT)
        grad = grad + matmul(dv_ref[rows, :], weight_ref[:, 2 * HALF :], NT)
        if i < 2:
            grad = grad + matmul(dq_ref[rows, :], weight_ref[:, :HALF], NT)
        target[...] = grad.astype(target.dtype)


def qkv_input_gradient(*args):
    bf16 = jnp.bfloat16
    outs = [((256, D), bf16), ((256, D), bf16), ((2, 256, D), bf16)]
    return kernel_call(qkv_input_kernel, outs, [], "qkv_inputs", 2 * 10**9, 6 * MEGA)(*args)


def paired_chips(hidden_in, grad_out, segment_ids, w_qkv, w_out, w_in, w_down, gain_attn, gain_mlp):
    bf16, f32 = jnp.bfloat16, jnp.float32
    dp, ctx = lax.axis_index("dp"), lax.axis_index("ctx")
    me = dp * 8 + ctx
    me_ref = me.reshape(1).astype(jnp.int32)
    c, zl, x = dp % 2, (ctx // 2) % 2, ctx % 2
    rows = hidden_in.shape[1]

    def to_chips(values):
        return (
            send_swapped(pick(zl, values[0], values[1]), 0),
            send_swapped(pick(zl, values[1], values[0]), 2),
        )

    def from_chips(values):
        block_a, block_b = send_swapped(values[:rows], 0), send_swapped(values[rows:], 2)
        return jnp.stack([pick(zl, block_a, block_b), pick(zl, block_b, block_a)])

    ids = jnp.pad(segment_ids[:, None, :], ((0, 0), (0, 7), (0, D - rows))).astype(bf16)
    packed = [pick(zl, a, b) for a, b in ((hidden_in, hidden_in[::-1]), (ids, ids[::-1]))]
    packed = jnp.concatenate(packed, 1)

    gains = lax.dynamic_update_slice(
        jnp.zeros((8, 3 * HALF), f32), jnp.stack([gain_attn, gain_mlp]), (0, 192 * dp)
    )

    def my_columns(core):
        columns = [lax.dynamic_slice_in_dim(w_qkv, t * D + core * HALF, HALF, 1) for t in range(3)]
        return jnp.concatenate([jnp.concatenate(columns, 1), gains]).astype(bf16)

    mine, other = my_columns(c), my_columns(1 - c)
    by_y, by_both = send(mine, 16), send(other, 24)
    own = send_swapped(packed[0], 0), send_swapped(packed[1], 2)
    by_core = send(other, 8)
    own, by_core = stage(jnp.stack(own), by_core)
    across = send(own, 1)
    grad_low = jnp.concatenate(to_chips(after(grad_out, own)))
    w_down = w_down.T
    cut, rest = slice(0, 768), slice(768, FF)
    late = slice(FF + 768, None)
    first = jnp.concatenate([w_out, w_in[:, cut], w_in[:, FF : FF + 768], w_down[:, cut]], 1)
    second = jnp.concatenate([w_in[:, rest], w_in[:, late], w_down[:, rest]], 1)
    first, second = first.astype(bf16), second.astype(bf16)
    across, by_y, by_both, first, grad_low = stage(across, by_y, by_both, first, grad_low)
    got_first = send(first, 16)
    peer = send(jnp.stack([own, across]), 8)

    def both_cores(shard, got):
        pair = jnp.stack([shard, got])
        return pair, send(pair, 8)

    within = jnp.arange(rows, dtype=jnp.int32)
    starts = []
    for far in range(2):
        for core in range(2):
            for low in range(2):
                starts.append((2 * (2 * (c ^ core) + (zl ^ low)) + (x ^ far)) * rows + within)
    cosine, sine = rotary_tables(jnp.concatenate(starts), HD)
    sine = sine * jnp.where(jnp.arange(HD) < HD // 2, -1.0, 1.0)
    cosine, sine = jnp.concatenate([cosine] * 2, 1), jnp.concatenate([sine] * 2, 1)

    normed, queries, keys, values, probs, att_own, att_peer, att, inverse, weight, gains = (
        attention_forward(
            me_ref, own, across, peer, mine, by_core, by_y, by_both, cosine, sine
        )
    )
    att_peer = send(att_peer, 8)
    got_first, att_peer, second = stage(got_first, att_peer, second)
    got_second = send(second, 16)
    first, first_far = both_cores(first, got_first)
    got_second, first_far = stage(got_second, first_far)
    second, second_far = both_cores(second, got_second)
    down, g_norm, xhat, scale, w_out, away_1, stay_1 = mlp_first(
        me_ref, own, att_own, att_peer, grad_low, gains, first, first_far
    )

    def halves(values, got):
        count = values.shape[0] // 2
        return [
            plus(values[part, :, columns], got[part, :, columns])
            for columns in (slice(0, 3 * WIDTH), slice(3 * WIDTH, None))
            for part in (slice(0, count), slice(count, None))
        ]

    def fold(stay, got):
        return plus(stay[:4], got[:4]), plus(stay[4:], got[4:])

    def fold_near(part):
        return jnp.stack([part[0], part[2]]), jnp.stack([part[1], part[3]])

    def natural(part, far):
        return to_natural(jnp.concatenate([part, far]), me_ref % 8, XZ, f32)

    def joined(stay_a, got_a, stay_b, got_b):
        return fold_near(jnp.concatenate([plus(stay_a, got_a), plus(stay_b, got_b)], 2))

    away_1, second_far, down = stage(away_1, second_far, down)
    got_1 = send(away_1, 8)
    layer_out, g_mixed, g_att, g_att_peer, away_2, stay_2, g_gain = mlp_second(
        me_ref, att_own, att_peer, grad_low, gains, second, second_far, down, g_norm, xhat, scale, w_out
    )
    got_1, away_2, g_att_peer, layer_out = stage(got_1, away_2, g_att_peer, layer_out)
    g_att_peer = send(g_att_peer, 8)
    got_2 = send(away_2, 8)
    stay_1a, leave_a, stay_1b, leave_b = halves(stay_1, got_1)
    got_1a, got_1b = send(leave_a, 16), send(leave_b, 1)
    g_att_peer, layer_out = stage(g_att_peer, layer_out)
    layer_out = from_chips(layer_out)
    grads = attention_backward(
        me_ref, g_att, g_att_peer, att, inverse, queries, keys, values, probs, cosine, sine
    )
    got_1a, got_1b, got_2, layer_out, *grads = stage(got_1a, got_1b, got_2, layer_out, *grads)

    stay_1a, leave_1a = fold(stay_1a, got_1a)
    stay_1b, leave_1b = fold(stay_1b, got_1b)
    got_1a, got_1b = send(leave_1a, 1), send(leave_1b, 16)
    stay_2a, leave_a, stay_2b, leave_b = halves(stay_2, got_2)
    got_2a, got_2b = send(leave_a, 16), send(leave_b, 1)
    g_gain, *_ = stage(g_gain, leave_1a, leave_1b, leave_a, leave_b)
    keep_a, away_a, keep_b, away_b = qkv_weight_gradient(me_ref, normed, weight, g_gain, *grads)

    got_1a, got_1b, away_a, away_b, *grads = stage(got_1a, got_1b, away_a, away_b, *grads)
    got_a, got_b = send(away_a, 16), send(away_b, 1)
    keep_1, leave_1 = joined(stay_1a, got_1a, stay_1b, got_1b)
    got_1 = send(leave_1, 2)
    weight, _ = stage(weight, leave_1)
    near, across, peer = qkv_input_gradient(me_ref, weight, *grads)

    got_2a, got_2b, got_1, near, across, peer = stage(got_2a, got_2b, got_1, near, across, peer)
    peer = send(peer, 8)
    stay_2a, leave_2a = fold(stay_2a, got_2a)
    stay_2b, leave_2b = fold(stay_2b, got_2b)
    got_2a, got_2b = send(leave_2a, 1), send(leave_2b, 16)
    keep_1 = plus(keep_1, got_1)
    peer, keep_1, *_ = stage(peer, keep_1, leave_2a, leave_2b)
    got_1 = send(keep_1[1], 4)
    across = plus(across, peer[1])
    got_a, got_b, across, *_ = stage(got_a, got_b, across, keep_1, leave_2a, leave_2b)

    stay_a, leave_a = fold(keep_a, got_a)
    stay_b, leave_b = fold(keep_b, got_b)
    got_a, got_b = send(leave_a, 1), send(leave_b, 16)
    got_1, got_2a, got_2b, across, *_ = stage(got_1, got_2a, got_2b, across, leave_a, leave_b)
    sum_1 = plus(keep_1[0], got_1)
    far_1 = send(sum_1, 4)
    keep_2, leave_2 = joined(stay_2a, got_2a, stay_2b, got_2b)
    got_2 = send(leave_2, 2)
    got_across = send(across, 1)
    got_a, got_b, *_ = stage(got_a, got_b, sum_1, leave_2, across)

    total = jnp.concatenate([plus(stay_a, got_a), plus(stay_b, got_b)], 2)
    got = [send(total[dz], 2 * dz) for dz in range(1, 4)]
    far_1, got_2, got_across, _ = stage(far_1, got_2, got_across, total)
    sum_1 = jnp.stack([sum_1, far_1])
    far_1 = send(sum_1, 2)
    keep_2 = plus(keep_2, got_2)
    got_2 = send(keep_2[1], 4)
    g_normed = plus(near, peer[0]).astype(f32) + got_across.astype(f32)
    xhat, scale = norm_parts(own[:, :rows].reshape(2 * rows, D).astype(f32))
    grad_in = (g_mixed + norm_back(xhat, scale, g_normed, gains[0])).astype(bf16)
    grad_in, _, _, *got = stage(grad_in, sum_1, keep_2, *got)

    total = sum((part.astype(f32) for part in got), total[0].astype(f32)).astype(bf16)
    wide = 3 * HALF
    other = send(total[:, wide + 128 :], 8)
    far_1, got_2, _ = stage(far_1, got_2, total)
    sum_1 = jnp.stack([sum_1, far_1], 1).reshape(4, PIECE, -1)
    far_1 = send(sum_1, 1)
    sum_2 = plus(keep_2[0], got_2)
    far_2 = send(sum_2, 4)
    other, *_ = stage(other, sum_1, sum_2)

    total = total[:, : wide + 128]
    low, high = pick(c, total, other), pick(c, other, total)
    total = jnp.concatenate(
        [h[:, t * HALF : (t + 1) * HALF] for t in range(3) for h in (low, high)]
        + [plus(total[:, wide:], other[:, wide:])],
        1,
    )
    got = [send(total, 2 * dz) for dz in range(1, 4)]
    far_2, _ = stage(far_2, total)
    sum_2 = jnp.stack([sum_2, far_2])
    far_2 = send(sum_2, 2)
    far_1, far_2 = stage(far_1, far_2)
    sum_2 = jnp.stack([sum_2, far_2], 1).reshape(4, PIECE, -1)
    far_2 = send(sum_2, 1)
    total, grad_in, _, *got = stage(total, grad_in, sum_2, *got)
    total = jnp.stack([total, *got])
    far = send(total, 1)
    grad_in, _ = stage(grad_in, total)
    grad_in = from_chips(grad_in)
    sum_1, sum_2 = natural(sum_1, far_1), natural(sum_2, far_2)
    g_w_in = jnp.concatenate(
        [sum_1[:, :768], sum_2[:, :384], sum_1[:, 768:1536], sum_2[:, 384:768]], 1
    )
    g_w_out = jnp.concatenate([sum_2[:, 768:1152], sum_2[:, 1536:]], 1)
    g_w_down = jnp.concatenate([sum_1[:, 1536:], sum_2[:, 1152:1536]], 1)
    g_w_qkv, total = natural_qkv(total, far, me_ref % 8)
    g_gain_attn = total[:, 0] / gain_attn.astype(bf16).astype(f32)
    g_gain_mlp = total[:, 1]
    return (layer_out, grad_in, g_w_qkv, g_w_out, g_w_in, g_w_down.T, g_gain_attn, g_gain_mlp)


def solution(mesh):
    whole_fit = mesh.shape["dp"] == 4 and mesh.shape["ctx"] == 8
    return jax.shard_map(
        paired_chips if whole_fit else on_device,
        mesh=mesh,
        in_specs=(
            P("dp", "ctx", None),
            P("dp", "ctx", None),
            P("dp", "ctx"),
            P("dp", None),
            P("dp", None),
            P("dp", None),
            P(None, "dp"),
            P("dp"),
            P("dp"),
        ),
        out_specs=(
            P("dp", "ctx", None),
            P("dp", "ctx", None),
            P("dp", None),
            P("dp", None),
            P("dp", None),
            P(None, "dp"),
            P("dp"),
            P("dp"),
        ),
        check_vma=False,
    )
```

```python
import math

import jax
import jax.numpy as jnp
from jax import lax
from jax.experimental import pallas as pl
from jax.experimental.pallas import tpu as pltpu
from jax.sharding import PartitionSpec as P

D = 768
HEADS = 12
HD = 64
FF = 1152


norm_eps = 1e-05
theta_base = 160000.0


def layer_norm(values, gain):
    mean_val = jnp.mean(values, axis=-1, keepdims=True)
    centred = values - mean_val
    variance = jnp.mean(centred * centred, axis=-1, keepdims=True)
    return centred * lax.rsqrt(variance + norm_eps) * gain


def rotary_tables(positions, head_size):
    half_size = head_size // 2
    exponents = jnp.arange(half_size, dtype=jnp.float32) * (2.0 / head_size)
    inv_freq = 1.0 / theta_base**exponents
    angles = positions.astype(jnp.float32)[:, None] * inv_freq[None, :]
    cosine = jnp.cos(angles)
    sine = jnp.sin(angles)
    return (jnp.concatenate([cosine, cosine], -1), jnp.concatenate([sine, sine], -1))


def rotate(values, cosine, sine):
    half_size = values.shape[-1] // 2
    turned = jnp.concatenate([-values[..., half_size:], values[..., :half_size]], -1)
    return values * cosine[:, None, :] + turned * sine[:, None, :]


def fold_blocks(carry, pieces, piece_segments, work, rows):
    count = piece_segments.shape[0]
    size = math.gcd(count, 4 * rows)
    number = count // size
    blocks = tuple((part.reshape((number, size) + part.shape[1:]) for part in pieces))
    blocks = blocks + (piece_segments.reshape(number, size),)

    def step(acc, block):
        acc = work(acc, block)
        return (acc, None)

    carry, _ = lax.scan(step, carry, blocks)
    return carry


def on_device(hidden_in, grad_out, segment_ids, w_qkv, w_out, w_in, w_down, gain_attn, gain_mlp):
    rows = hidden_in.shape[1]
    local_seqs = hidden_in.shape[0]
    score_scale = HD ** (-0.5)
    bf16 = jnp.bfloat16
    f32 = jnp.float32
    gathered = (
        lax.all_gather(w_qkv.astype(bf16), "dp", axis=0, tiled=True),
        lax.all_gather(w_out.astype(bf16), "dp", axis=0, tiled=True),
        lax.all_gather(w_in.astype(bf16), "dp", axis=0, tiled=True),
        lax.all_gather(w_down.astype(bf16), "dp", axis=1, tiled=True),
        lax.all_gather(gain_attn.astype(bf16), "dp", axis=0, tiled=True),
        lax.all_gather(gain_mlp.astype(bf16), "dp", axis=0, tiled=True),
    )
    weight_qkv, weight_out, weight_in, weight_down, gain_low_a, gain_low_b = gathered
    gain_first = gain_low_a.astype(f32)
    gain_second = gain_low_b.astype(f32)
    whole_segments = lax.all_gather(segment_ids, "ctx", axis=1, tiled=True)
    positions = lax.axis_index("ctx") * rows + jnp.arange(rows, dtype=jnp.int32)
    cosine, sine = rotary_tables(positions, HD)

    def gated(values_in):
        return jax.nn.gelu(values_in[:, :FF], approximate=False) * values_in[:, FF:]

    def turn(pair):
        return (rotate(pair[0], cosine, sine), rotate(pair[1], cosine, sine))

    def one_sequence(seq_index):
        hidden = hidden_in[seq_index].astype(f32)
        own_segments = segment_ids[seq_index]
        all_segments = whole_segments[seq_index]
        normed_first, first_back = jax.vjp(layer_norm, hidden, gain_first)
        normed_attn = normed_first.astype(bf16)
        qkv = jnp.dot(normed_attn, weight_qkv, preferred_element_type=f32)
        q_lin = qkv[:, :D].reshape(rows, HEADS, HD)
        k_lin = qkv[:, D : 2 * D].reshape(rows, HEADS, HD)
        v_lin = qkv[:, 2 * D :].reshape(rows, HEADS, HD)
        turned, turn_back = jax.vjp(turn, (q_lin, k_lin))
        queries = turned[0].astype(bf16)
        keys = turned[1].astype(bf16)
        values = v_lin.astype(bf16)

        def forward_work(acc, block):
            key_blk, value_blk, seg_blk = block
            total, summed = acc
            scores = (
                jnp.einsum("thd,shd->hts", queries, key_blk, preferred_element_type=f32)
                * score_scale
            )
            same = own_segments[:, None] == seg_blk[None, :]
            expo = jnp.where(same[None], jnp.exp(scores), 0.0)
            total = total + jnp.sum(expo, axis=-1)
            summed = summed + jnp.einsum(
                "hts,shd->thd", expo.astype(bf16), value_blk, preferred_element_type=f32
            )
            return (total, summed)

        start_fwd = (jnp.zeros((HEADS, rows), f32), jnp.zeros((rows, HEADS, HD), f32))
        key_piece = lax.all_gather(keys.reshape(rows, D), "ctx", axis=0, tiled=True)
        value_piece = lax.all_gather(values.reshape(rows, D), "ctx", axis=0, tiled=True)
        count = key_piece.shape[0]
        piece_segments = all_segments
        parts = (key_piece.reshape(count, HEADS, HD), value_piece.reshape(count, HEADS, HD))
        total, summed = fold_blocks(start_fwd, parts, piece_segments, forward_work, rows)
        total_rows = jnp.transpose(total)
        attended = (summed / total_rows[:, :, None]).reshape(rows, D).astype(bf16)
        mixed = hidden + jnp.dot(attended, weight_out, preferred_element_type=f32)
        normed_second, second_back = jax.vjp(layer_norm, mixed, gain_second)
        normed_mlp = normed_second.astype(bf16)
        gate_up = jnp.dot(normed_mlp, weight_in, preferred_element_type=f32)
        activ_f, gated_back = jax.vjp(gated, gate_up)
        activ = activ_f.astype(bf16)
        layer_out = (mixed + jnp.dot(activ, weight_down, preferred_element_type=f32)).astype(bf16)
        grad_low = grad_out[seq_index]
        g_w_down = jnp.einsum("tf,td->fd", activ, grad_low, preferred_element_type=f32)
        g_activ = jnp.einsum("td,fd->tf", grad_low, weight_down, preferred_element_type=f32)
        g_gate_up = gated_back(g_activ)[0].astype(bf16)
        g_w_in = jnp.einsum("ti,tj->ij", normed_mlp, g_gate_up, preferred_element_type=f32)
        g_normed_mlp = jnp.einsum("tj,ij->ti", g_gate_up, weight_in, preferred_element_type=f32)
        g_mixed_norm, g_gain_mlp = second_back(g_normed_mlp)
        g_mixed = grad_low.astype(f32) + g_mixed_norm
        g_mixed_low = g_mixed.astype(bf16)
        g_w_out = jnp.einsum("ti,tj->ij", attended, g_mixed_low, preferred_element_type=f32)
        g_att = jnp.einsum(
            "tj,ij->ti", g_mixed_low, weight_out, preferred_element_type=f32
        ).reshape(rows, HEADS, HD)
        g_summed = (g_att / total_rows[:, :, None]).astype(bf16)
        row_term = jnp.sum(g_att * summed, axis=-1) / (total_rows * total_rows)
        own_rows = jnp.transpose(row_term)
        all_rows = lax.all_gather(row_term, "ctx", axis=0, tiled=True)

        def query_work(acc, block):
            key_blk, value_blk, seg_blk = block
            scores = (
                jnp.einsum("thd,shd->hts", queries, key_blk, preferred_element_type=f32)
                * score_scale
            )
            same = own_segments[:, None] == seg_blk[None, :]
            expo = jnp.where(same[None], jnp.exp(scores), 0.0)
            product = jnp.einsum("thd,shd->hts", g_summed, value_blk, preferred_element_type=f32)
            g_scores = (expo * (product - own_rows[:, :, None])).astype(bf16)
            return acc + jnp.einsum("hts,shd->thd", g_scores, key_blk, preferred_element_type=f32)

        key_piece = lax.all_gather(keys.reshape(rows, D), "ctx", axis=0, tiled=True)
        value_piece = lax.all_gather(values.reshape(rows, D), "ctx", axis=0, tiled=True)
        count = key_piece.shape[0]
        piece_segments = all_segments
        parts = (key_piece.reshape(count, HEADS, HD), value_piece.reshape(count, HEADS, HD))
        g_queries = (
            fold_blocks(jnp.zeros((rows, HEADS, HD), f32), parts, piece_segments, query_work, rows)
            * score_scale
        )

        def key_work(acc, block):
            query_blk, gsum_blk, row_blk, seg_blk = block
            g_keys, g_values = acc
            scores = (
                jnp.einsum("shd,thd->hst", query_blk, keys, preferred_element_type=f32)
                * score_scale
            )
            same = seg_blk[:, None] == own_segments[None, :]
            expo = jnp.where(same[None], jnp.exp(scores), 0.0)
            g_values = g_values + jnp.einsum(
                "hst,shd->thd", expo.astype(bf16), gsum_blk, preferred_element_type=f32
            )
            product = jnp.einsum("shd,thd->hst", gsum_blk, values, preferred_element_type=f32)
            g_scores = (expo * (product - jnp.transpose(row_blk)[:, :, None])).astype(bf16)
            g_keys = g_keys + jnp.einsum(
                "hst,shd->thd", g_scores, query_blk, preferred_element_type=f32
            )
            return (g_keys, g_values)

        start_keys = (jnp.zeros((rows, HEADS, HD), f32), jnp.zeros((rows, HEADS, HD), f32))
        query_piece = lax.all_gather(queries.reshape(rows, D), "ctx", axis=0, tiled=True)
        gsum_piece = lax.all_gather(g_summed.reshape(rows, D), "ctx", axis=0, tiled=True)
        count = query_piece.shape[0]
        piece_segments = all_segments
        parts = (
            query_piece.reshape(count, HEADS, HD),
            gsum_piece.reshape(count, HEADS, HD),
            all_rows,
        )
        g_keys, g_values = fold_blocks(start_keys, parts, piece_segments, key_work, rows)
        g_keys = g_keys * score_scale
        unturned = turn_back((g_queries, g_keys))[0]
        g_qkv = jnp.concatenate(
            [unturned[0].reshape(rows, D), unturned[1].reshape(rows, D), g_values.reshape(rows, D)],
            -1,
        ).astype(bf16)
        g_w_qkv = jnp.einsum("ti,tj->ij", normed_attn, g_qkv, preferred_element_type=f32)
        g_normed_attn = jnp.einsum("tj,ij->ti", g_qkv, weight_qkv, preferred_element_type=f32)
        g_hidden_norm, g_gain_attn = first_back(g_normed_attn)
        grad_in = (g_mixed + g_hidden_norm).astype(bf16)
        terms = (g_w_qkv, g_w_out, g_w_in, g_w_down, g_gain_attn, g_gain_mlp)
        return (layer_out, grad_in, terms)

    outputs_fwd = []
    outputs_back = []
    terms = None
    for seq_index in range(local_seqs):
        layer_out, grad_in, seq_terms = one_sequence(seq_index)
        outputs_fwd.append(layer_out)
        outputs_back.append(grad_in)
        if terms is None:
            terms = seq_terms
        else:
            terms = tuple((old + new for old, new in zip(terms, seq_terms)))
    everywhere = lax.psum(terms, "ctx")
    owned = (
        lax.psum_scatter(
            everywhere[0].astype(jnp.bfloat16), "dp", scatter_dimension=0, tiled=True
        ).astype(jnp.float32),
        lax.psum_scatter(
            everywhere[1].astype(jnp.bfloat16), "dp", scatter_dimension=0, tiled=True
        ).astype(jnp.float32),
        lax.psum_scatter(
            everywhere[2].astype(jnp.bfloat16), "dp", scatter_dimension=0, tiled=True
        ).astype(jnp.float32),
        lax.psum_scatter(
            everywhere[3].astype(jnp.bfloat16), "dp", scatter_dimension=1, tiled=True
        ).astype(jnp.float32),
        lax.psum_scatter(
            everywhere[4].astype(jnp.bfloat16), "dp", scatter_dimension=0, tiled=True
        ).astype(jnp.float32),
        lax.psum_scatter(
            everywhere[5].astype(jnp.bfloat16), "dp", scatter_dimension=0, tiled=True
        ).astype(jnp.float32),
    )
    return (
        jnp.stack(outputs_fwd),
        jnp.stack(outputs_back),
        owned[0],
        owned[1],
        owned[2],
        owned[3],
        owned[4],
        owned[5],
    )


HALF = 384
PIECE = 24


def send(values, mask):
    return lax.ppermute(values, ("dp", "ctx"), [(i, i ^ mask) for i in range(32)])


def send_swapped(values, mask):
    def target(i):
        core, high = (i >> 3) & 1, (i >> 2) & 1
        return (i & ~12) | (high << 3) | (core << 2)

    return lax.ppermute(values, ("dp", "ctx"), [(i, target(i) ^ mask) for i in range(32)])


def pick(flag, first, second):
    return jnp.where(flag == 0, first, second)


VM = pl.BlockSpec(memory_space=pltpu.VMEM)
SM = pl.BlockSpec(memory_space=pltpu.SMEM)


def pieces_of(me, near_ref, far_ref):
    for slot, mask in enumerate(XZ):
        start = pl.multiple_of((me % 8 ^ mask) * PIECE, 8)
        yield start, (near_ref, far_ref)[slot // 4][slot % 4].astype(jnp.float32)


def qkv_result_kernel(me_ref, near_ref, far_ref, out_ref, gains_ref, buffer_ref):
    me = me_ref[0]
    core = (me // 8) % 2
    wide = 3 * HALF + 128
    for start, piece in pieces_of(me, near_ref, far_ref):
        rows = pl.ds(start, PIECE)
        for half in range(2):
            for t in range(3):
                column = pl.multiple_of(t * D + (half ^ core) * HALF, 128)
                first = half * wide + t * HALF
                out_ref[rows, pl.ds(column, HALF)] = piece[:, first : first + HALF]
        buffer_ref[rows, :] = piece[:, 3 * HALF : wide] + piece[:, wide + 3 * HALF :]
    gains_ref[...] = buffer_ref[...].T[:8, :192]


def mlp_result_kernel(
    me_ref, near_1, far_1, near_2, far_2, w_in_ref, w_out_ref, w_down_ref
):
    me = me_ref[0]
    for start, piece in pieces_of(me, near_1, far_1):
        rows = pl.ds(start, PIECE)
        w_in_ref[rows, :768] = piece[:, :768]
        w_in_ref[rows, FF : FF + 768] = piece[:, 768:1536]
        w_down_ref[rows, :768] = piece[:, 1536:]
    for start, piece in pieces_of(me, near_2, far_2):
        rows = pl.ds(start, PIECE)
        w_in_ref[rows, 768:FF] = piece[:, :384]
        w_in_ref[rows, FF + 768 :] = piece[:, 384:768]
        w_out_ref[rows, :384] = piece[:, 768:1152]
        w_out_ref[rows, 384:] = piece[:, 1536:]
        w_down_ref[rows, 768:] = piece[:, 1152:1536]


def plus(first, second):
    return (first.astype(jnp.float32) + second.astype(jnp.float32)).astype(jnp.bfloat16)


def finish(body, me, pieces, shapes, scratch, name):
    return pl.pallas_call(
        body,
        out_shape=tuple(jax.ShapeDtypeStruct(shape, jnp.float32) for shape in shapes),
        in_specs=[SM] + [VM] * len(pieces),
        out_specs=(VM,) * len(shapes),
        scratch_shapes=[pltpu.VMEM(scratch, jnp.float32)] if scratch else [],
        compiler_params=pltpu.CompilerParams(vmem_limit_bytes=48 << 20),
        name=name,
    )(me, *pieces)


XZ = [dx | (dz << 1) for dx in range(2) for dz in range(4)]


def masks(*bits):
    order = [0]
    for bit in bits:
        choices = (0, bit) if bit != 6 else (0, 2, 4, 6)
        order = [m | choice for m in order for choice in choices]
    return order


def after(values, *others):
    return lax.optimization_barrier((values,) + others)[0]


def stage(*values):
    return lax.optimization_barrier(values)


def norm_parts(values):
    mean_val = jnp.mean(values, axis=-1, keepdims=True)
    centred = values - mean_val
    variance = jnp.mean(centred * centred, axis=-1, keepdims=True)
    scale = lax.rsqrt(variance + norm_eps)
    return centred * scale, scale


def norm_back(xhat, scale, grad, gain):
    e = grad * gain
    return scale * (
        e
        - jnp.mean(e, axis=-1, keepdims=True)
        - xhat * jnp.mean(e * xhat, axis=-1, keepdims=True)
    )


NT = (((1,), (1,)), ((), ()))
FAR_APART = -1.0e30
MEGA = 1 << 20


def matmul(first, second, dims=None):
    dims = dims or (((1,), (0,)), ((), ()))
    return lax.dot_general(first, second, dims, preferred_element_type=jnp.float32)


def kernel_call(body, outs, scratch, name, flops, moved):
    count = len(outs)
    return lambda *args: pl.pallas_call(
        body,
        out_shape=tuple(jax.ShapeDtypeStruct(shape, kind) for shape, kind in outs),
        in_specs=[SM] + [VM] * (len(args) - 1),
        out_specs=(VM,) * count,
        scratch_shapes=[pltpu.VMEM(shape, kind) for shape, kind in scratch],
        compiler_params=pltpu.CompilerParams(vmem_limit_bytes=56 * MEGA),
        cost_estimate=pl.CostEstimate(flops=flops, bytes_accessed=moved, transcendentals=0),
        name=name,
    )(*args)


def swap_halves(pair):
    lane = lax.broadcasted_iota(jnp.int32, pair.shape, 1) % HD
    return jnp.where(lane < HD // 2, pltpu.roll(pair, 96, 1), pltpu.roll(pair, 32, 1))


def place_rows(me, pieces, whole_ref):
    for mask, piece in pieces:
        start = pl.multiple_of((me // 8 ^ mask) * 192, 16)
        whole_ref[pl.ds(start, 192), :] = piece


def attention_kernel(
    me_ref,
    own_ref,
    across_ref,
    peer_ref,
    pack_ref,
    up_ref,
    core_ref,
    cos_ref,
    sin_ref,
    normed_ref,
    q_ref,
    k_ref,
    v_ref,
    probs_ref,
    att_own_ref,
    att_peer_ref,
    att_ref,
    inv_ref,
    weight_ref,
    gains_ref,
    q_id_ref,
    keys_ref,
    values_ref,
):
    f32, bf16 = jnp.float32, jnp.bfloat16
    me = me_ref[0]
    shards = (pack_ref.at[0], core_ref.at[0], up_ref.at[0], core_ref.at[1])
    place_rows(me, [(mask, ref[:192, :]) for mask, ref in enumerate(shards)], weight_ref)
    gains = sum(ref[192:200, :].astype(f32) for ref in shards)[:, :D]
    gains_ref[...] = gains
    gain = gains[0:1, :]
    row_id = lax.broadcasted_iota(jnp.int32, (128, 128), 0).astype(f32)
    blocks = [own_ref.at[i] for i in range(2)] + [peer_ref.at[0, i] for i in range(2)]
    blocks += [across_ref.at[i] for i in range(2)] + [peer_ref.at[1, i] for i in range(2)]
    for i, block in enumerate(blocks):
        rows = slice(128 * i, 128 * (i + 1))
        hidden = block[:128, :].astype(f32)
        centred = hidden - jnp.mean(hidden, axis=1, keepdims=True)
        variance = jnp.mean(centred * centred, axis=1, keepdims=True)
        normed = (centred * lax.rsqrt(variance + norm_eps) * gain).astype(bf16)
        normed_ref[rows, :] = normed
        ids = block[128:136, :128].astype(f32)[0:1, :]
        hit = jnp.where(row_id == ids, 1.0, 0.0).T
        keys_ref[rows, 128:] = (1.0 - hit).astype(bf16)
        values_ref[rows, 128:] = jnp.ones((128, 128), bf16)
        if i < 4:
            q_id_ref[rows, :] = (hit * FAR_APART).astype(bf16)

    for i in range(4):
        rows = slice(256 * i, 256 * (i + 1))
        normed = normed_ref[rows, :]
        first = 0 if i < 2 else HALF
        qkv = matmul(normed, weight_ref[:, first:])
        for j in range(first // 128, 9):
            part = qkv[:, 128 * j - first : 128 * j - first + 128]
            columns = slice(128 * (j % 3), 128 * (j % 3) + 128)
            if j < 6:
                part = part * cos_ref[rows, :] + swap_halves(part) * sin_ref[rows, :]
            if j < 3:
                q_ref[rows, columns] = (part * HD**-0.5).astype(bf16)
            elif j < 6:
                k_ref[rows, columns] = part.astype(bf16)
            else:
                v_ref[rows, columns] = part.astype(bf16)

    low_head = lax.broadcasted_iota(jnp.int32, (256, 128), 1) < HD
    for pair in range(3):
        columns = slice(128 * pair, 128 * pair + 128)
        keys_ref[:, :128] = k_ref[:, columns]
        values_ref[:, :128] = v_ref[:, columns]
        for i in range(2):
            rows = slice(256 * i, 256 * (i + 1))
            queries = q_ref[rows, columns]
            found = []
            for head in range(2):
                picked = jnp.where(low_head == (head == 0), queries, jnp.zeros_like(queries))
                scores = matmul(
                    jnp.concatenate([picked, q_id_ref[rows, :]], 1), keys_ref[...], NT
                )
                probs = jnp.exp(scores).astype(bf16)
                probs_ref[2 * pair + head, rows, :] = probs
                found.append(matmul(probs, values_ref[...]))
            inverse = 1.0 / jnp.where(low_head, found[0][:, 128:], found[1][:, 128:])
            attended = jnp.where(low_head, found[0][:, :128], found[1][:, :128]) * inverse
            inv_ref[rows, columns] = inverse
            att_ref[rows, columns] = attended
            out_ref = att_own_ref if i == 0 else att_peer_ref
            out_ref[:, columns] = attended.astype(bf16)


def attention_forward(*args):
    f32, bf16 = jnp.float32, jnp.bfloat16
    outs = [
        ((1024, D), bf16),
        ((512, HALF), bf16),
        ((1024, HALF), bf16),
        ((1024, HALF), bf16),
        ((6, 512, 1024), bf16),
        ((256, HALF), bf16),
        ((256, HALF), bf16),
        ((512, HALF), f32),
        ((512, HALF), f32),
        ((D, 3 * HALF), bf16),
        ((8, D), f32),
    ]
    scratch = [((512, 128), bf16), ((1024, 256), bf16), ((1024, 256), bf16)]
    return kernel_call(attention_kernel, outs, scratch, "attention_fwd", 4 * 10**9, 8 * MEGA)(*args)


def put_pieces(me, order, values_ref, out_ref, columns):
    for slot, mask in enumerate(order):
        start = pl.multiple_of((me ^ mask) * PIECE, 8)
        out_ref[slot, :, columns] = values_ref[pl.ds(start, PIECE), :].astype(out_ref.dtype)


def gated_block(normed, grad, gate_rows, upper_rows, down_rows):
    bf16 = jnp.bfloat16
    gate = matmul(normed, gate_rows)
    upper = matmul(normed, upper_rows)
    chance = 0.5 + 0.5 * lax.erf(gate * math.sqrt(0.5))
    bell = jnp.exp(-0.5 * gate * gate) * (1.0 / math.sqrt(2.0 * math.pi))
    gelu = gate * chance
    g_activ = matmul(grad, down_rows)
    g_gate = (g_activ * upper * (chance + gate * bell)).astype(bf16)
    g_upper = (g_activ * gelu).astype(bf16)
    return (gelu * upper).astype(bf16), g_gate, g_upper


WIDTH = 384


def mlp_first_kernel(
    me_ref,
    own_ref,
    att_ref,
    att_peer_ref,
    grad_ref,
    gains_ref,
    shard_ref,
    core_ref,
    up_ref,
    both_ref,
    down_ref,
    g_normed_ref,
    xhat_ref,
    scale_ref,
    w_out_ref,
    away_ref,
    stay_ref,
    w_ref,
    buffer_ref,
):
    f32, bf16 = jnp.float32, jnp.bfloat16
    me = me_ref[0]
    core = (me // 8) % 2
    shards = (shard_ref, core_ref, up_ref, both_ref)
    for mask, ref in enumerate(shards):
        shard = me // 8 ^ mask
        head_row = (shard // 2 ^ core) * HALF + (shard % 2) * 192
        w_out_ref[pl.ds(pl.multiple_of(head_row, 16), 192), :] = ref[:, :D]
    place_rows(me, [(mask, ref[:, D:]) for mask, ref in enumerate(shards)], w_ref)

    attended = jnp.concatenate([att_ref[...], att_peer_ref[...]], 1)
    hidden = jnp.concatenate([own_ref[0, :128, :], own_ref[1, :128, :]]).astype(f32)
    mixed = hidden + matmul(attended, w_out_ref[...])
    centred = mixed - jnp.mean(mixed, axis=1, keepdims=True)
    scale = lax.rsqrt(jnp.mean(centred * centred, axis=1, keepdims=True) + norm_eps)
    xhat = centred * scale
    xhat_ref[...] = xhat
    scale_ref[...] = jnp.broadcast_to(scale, (256, 128))
    normed = (xhat * gains_ref[1:2, :]).astype(bf16)
    grad = grad_ref[...]
    normed_t, grad_t = normed.T, grad.T
    y_first, x_first = masks(16, 1, 6), masks(1, 16, 6)

    def emit(values, order, first):
        buffer_ref[...] = values
        columns = slice(first, first + WIDTH)
        put_pieces(me, [m | 8 for m in order], buffer_ref, away_ref, columns)
        put_pieces(me, order, buffer_ref, stay_ref, columns)

    down = jnp.zeros_like(mixed)
    g_normed = jnp.zeros_like(mixed)
    for i in range(2):
        low, high, last = (slice(first + WIDTH * i, first + WIDTH * (i + 1)) for first in (0, 768, 1536))
        activ, g_gate, g_upper = gated_block(normed, grad, w_ref[:, low], w_ref[:, high], w_ref[:, last])
        down = down + matmul(activ, w_ref[:, last], NT)
        g_normed = g_normed + matmul(g_gate, w_ref[:, low], NT)
        g_normed = g_normed + matmul(g_upper, w_ref[:, high], NT)
        emit(matmul(normed_t, g_gate), y_first, WIDTH * i)
        emit(matmul(normed_t, g_upper), y_first if i == 0 else x_first, 768 + WIDTH * i)
        emit(matmul(grad_t, activ), x_first, 1536 + WIDTH * i)
    down_ref[...] = mixed + down
    g_normed_ref[...] = g_normed


def mlp_first(*args):
    f32, bf16 = jnp.float32, jnp.bfloat16
    outs = [
        ((256, D), f32),
        ((256, D), f32),
        ((256, D), f32),
        ((256, 128), f32),
        ((D, D), bf16),
        ((16, PIECE, 6 * WIDTH), bf16),
        ((16, PIECE, 6 * WIDTH), bf16),
    ]
    scratch = [((D, 6 * WIDTH), bf16), ((D, WIDTH), f32)]
    return kernel_call(mlp_first_kernel, outs, scratch, "mlp_first", 3 * 10**9, 16 * MEGA)(*args)


def mlp_second_kernel(
    me_ref,
    att_ref,
    att_peer_ref,
    grad_ref,
    gains_ref,
    shard_ref,
    core_ref,
    up_ref,
    both_ref,
    down_ref,
    g_normed_ref,
    xhat_ref,
    scale_ref,
    w_out_ref,
    out_ref,
    g_mixed_ref,
    g_att_ref,
    g_att_peer_ref,
    away_ref,
    stay_ref,
    g_gain_ref,
    w_ref,
    buffer_ref,
):
    f32, bf16 = jnp.float32, jnp.bfloat16
    me = me_ref[0]
    core = (me // 8) % 2
    shards = (shard_ref, core_ref, up_ref, both_ref)
    place_rows(me, [(mask, ref[...]) for mask, ref in enumerate(shards)], w_ref)
    gain = gains_ref[1:2, :]
    xhat = xhat_ref[...]
    scale = scale_ref[:, 0:1]
    normed = (xhat * gain).astype(bf16)
    grad = grad_ref[...]
    normed_t, grad_t = normed.T, grad.T
    y_first, x_first = masks(16, 1, 6), masks(1, 16, 6)

    def emit(order, first):
        columns = slice(first, first + WIDTH)
        put_pieces(me, [m | 8 for m in order], buffer_ref, away_ref, columns)
        put_pieces(me, order, buffer_ref, stay_ref, columns)

    low, high, last = (slice(first, first + WIDTH) for first in (0, 384, 768))
    activ, g_gate, g_upper = gated_block(normed, grad, w_ref[:, low], w_ref[:, high], w_ref[:, last])
    g_normed = g_normed_ref[...] + matmul(g_gate, w_ref[:, low], NT)
    g_normed = g_normed + matmul(g_upper, w_ref[:, high], NT)
    e = g_normed * gain
    g_mixed = grad.astype(f32) + scale * (
        e
        - jnp.mean(e, axis=1, keepdims=True)
        - xhat * jnp.mean(e * xhat, axis=1, keepdims=True)
    )
    g_mixed_ref[...] = g_mixed
    g_low = g_mixed.astype(bf16)
    g_att = matmul(g_low, w_out_ref[...], NT).astype(bf16)
    g_att_ref[...] = g_att[:, :HALF]
    g_att_peer_ref[...] = g_att[:, HALF:]
    out_ref[...] = (down_ref[...] + matmul(activ, w_ref[:, last], NT)).astype(bf16)
    g_gain = jnp.broadcast_to(jnp.sum(xhat * g_normed, axis=0, keepdims=True), (128, D))
    row = lax.broadcasted_iota(jnp.int32, (128, D), 0)
    g_gain_ref[...] = jnp.where(row == 1, g_gain, 0.0).T
    buffer_ref[...] = matmul(normed_t, g_gate)
    emit(y_first, 0)
    buffer_ref[...] = matmul(normed_t, g_upper)
    emit(y_first, WIDTH)
    buffer_ref[...] = matmul(grad_t, activ)
    emit(x_first, 3 * WIDTH)
    attended_t = jnp.concatenate([att_ref[...], att_peer_ref[...]], 1).T
    for i in range(2):
        rows_out = matmul(attended_t, g_low[:, WIDTH * i : WIDTH * (i + 1)])
        for half in range(2):
            start = pl.multiple_of((half ^ core) * HALF, HALF)
            buffer_ref[pl.ds(start, HALF), :] = rows_out[HALF * half : HALF * (half + 1), :]
        emit(y_first if i == 0 else x_first, (2 + 2 * i) * WIDTH)


def mlp_second(*args):
    f32, bf16 = jnp.float32, jnp.bfloat16
    outs = [
        ((256, D), bf16),
        ((256, D), f32),
        ((256, HALF), bf16),
        ((256, HALF), bf16),
        ((16, PIECE, 5 * WIDTH), bf16),
        ((16, PIECE, 5 * WIDTH), bf16),
        ((D, 128), f32),
    ]
    scratch = [((D, 3 * WIDTH), bf16), ((D, WIDTH), f32)]
    return kernel_call(mlp_second_kernel, outs, scratch, "mlp_second", 2 * 10**9, 10 * MEGA)(*args)


def attention_back_kernel(
    me_ref,
    g_own_ref,
    g_peer_ref,
    att_ref,
    inv_ref,
    q_ref,
    k_ref,
    v_ref,
    probs_ref,
    cos_ref,
    sin_ref,
    dq_ref,
    dk_ref,
    dv_ref,
    values_ref,
):
    f32, bf16 = jnp.float32, jnp.bfloat16
    low_head = lax.broadcasted_iota(jnp.int32, (1024, 128), 1) < HD
    lane = lax.broadcasted_iota(jnp.int32, (512, 128), 1)
    values_ref[:, 128:] = jnp.ones((1024, 128), bf16)
    for pair in range(3):
        columns = slice(128 * pair, 128 * pair + 128)
        values_ref[:, :128] = v_ref[:, columns]
        queries_t, keys = q_ref[:, columns].T, k_ref[:, columns]
        grad = jnp.concatenate([g_own_ref[:, columns], g_peer_ref[:, columns]]).astype(f32)
        grad = grad * inv_ref[:, columns]
        terms = grad * att_ref[:, columns]
        grad = grad.astype(bf16)
        grad_t = grad.T
        g_queries = jnp.zeros((512, 128), f32)
        g_keys, g_values = [], []
        for head in range(2):
            mine = low_head == (head == 0)
            rows = slice(HD * head, HD * head + HD)
            row = jnp.sum(jnp.where(mine[:512], terms, 0.0), axis=1, keepdims=True)
            high = row.astype(bf16)
            middle = (row - high.astype(f32)).astype(bf16)
            rest = (row - high.astype(f32) - middle.astype(f32)).astype(bf16)
            extra = jnp.where(lane == 0, -high.astype(f32), 0.0)
            extra = jnp.where(lane == 1, -middle.astype(f32), extra)
            extra = jnp.where(lane == 2, -rest.astype(f32), extra).astype(bf16)
            picked = jnp.where(mine[:512], grad, jnp.zeros_like(grad))
            product = matmul(jnp.concatenate([picked, extra], 1), values_ref[...], NT)
            probs = probs_ref[2 * pair + head]
            g_scores = (probs.astype(f32) * product).astype(bf16)
            g_queries = g_queries + matmul(g_scores, jnp.where(mine, keys, jnp.zeros_like(keys)))
            g_keys.append(matmul(queries_t[rows, :], g_scores))
            g_values.append(matmul(grad_t[rows, :], probs))
        g_queries = g_queries * HD**-0.5
        near = slice(0, 512)
        dq_ref[:, columns] = (
            g_queries * cos_ref[near, :] - swap_halves(g_queries) * sin_ref[near, :]
        ).astype(bf16)
        g_keys = jnp.concatenate(g_keys).T
        dk_ref[:, columns] = (
            g_keys * cos_ref[...] - swap_halves(g_keys) * sin_ref[...]
        ).astype(bf16)
        dv_ref[:, columns] = jnp.concatenate(g_values).T.astype(bf16)


def attention_backward(*args):
    bf16 = jnp.bfloat16
    outs = [((512, HALF), bf16), ((1024, HALF), bf16), ((1024, HALF), bf16)]
    scratch = [((1024, 256), bf16)]
    return kernel_call(
        attention_back_kernel, outs, scratch, "attention_bwd", 5 * 10**9, 10 * MEGA
    )(*args)


def qkv_weight_kernel(
    me_ref,
    normed_ref,
    weight_ref,
    g_gain_ref,
    dq_ref,
    dk_ref,
    dv_ref,
    keep_a,
    away_a,
    peer_b,
    buffer_ref,
):
    me = me_ref[0]
    order_a, order_b = masks(1, 6), masks(1, 16, 6)
    normed_t = normed_ref[...].T

    def emit(values_ref, columns):
        put_pieces(me, order_a, values_ref, keep_a, columns)
        put_pieces(me, [m | 16 for m in order_a], values_ref, away_a, columns)
        put_pieces(me, [m | 8 for m in order_b], values_ref, peer_b, columns)

    g_gain = jnp.zeros((D, 1), jnp.float32)
    for i, ref in enumerate((dq_ref, dk_ref, dv_ref)):
        columns = slice(HALF * i, HALF * (i + 1))
        values = matmul(normed_t[:, : ref.shape[0]], ref[...])
        weight = weight_ref[:, columns].astype(jnp.float32)
        g_gain = g_gain + jnp.sum(values * weight, axis=1, keepdims=True)
        buffer_ref[...] = values
        emit(buffer_ref, columns)
    lane = lax.broadcasted_iota(jnp.int32, (D, 128), 1)
    buffer_ref[:, :128] = jnp.where(lane == 0, g_gain, g_gain_ref[...])
    emit(buffer_ref.at[:, :128], slice(3 * HALF, 3 * HALF + 128))


def qkv_weight_gradient(*args):
    outs = [((count, PIECE, 3 * HALF + 128), jnp.bfloat16) for count in (8, 8, 16)]
    scratch = [((D, HALF), jnp.float32)]
    return kernel_call(qkv_weight_kernel, outs, scratch, "qkv_weights", 2 * 10**9, 8 * MEGA)(*args)


def qkv_input_kernel(me_ref, weight_ref, dq_ref, dk_ref, dv_ref, own_ref, across_ref, peer_ref):
    targets = (own_ref, peer_ref.at[0], across_ref, peer_ref.at[1])
    for i, target in enumerate(targets):
        rows = slice(256 * i, 256 * (i + 1))
        grad = matmul(dk_ref[rows, :], weight_ref[:, HALF : 2 * HALF], NT)
        grad = grad + matmul(dv_ref[rows, :], weight_ref[:, 2 * HALF :], NT)
        if i < 2:
            grad = grad + matmul(dq_ref[rows, :], weight_ref[:, :HALF], NT)
        target[...] = grad.astype(target.dtype)


def qkv_input_gradient(*args):
    bf16 = jnp.bfloat16
    outs = [((256, D), bf16), ((256, D), bf16), ((2, 256, D), bf16)]
    return kernel_call(qkv_input_kernel, outs, [], "qkv_inputs", 2 * 10**9, 6 * MEGA)(*args)


def paired_chips(hidden_in, grad_out, segment_ids, w_qkv, w_out, w_in, w_down, gain_attn, gain_mlp):
    bf16, f32 = jnp.bfloat16, jnp.float32
    dp, ctx = lax.axis_index("dp"), lax.axis_index("ctx")
    me = dp * 8 + ctx
    me_ref = me.reshape(1).astype(jnp.int32)
    c, zl, x = dp % 2, (ctx // 2) % 2, ctx % 2
    rows = hidden_in.shape[1]

    def to_chips(values):
        return (
            send_swapped(pick(zl, values[0], values[1]), 0),
            send_swapped(pick(zl, values[1], values[0]), 2),
        )

    def from_chips(values):
        block_a, block_b = send_swapped(values[:rows], 0), send_swapped(values[rows:], 2)
        return jnp.stack([pick(zl, block_a, block_b), pick(zl, block_b, block_a)])

    ids = jnp.pad(segment_ids[:, None, :], ((0, 0), (0, 7), (0, D - rows))).astype(bf16)
    packed = [pick(zl, a, b) for a, b in ((hidden_in, hidden_in[::-1]), (ids, ids[::-1]))]
    packed = jnp.concatenate(packed, 1)

    gains = lax.dynamic_update_slice(
        jnp.zeros((8, 3 * HALF), f32), jnp.stack([gain_attn, gain_mlp]), (0, 192 * dp)
    )

    def my_columns(core):
        columns = [lax.dynamic_slice_in_dim(w_qkv, t * D + core * HALF, HALF, 1) for t in range(3)]
        return jnp.concatenate([jnp.concatenate(columns, 1), gains]).astype(bf16)

    within = jnp.arange(rows, dtype=jnp.int32)
    starts = []
    for far in range(2):
        for core in range(2):
            for low in range(2):
                starts.append((2 * (2 * (c ^ core) + (zl ^ low)) + (x ^ far)) * rows + within)
    cosine, sine = rotary_tables(jnp.concatenate(starts), HD)
    sine = sine * jnp.where(jnp.arange(HD) < HD // 2, -1.0, 1.0)
    cosine, sine = jnp.concatenate([cosine] * 2, 1), jnp.concatenate([sine] * 2, 1)

    pack = jnp.stack([my_columns(c), my_columns(1 - c)])
    pack, packed = stage(pack, packed)
    own = jnp.stack([send_swapped(packed[0], 0), send_swapped(packed[1], 2)])
    up = send(pack, 16)
    w_down = w_down.T
    cut, rest = slice(0, 768), slice(768, FF)
    late = slice(FF + 768, None)
    first = jnp.concatenate([w_out, w_in[:, cut], w_in[:, FF : FF + 768], w_down[:, cut]], 1)
    second = jnp.concatenate([w_in[:, rest], w_in[:, late], w_down[:, rest]], 1)
    own, first, second = stage(own, first.astype(bf16), second.astype(bf16))
    up_first, up_second = send(first, 16), send(second, 16)
    across = send(own, 1)
    across, up, cosine, sine = stage(across, up, cosine, sine)
    by_core = send(jnp.stack([pack[1], up[1]]), 8)
    peer = send(jnp.stack([own, across]), 8)
    grad_low = to_chips(after(grad_out, across))

    normed, queries, keys, values, probs, att_own, att_peer, att, inverse, weight, gains = (
        attention_forward(
            me_ref, own, across, peer, pack, up, by_core, cosine, sine
        )
    )
    grad_a, grad_b, att_peer, first = stage(*grad_low, att_peer, first)
    grad_low = jnp.concatenate([grad_a, grad_b])
    att_peer = send(att_peer, 8)
    core_first = send(first, 8)
    core_second = send(after(second, grad_low), 8)
    up_first, att_peer = stage(up_first, att_peer)
    both_first = send(up_first, 8)
    down, g_norm, xhat, scale, w_out, away_1, stay_1 = mlp_first(
        me_ref, own, att_own, att_peer, grad_low, gains, first, core_first, up_first, both_first
    )
    away_1, up_second, core_second = stage(away_1, up_second, core_second)
    both_second = send(up_second, 8)

    def halves(values, got):
        count = values.shape[0] // 2
        return [
            plus(values[part, :, columns], got[part, :, columns])
            for columns in (slice(0, 3 * WIDTH), slice(3 * WIDTH, None))
            for part in (slice(0, count), slice(count, None))
        ]

    def fold(stay, got):
        return plus(stay[:4], got[:4]), plus(stay[4:], got[4:])

    def fold_near(part):
        return jnp.stack([part[0], part[2]]), jnp.stack([part[1], part[3]])

    def joined(stay_a, got_a, stay_b, got_b):
        return fold_near(jnp.concatenate([plus(stay_a, got_a), plus(stay_b, got_b)], 2))

    got_1 = send(away_1, 8)
    both_second, down = stage(both_second, down)
    layer_out, g_mixed, g_att, g_att_peer, away_2, stay_2, g_gain = mlp_second(
        me_ref,
        *(att_own, att_peer, grad_low, gains),
        *(second, core_second, up_second, both_second),
        *(down, g_norm, xhat, scale, w_out),
    )
    got_1, away_2, g_att_peer, layer_out = stage(got_1, away_2, g_att_peer, layer_out)
    g_att_peer = send(g_att_peer, 8)
    got_2 = send(away_2, 8)
    stay_1a, leave_a, stay_1b, leave_b = halves(stay_1, got_1)
    got_1a, got_1b = send(leave_a, 16), send(leave_b, 1)
    g_att_peer, layer_out = stage(g_att_peer, layer_out)
    layer_out = from_chips(layer_out)
    grads = attention_backward(
        me_ref, g_att, g_att_peer, att, inverse, queries, keys, values, probs, cosine, sine
    )
    got_1a, got_1b, got_2, layer_out, *grads = stage(got_1a, got_1b, got_2, layer_out, *grads)

    stay_1a, leave_1a = fold(stay_1a, got_1a)
    stay_1b, leave_1b = fold(stay_1b, got_1b)
    got_1a, got_1b = send(leave_1a, 1), send(leave_1b, 16)
    stay_2a, leave_a, stay_2b, leave_b = halves(stay_2, got_2)
    got_2a, got_2b = send(leave_a, 16), send(leave_b, 1)
    g_gain, *_ = stage(g_gain, leave_1a, leave_1b, leave_a, leave_b)
    keep_a, away_a, peer_b = qkv_weight_gradient(me_ref, normed, weight, g_gain, *grads)

    got_1a, got_1b, away_a, peer_b, *grads = stage(got_1a, got_1b, away_a, peer_b, *grads)
    got_core, got_a = send(peer_b, 8), send(away_a, 16)
    keep_1, leave_1 = joined(stay_1a, got_1a, stay_1b, got_1b)
    got_1 = send(leave_1, 2)
    weight, _ = stage(weight, leave_1)
    near, across, peer = qkv_input_gradient(me_ref, weight, *grads)

    got_core, near, across, peer = stage(got_core, near, across, peer)
    keep_b, away_b = got_core[:8], got_core[8:]
    got_b = send(away_b, 1)
    peer = send(peer, 8)
    got_2a, got_2b, got_1, _ = stage(got_2a, got_2b, got_1, away_b)
    stay_2a, leave_2a = fold(stay_2a, got_2a)
    stay_2b, leave_2b = fold(stay_2b, got_2b)
    got_2a, got_2b = send(leave_2a, 1), send(leave_2b, 16)
    keep_1 = plus(keep_1, got_1)
    peer, keep_1, *_ = stage(peer, keep_1, leave_2a, leave_2b)
    got_1 = send(keep_1[1], 4)
    across = plus(across, peer[1])
    got_a, got_b, across, _ = stage(got_a, got_b, across, keep_1)

    stay_a, leave_a = fold(keep_a, got_a)
    stay_b, leave_b = fold(keep_b, got_b)
    got_a, got_b = send(leave_a, 1), send(leave_b, 16)
    got_1, got_2a, got_2b, across, *_ = stage(got_1, got_2a, got_2b, across, leave_a, leave_b)
    sum_1 = plus(keep_1[0], got_1)
    far_1 = send(sum_1, 4)
    keep_2, leave_2 = joined(stay_2a, got_2a, stay_2b, got_2b)
    got_2 = send(leave_2, 2)
    got_across = send(across, 1)
    got_a, got_b, *_ = stage(got_a, got_b, sum_1, leave_2, across)

    total = jnp.concatenate([plus(stay_a, got_a), plus(stay_b, got_b)], 2)
    got = [send(total[dz], 2 * dz) for dz in range(1, 4)]
    far_1, got_2, got_across, _ = stage(far_1, got_2, got_across, total)
    sum_1 = jnp.stack([sum_1, far_1])
    far_1 = send(sum_1, 2)
    keep_2 = plus(keep_2, got_2)
    got_2 = send(keep_2[1], 4)
    g_normed = plus(near, peer[0]).astype(f32) + got_across.astype(f32)
    xhat, scale = norm_parts(own[:, :rows].reshape(2 * rows, D).astype(f32))
    grad_in = (g_mixed + norm_back(xhat, scale, g_normed, gains[0])).astype(bf16)
    grad_in, _, _, *got = stage(grad_in, sum_1, keep_2, *got)

    total = sum((part.astype(f32) for part in got), total[0].astype(f32)).astype(bf16)
    got = [send(total, 2 * dz) for dz in range(1, 4)]
    far_1, got_2, _ = stage(far_1, got_2, total)
    sum_1 = jnp.stack([sum_1, far_1], 1).reshape(4, PIECE, -1)
    far_1 = send(sum_1, 1)
    sum_2 = plus(keep_2[0], got_2)
    far_2 = send(sum_2, 4)
    far_2, total, *got = stage(far_2, total, *got)
    total = jnp.stack([total, *got])
    far = send(total, 1)
    sum_2 = jnp.stack([sum_2, far_2])
    far_2 = send(sum_2, 2)
    grad_in, far_1, _ = stage(grad_in, far_1, total)
    grad_in = from_chips(grad_in)
    far_2, total = stage(far_2, total)
    sum_2 = jnp.stack([sum_2, far_2], 1).reshape(4, PIECE, -1)
    far_2 = send(sum_2, 1)
    g_w_qkv, g_gains = finish(
        qkv_result_kernel, me_ref, (total, far), ((192, 3 * D), (8, 192)), (256, 128), "qkv_result"
    )
    g_w_in, g_w_out, g_w_down = finish(
        mlp_result_kernel,
        me_ref,
        (sum_1, far_1, sum_2, far_2),
        ((192, 2 * FF), (192, D), (192, FF)),
        None,
        "mlp_result",
    )
    g_gain_attn = g_gains[0] / gain_attn.astype(bf16).astype(f32)
    return (layer_out, grad_in, g_w_qkv, g_w_out, g_w_in, g_w_down.T, g_gain_attn, g_gains[1])


def solution(mesh):
    whole_fit = mesh.shape["dp"] == 4 and mesh.shape["ctx"] == 8
    return jax.shard_map(
        paired_chips if whole_fit else on_device,
        mesh=mesh,
        in_specs=(
            P("dp", "ctx", None),
            P("dp", "ctx", None),
            P("dp", "ctx"),
            P("dp", None),
            P("dp", None),
            P("dp", None),
            P(None, "dp"),
            P("dp"),
            P("dp"),
        ),
        out_specs=(
            P("dp", "ctx", None),
            P("dp", "ctx", None),
            P("dp", None),
            P("dp", None),
            P("dp", None),
            P(None, "dp"),
            P("dp"),
            P("dp"),
        ),
        check_vma=False,
    )
```

```python
import math

import jax
import jax.numpy as jnp
from jax import lax
from jax.experimental import pallas as pl
from jax.experimental.pallas import tpu as pltpu
from jax.sharding import PartitionSpec as P

D = 768
HEADS = 12
HD = 64
FF = 1152


norm_eps = 1e-05
theta_base = 160000.0


def layer_norm(values, gain):
    mean_val = jnp.mean(values, axis=-1, keepdims=True)
    centred = values - mean_val
    variance = jnp.mean(centred * centred, axis=-1, keepdims=True)
    return centred * lax.rsqrt(variance + norm_eps) * gain


def rotary_tables(positions, head_size):
    half_size = head_size // 2
    exponents = jnp.arange(half_size, dtype=jnp.float32) * (2.0 / head_size)
    inv_freq = 1.0 / theta_base**exponents
    angles = positions.astype(jnp.float32)[:, None] * inv_freq[None, :]
    cosine = jnp.cos(angles)
    sine = jnp.sin(angles)
    return (jnp.concatenate([cosine, cosine], -1), jnp.concatenate([sine, sine], -1))


def rotate(values, cosine, sine):
    half_size = values.shape[-1] // 2
    turned = jnp.concatenate([-values[..., half_size:], values[..., :half_size]], -1)
    return values * cosine[:, None, :] + turned * sine[:, None, :]


def fold_blocks(carry, pieces, piece_segments, work, rows):
    count = piece_segments.shape[0]
    size = math.gcd(count, 4 * rows)
    number = count // size
    blocks = tuple((part.reshape((number, size) + part.shape[1:]) for part in pieces))
    blocks = blocks + (piece_segments.reshape(number, size),)

    def step(acc, block):
        acc = work(acc, block)
        return (acc, None)

    carry, _ = lax.scan(step, carry, blocks)
    return carry


def on_device(hidden_in, grad_out, segment_ids, w_qkv, w_out, w_in, w_down, gain_attn, gain_mlp):
    rows = hidden_in.shape[1]
    local_seqs = hidden_in.shape[0]
    score_scale = HD ** (-0.5)
    bf16 = jnp.bfloat16
    f32 = jnp.float32
    gathered = (
        lax.all_gather(w_qkv.astype(bf16), "dp", axis=0, tiled=True),
        lax.all_gather(w_out.astype(bf16), "dp", axis=0, tiled=True),
        lax.all_gather(w_in.astype(bf16), "dp", axis=0, tiled=True),
        lax.all_gather(w_down.astype(bf16), "dp", axis=1, tiled=True),
        lax.all_gather(gain_attn.astype(bf16), "dp", axis=0, tiled=True),
        lax.all_gather(gain_mlp.astype(bf16), "dp", axis=0, tiled=True),
    )
    weight_qkv, weight_out, weight_in, weight_down, gain_low_a, gain_low_b = gathered
    gain_first = gain_low_a.astype(f32)
    gain_second = gain_low_b.astype(f32)
    whole_segments = lax.all_gather(segment_ids, "ctx", axis=1, tiled=True)
    positions = lax.axis_index("ctx") * rows + jnp.arange(rows, dtype=jnp.int32)
    cosine, sine = rotary_tables(positions, HD)

    def gated(values_in):
        return jax.nn.gelu(values_in[:, :FF], approximate=False) * values_in[:, FF:]

    def turn(pair):
        return (rotate(pair[0], cosine, sine), rotate(pair[1], cosine, sine))

    def one_sequence(seq_index):
        hidden = hidden_in[seq_index].astype(f32)
        own_segments = segment_ids[seq_index]
        all_segments = whole_segments[seq_index]
        normed_first, first_back = jax.vjp(layer_norm, hidden, gain_first)
        normed_attn = normed_first.astype(bf16)
        qkv = jnp.dot(normed_attn, weight_qkv, preferred_element_type=f32)
        q_lin = qkv[:, :D].reshape(rows, HEADS, HD)
        k_lin = qkv[:, D : 2 * D].reshape(rows, HEADS, HD)
        v_lin = qkv[:, 2 * D :].reshape(rows, HEADS, HD)
        turned, turn_back = jax.vjp(turn, (q_lin, k_lin))
        queries = turned[0].astype(bf16)
        keys = turned[1].astype(bf16)
        values = v_lin.astype(bf16)

        def forward_work(acc, block):
            key_blk, value_blk, seg_blk = block
            total, summed = acc
            scores = (
                jnp.einsum("thd,shd->hts", queries, key_blk, preferred_element_type=f32)
                * score_scale
            )
            same = own_segments[:, None] == seg_blk[None, :]
            expo = jnp.where(same[None], jnp.exp(scores), 0.0)
            total = total + jnp.sum(expo, axis=-1)
            summed = summed + jnp.einsum(
                "hts,shd->thd", expo.astype(bf16), value_blk, preferred_element_type=f32
            )
            return (total, summed)

        start_fwd = (jnp.zeros((HEADS, rows), f32), jnp.zeros((rows, HEADS, HD), f32))
        key_piece = lax.all_gather(keys.reshape(rows, D), "ctx", axis=0, tiled=True)
        value_piece = lax.all_gather(values.reshape(rows, D), "ctx", axis=0, tiled=True)
        count = key_piece.shape[0]
        piece_segments = all_segments
        parts = (key_piece.reshape(count, HEADS, HD), value_piece.reshape(count, HEADS, HD))
        total, summed = fold_blocks(start_fwd, parts, piece_segments, forward_work, rows)
        total_rows = jnp.transpose(total)
        attended = (summed / total_rows[:, :, None]).reshape(rows, D).astype(bf16)
        mixed = hidden + jnp.dot(attended, weight_out, preferred_element_type=f32)
        normed_second, second_back = jax.vjp(layer_norm, mixed, gain_second)
        normed_mlp = normed_second.astype(bf16)
        gate_up = jnp.dot(normed_mlp, weight_in, preferred_element_type=f32)
        activ_f, gated_back = jax.vjp(gated, gate_up)
        activ = activ_f.astype(bf16)
        layer_out = (mixed + jnp.dot(activ, weight_down, preferred_element_type=f32)).astype(bf16)
        grad_low = grad_out[seq_index]
        g_w_down = jnp.einsum("tf,td->fd", activ, grad_low, preferred_element_type=f32)
        g_activ = jnp.einsum("td,fd->tf", grad_low, weight_down, preferred_element_type=f32)
        g_gate_up = gated_back(g_activ)[0].astype(bf16)
        g_w_in = jnp.einsum("ti,tj->ij", normed_mlp, g_gate_up, preferred_element_type=f32)
        g_normed_mlp = jnp.einsum("tj,ij->ti", g_gate_up, weight_in, preferred_element_type=f32)
        g_mixed_norm, g_gain_mlp = second_back(g_normed_mlp)
        g_mixed = grad_low.astype(f32) + g_mixed_norm
        g_mixed_low = g_mixed.astype(bf16)
        g_w_out = jnp.einsum("ti,tj->ij", attended, g_mixed_low, preferred_element_type=f32)
        g_att = jnp.einsum(
            "tj,ij->ti", g_mixed_low, weight_out, preferred_element_type=f32
        ).reshape(rows, HEADS, HD)
        g_summed = (g_att / total_rows[:, :, None]).astype(bf16)
        row_term = jnp.sum(g_att * summed, axis=-1) / (total_rows * total_rows)
        own_rows = jnp.transpose(row_term)
        all_rows = lax.all_gather(row_term, "ctx", axis=0, tiled=True)

        def query_work(acc, block):
            key_blk, value_blk, seg_blk = block
            scores = (
                jnp.einsum("thd,shd->hts", queries, key_blk, preferred_element_type=f32)
                * score_scale
            )
            same = own_segments[:, None] == seg_blk[None, :]
            expo = jnp.where(same[None], jnp.exp(scores), 0.0)
            product = jnp.einsum("thd,shd->hts", g_summed, value_blk, preferred_element_type=f32)
            g_scores = (expo * (product - own_rows[:, :, None])).astype(bf16)
            return acc + jnp.einsum("hts,shd->thd", g_scores, key_blk, preferred_element_type=f32)

        key_piece = lax.all_gather(keys.reshape(rows, D), "ctx", axis=0, tiled=True)
        value_piece = lax.all_gather(values.reshape(rows, D), "ctx", axis=0, tiled=True)
        count = key_piece.shape[0]
        piece_segments = all_segments
        parts = (key_piece.reshape(count, HEADS, HD), value_piece.reshape(count, HEADS, HD))
        g_queries = (
            fold_blocks(jnp.zeros((rows, HEADS, HD), f32), parts, piece_segments, query_work, rows)
            * score_scale
        )

        def key_work(acc, block):
            query_blk, gsum_blk, row_blk, seg_blk = block
            g_keys, g_values = acc
            scores = (
                jnp.einsum("shd,thd->hst", query_blk, keys, preferred_element_type=f32)
                * score_scale
            )
            same = seg_blk[:, None] == own_segments[None, :]
            expo = jnp.where(same[None], jnp.exp(scores), 0.0)
            g_values = g_values + jnp.einsum(
                "hst,shd->thd", expo.astype(bf16), gsum_blk, preferred_element_type=f32
            )
            product = jnp.einsum("shd,thd->hst", gsum_blk, values, preferred_element_type=f32)
            g_scores = (expo * (product - jnp.transpose(row_blk)[:, :, None])).astype(bf16)
            g_keys = g_keys + jnp.einsum(
                "hst,shd->thd", g_scores, query_blk, preferred_element_type=f32
            )
            return (g_keys, g_values)

        start_keys = (jnp.zeros((rows, HEADS, HD), f32), jnp.zeros((rows, HEADS, HD), f32))
        query_piece = lax.all_gather(queries.reshape(rows, D), "ctx", axis=0, tiled=True)
        gsum_piece = lax.all_gather(g_summed.reshape(rows, D), "ctx", axis=0, tiled=True)
        count = query_piece.shape[0]
        piece_segments = all_segments
        parts = (
            query_piece.reshape(count, HEADS, HD),
            gsum_piece.reshape(count, HEADS, HD),
            all_rows,
        )
        g_keys, g_values = fold_blocks(start_keys, parts, piece_segments, key_work, rows)
        g_keys = g_keys * score_scale
        unturned = turn_back((g_queries, g_keys))[0]
        g_qkv = jnp.concatenate(
            [unturned[0].reshape(rows, D), unturned[1].reshape(rows, D), g_values.reshape(rows, D)],
            -1,
        ).astype(bf16)
        g_w_qkv = jnp.einsum("ti,tj->ij", normed_attn, g_qkv, preferred_element_type=f32)
        g_normed_attn = jnp.einsum("tj,ij->ti", g_qkv, weight_qkv, preferred_element_type=f32)
        g_hidden_norm, g_gain_attn = first_back(g_normed_attn)
        grad_in = (g_mixed + g_hidden_norm).astype(bf16)
        terms = (g_w_qkv, g_w_out, g_w_in, g_w_down, g_gain_attn, g_gain_mlp)
        return (layer_out, grad_in, terms)

    outputs_fwd = []
    outputs_back = []
    terms = None
    for seq_index in range(local_seqs):
        layer_out, grad_in, seq_terms = one_sequence(seq_index)
        outputs_fwd.append(layer_out)
        outputs_back.append(grad_in)
        if terms is None:
            terms = seq_terms
        else:
            terms = tuple((old + new for old, new in zip(terms, seq_terms)))
    everywhere = lax.psum(terms, "ctx")
    owned = (
        lax.psum_scatter(
            everywhere[0].astype(jnp.bfloat16), "dp", scatter_dimension=0, tiled=True
        ).astype(jnp.float32),
        lax.psum_scatter(
            everywhere[1].astype(jnp.bfloat16), "dp", scatter_dimension=0, tiled=True
        ).astype(jnp.float32),
        lax.psum_scatter(
            everywhere[2].astype(jnp.bfloat16), "dp", scatter_dimension=0, tiled=True
        ).astype(jnp.float32),
        lax.psum_scatter(
            everywhere[3].astype(jnp.bfloat16), "dp", scatter_dimension=1, tiled=True
        ).astype(jnp.float32),
        lax.psum_scatter(
            everywhere[4].astype(jnp.bfloat16), "dp", scatter_dimension=0, tiled=True
        ).astype(jnp.float32),
        lax.psum_scatter(
            everywhere[5].astype(jnp.bfloat16), "dp", scatter_dimension=0, tiled=True
        ).astype(jnp.float32),
    )
    return (
        jnp.stack(outputs_fwd),
        jnp.stack(outputs_back),
        owned[0],
        owned[1],
        owned[2],
        owned[3],
        owned[4],
        owned[5],
    )


HALF = 384
PIECE = 24


def send(values, mask):
    return lax.ppermute(values, ("dp", "ctx"), [(i, i ^ mask) for i in range(32)])


def send_swapped(values, mask):
    def target(i):
        core, high = (i >> 3) & 1, (i >> 2) & 1
        return (i & ~12) | (high << 3) | (core << 2)

    return lax.ppermute(values, ("dp", "ctx"), [(i, target(i) ^ mask) for i in range(32)])


def pick(flag, first, second):
    return jnp.where(flag == 0, first, second)


VM = pl.BlockSpec(memory_space=pltpu.VMEM)
SM = pl.BlockSpec(memory_space=pltpu.SMEM)


def pieces_of(me, near_ref, far_ref):
    for slot, mask in enumerate(XZ):
        start = pl.multiple_of((me % 8 ^ mask) * PIECE, 8)
        yield start, (near_ref, far_ref)[slot // 4][slot % 4].astype(jnp.float32)


def qkv_result_kernel(me_ref, near_ref, far_ref, out_ref, gains_ref, buffer_ref):
    me = me_ref[0]
    core = (me // 8) % 2
    wide = 3 * HALF + 128
    for start, piece in pieces_of(me, near_ref, far_ref):
        rows = pl.ds(start, PIECE)
        for half in range(2):
            for t in range(3):
                column = pl.multiple_of(t * D + (half ^ core) * HALF, 128)
                first = half * wide + t * HALF
                out_ref[rows, pl.ds(column, HALF)] = piece[:, first : first + HALF]
        buffer_ref[rows, :] = piece[:, 3 * HALF : wide] + piece[:, wide + 3 * HALF :]
    gains_ref[...] = buffer_ref[...].T[:8, :192]


def mlp_result_kernel(
    me_ref, near_1, far_1, near_2, far_2, w_in_ref, w_out_ref, w_down_ref
):
    me = me_ref[0]
    for start, piece in pieces_of(me, near_1, far_1):
        rows = pl.ds(start, PIECE)
        w_in_ref[rows, :768] = piece[:, :768]
        w_in_ref[rows, FF : FF + 768] = piece[:, 768:1536]
        w_down_ref[rows, :768] = piece[:, 1536:]
    for start, piece in pieces_of(me, near_2, far_2):
        rows = pl.ds(start, PIECE)
        w_in_ref[rows, 768:FF] = piece[:, :384]
        w_in_ref[rows, FF + 768 :] = piece[:, 384:768]
        w_out_ref[rows, :384] = piece[:, 768:1152]
        w_out_ref[rows, 384:] = piece[:, 1536:]
        w_down_ref[rows, 768:] = piece[:, 1152:1536]


def plus(first, second):
    return (first.astype(jnp.float32) + second.astype(jnp.float32)).astype(jnp.bfloat16)


def finish(body, me, pieces, shapes, scratch, name):
    return pl.pallas_call(
        body,
        out_shape=tuple(jax.ShapeDtypeStruct(shape, jnp.float32) for shape in shapes),
        in_specs=[SM] + [VM] * len(pieces),
        out_specs=(VM,) * len(shapes),
        scratch_shapes=[pltpu.VMEM(scratch, jnp.float32)] if scratch else [],
        compiler_params=pltpu.CompilerParams(vmem_limit_bytes=24 << 20),
        name=name,
    )(me, *pieces)


XZ = [dx | (dz << 1) for dx in range(2) for dz in range(4)]


def masks(*bits):
    order = [0]
    for bit in bits:
        choices = (0, bit) if bit != 6 else (0, 2, 4, 6)
        order = [m | choice for m in order for choice in choices]
    return order


def after(values, *others):
    return lax.optimization_barrier((values,) + others)[0]


def stage(*values):
    return lax.optimization_barrier(values)


def norm_parts(values):
    mean_val = jnp.mean(values, axis=-1, keepdims=True)
    centred = values - mean_val
    variance = jnp.mean(centred * centred, axis=-1, keepdims=True)
    scale = lax.rsqrt(variance + norm_eps)
    return centred * scale, scale


def norm_back(xhat, scale, grad, gain):
    e = grad * gain
    return scale * (
        e
        - jnp.mean(e, axis=-1, keepdims=True)
        - xhat * jnp.mean(e * xhat, axis=-1, keepdims=True)
    )


NT = (((1,), (1,)), ((), ()))
FAR_APART = -1.0e30
MEGA = 1 << 20


def matmul(first, second, dims=None):
    dims = dims or (((1,), (0,)), ((), ()))
    return lax.dot_general(first, second, dims, preferred_element_type=jnp.float32)


def kernel_call(body, outs, scratch, name, flops, moved):
    count = len(outs)
    return lambda *args: pl.pallas_call(
        body,
        out_shape=tuple(jax.ShapeDtypeStruct(shape, kind) for shape, kind in outs),
        in_specs=[SM] + [VM] * (len(args) - 1),
        out_specs=(VM,) * count,
        scratch_shapes=[pltpu.VMEM(shape, kind) for shape, kind in scratch],
        compiler_params=pltpu.CompilerParams(vmem_limit_bytes=32 * MEGA),
        cost_estimate=pl.CostEstimate(flops=flops, bytes_accessed=moved, transcendentals=0),
        name=name,
    )(*args)


def swap_halves(pair):
    lane = lax.broadcasted_iota(jnp.int32, pair.shape, 1) % HD
    return jnp.where(lane < HD // 2, pltpu.roll(pair, 96, 1), pltpu.roll(pair, 32, 1))


def place_rows(me, pieces, whole_ref):
    for mask, piece in pieces:
        start = pl.multiple_of((me // 8 ^ mask) * 192, 16)
        whole_ref[pl.ds(start, 192), :] = piece


def attention_kernel(
    me_ref,
    own_ref,
    across_ref,
    peer_ref,
    pack_ref,
    up_ref,
    core_ref,
    cos_ref,
    sin_ref,
    normed_ref,
    q_ref,
    k_ref,
    v_ref,
    probs_ref,
    att_own_ref,
    att_peer_ref,
    att_ref,
    inv_ref,
    weight_ref,
    gains_ref,
    q_id_ref,
    keys_ref,
    values_ref,
):
    f32, bf16 = jnp.float32, jnp.bfloat16
    me = me_ref[0]
    shards = (pack_ref.at[0], core_ref.at[0], up_ref.at[0], core_ref.at[1])
    place_rows(me, [(mask, ref[:192, :]) for mask, ref in enumerate(shards)], weight_ref)
    gains = sum(ref[192:200, :].astype(f32) for ref in shards)[:, :D]
    gains_ref[...] = gains
    gain = gains[0:1, :]
    row_id = lax.broadcasted_iota(jnp.int32, (128, 128), 0).astype(f32)
    blocks = [own_ref.at[i] for i in range(2)] + [peer_ref.at[0, i] for i in range(2)]
    blocks += [across_ref.at[i] for i in range(2)] + [peer_ref.at[1, i] for i in range(2)]
    for i, block in enumerate(blocks):
        rows = slice(128 * i, 128 * (i + 1))
        hidden = block[:128, :].astype(f32)
        centred = hidden - jnp.mean(hidden, axis=1, keepdims=True)
        variance = jnp.mean(centred * centred, axis=1, keepdims=True)
        normed = (centred * lax.rsqrt(variance + norm_eps) * gain).astype(bf16)
        normed_ref[rows, :] = normed
        ids = block[128:136, :128].astype(f32)[0:1, :]
        hit = jnp.where(row_id == ids, 1.0, 0.0).T
        keys_ref[rows, 128:] = (1.0 - hit).astype(bf16)
        values_ref[rows, 128:] = jnp.ones((128, 128), bf16)
        if i < 4:
            q_id_ref[rows, :] = (hit * FAR_APART).astype(bf16)

    for i in range(4):
        rows = slice(256 * i, 256 * (i + 1))
        normed = normed_ref[rows, :]
        first = 0 if i < 2 else HALF
        qkv = matmul(normed, weight_ref[:, first:])
        for j in range(first // 128, 9):
            part = qkv[:, 128 * j - first : 128 * j - first + 128]
            columns = slice(128 * (j % 3), 128 * (j % 3) + 128)
            if j < 6:
                part = part * cos_ref[rows, :] + swap_halves(part) * sin_ref[rows, :]
            if j < 3:
                q_ref[rows, columns] = (part * HD**-0.5).astype(bf16)
            elif j < 6:
                k_ref[rows, columns] = part.astype(bf16)
            else:
                v_ref[rows, columns] = part.astype(bf16)

    low_head = lax.broadcasted_iota(jnp.int32, (256, 128), 1) < HD
    for pair in range(3):
        columns = slice(128 * pair, 128 * pair + 128)
        keys_ref[:, :128] = k_ref[:, columns]
        values_ref[:, :128] = v_ref[:, columns]
        for i in range(2):
            rows = slice(256 * i, 256 * (i + 1))
            queries = q_ref[rows, columns]
            found = []
            for head in range(2):
                picked = jnp.where(low_head == (head == 0), queries, jnp.zeros_like(queries))
                scores = matmul(
                    jnp.concatenate([picked, q_id_ref[rows, :]], 1), keys_ref[...], NT
                )
                probs = jnp.exp(scores).astype(bf16)
                probs_ref[2 * pair + head, rows, :] = probs
                found.append(matmul(probs, values_ref[...]))
            inverse = 1.0 / jnp.where(low_head, found[0][:, 128:], found[1][:, 128:])
            attended = jnp.where(low_head, found[0][:, :128], found[1][:, :128]) * inverse
            inv_ref[rows, columns] = inverse
            att_ref[rows, columns] = attended
            out_ref = att_own_ref if i == 0 else att_peer_ref
            out_ref[:, columns] = attended.astype(bf16)


def attention_forward(*args):
    f32, bf16 = jnp.float32, jnp.bfloat16
    outs = [
        ((1024, D), bf16),
        ((512, HALF), bf16),
        ((1024, HALF), bf16),
        ((1024, HALF), bf16),
        ((6, 512, 1024), bf16),
        ((256, HALF), bf16),
        ((256, HALF), bf16),
        ((512, HALF), f32),
        ((512, HALF), f32),
        ((D, 3 * HALF), bf16),
        ((8, D), f32),
    ]
    scratch = [((512, 128), bf16), ((1024, 256), bf16), ((1024, 256), bf16)]
    return kernel_call(attention_kernel, outs, scratch, "attention_fwd", 4 * 10**9, 8 * MEGA)(*args)


def put_pieces(me, order, values_ref, out_ref, columns):
    for slot, mask in enumerate(order):
        start = pl.multiple_of((me ^ mask) * PIECE, 8)
        out_ref[slot, :, columns] = values_ref[pl.ds(start, PIECE), :].astype(out_ref.dtype)


def gated_block(normed, grad, gate_rows, upper_rows, down_rows):
    bf16 = jnp.bfloat16
    gate = matmul(normed, gate_rows)
    upper = matmul(normed, upper_rows)
    chance = 0.5 + 0.5 * lax.erf(gate * math.sqrt(0.5))
    bell = jnp.exp(-0.5 * gate * gate) * (1.0 / math.sqrt(2.0 * math.pi))
    gelu = gate * chance
    g_activ = matmul(grad, down_rows)
    g_gate = (g_activ * upper * (chance + gate * bell)).astype(bf16)
    g_upper = (g_activ * gelu).astype(bf16)
    return (gelu * upper).astype(bf16), g_gate, g_upper


WIDTH = 384


def mlp_first_kernel(
    me_ref,
    own_ref,
    att_ref,
    att_peer_ref,
    grad_ref,
    gains_ref,
    shard_ref,
    core_ref,
    up_ref,
    both_ref,
    down_ref,
    g_normed_ref,
    xhat_ref,
    scale_ref,
    w_out_ref,
    away_ref,
    stay_ref,
    w_ref,
    buffer_ref,
):
    f32, bf16 = jnp.float32, jnp.bfloat16
    me = me_ref[0]
    core = (me // 8) % 2
    shards = (shard_ref, core_ref, up_ref, both_ref)
    for mask, ref in enumerate(shards):
        shard = me // 8 ^ mask
        head_row = (shard // 2 ^ core) * HALF + (shard % 2) * 192
        w_out_ref[pl.ds(pl.multiple_of(head_row, 16), 192), :] = ref[:, :D]
    place_rows(me, [(mask, ref[:, D:]) for mask, ref in enumerate(shards)], w_ref)

    attended = jnp.concatenate([att_ref[...], att_peer_ref[...]], 1)
    hidden = jnp.concatenate([own_ref[0, :128, :], own_ref[1, :128, :]]).astype(f32)
    mixed = hidden + matmul(attended, w_out_ref[...])
    centred = mixed - jnp.mean(mixed, axis=1, keepdims=True)
    scale = lax.rsqrt(jnp.mean(centred * centred, axis=1, keepdims=True) + norm_eps)
    xhat = centred * scale
    xhat_ref[...] = xhat
    scale_ref[...] = jnp.broadcast_to(scale, (256, 128))
    normed = (xhat * gains_ref[1:2, :]).astype(bf16)
    grad = grad_ref[...]
    normed_t, grad_t = normed.T, grad.T
    y_first, x_first = masks(16, 1, 6), masks(1, 16, 6)

    def emit(values, order, first):
        buffer_ref[...] = values
        columns = slice(first, first + WIDTH)
        put_pieces(me, [m | 8 for m in order], buffer_ref, away_ref, columns)
        put_pieces(me, order, buffer_ref, stay_ref, columns)

    down = jnp.zeros_like(mixed)
    g_normed = jnp.zeros_like(mixed)
    for i in range(2):
        low, high, last = (slice(first + WIDTH * i, first + WIDTH * (i + 1)) for first in (0, 768, 1536))
        activ, g_gate, g_upper = gated_block(normed, grad, w_ref[:, low], w_ref[:, high], w_ref[:, last])
        down = down + matmul(activ, w_ref[:, last], NT)
        g_normed = g_normed + matmul(g_gate, w_ref[:, low], NT)
        g_normed = g_normed + matmul(g_upper, w_ref[:, high], NT)
        emit(matmul(normed_t, g_gate), y_first, WIDTH * i)
        emit(matmul(normed_t, g_upper), y_first if i == 0 else x_first, 768 + WIDTH * i)
        emit(matmul(grad_t, activ), x_first, 1536 + WIDTH * i)
    down_ref[...] = mixed + down
    g_normed_ref[...] = g_normed


def mlp_first(*args):
    f32, bf16 = jnp.float32, jnp.bfloat16
    outs = [
        ((256, D), f32),
        ((256, D), f32),
        ((256, D), f32),
        ((256, 128), f32),
        ((D, D), bf16),
        ((16, PIECE, 6 * WIDTH), bf16),
        ((16, PIECE, 6 * WIDTH), bf16),
    ]
    scratch = [((D, 6 * WIDTH), bf16), ((D, WIDTH), f32)]
    return kernel_call(mlp_first_kernel, outs, scratch, "mlp_first", 3 * 10**9, 16 * MEGA)(*args)


def mlp_second_kernel(
    me_ref,
    att_ref,
    att_peer_ref,
    grad_ref,
    gains_ref,
    shard_ref,
    core_ref,
    up_ref,
    both_ref,
    down_ref,
    g_normed_ref,
    xhat_ref,
    scale_ref,
    w_out_ref,
    out_ref,
    g_mixed_ref,
    g_att_ref,
    g_att_peer_ref,
    away_ref,
    stay_ref,
    g_gain_ref,
    w_ref,
    buffer_ref,
):
    f32, bf16 = jnp.float32, jnp.bfloat16
    me = me_ref[0]
    core = (me // 8) % 2
    shards = (shard_ref, core_ref, up_ref, both_ref)
    place_rows(me, [(mask, ref[...]) for mask, ref in enumerate(shards)], w_ref)
    gain = gains_ref[1:2, :]
    xhat = xhat_ref[...]
    scale = scale_ref[:, 0:1]
    normed = (xhat * gain).astype(bf16)
    grad = grad_ref[...]
    normed_t, grad_t = normed.T, grad.T
    y_first, x_first = masks(16, 1, 6), masks(1, 16, 6)

    def emit(order, first):
        columns = slice(first, first + WIDTH)
        put_pieces(me, [m | 8 for m in order], buffer_ref, away_ref, columns)
        put_pieces(me, order, buffer_ref, stay_ref, columns)

    low, high, last = (slice(first, first + WIDTH) for first in (0, 384, 768))
    activ, g_gate, g_upper = gated_block(normed, grad, w_ref[:, low], w_ref[:, high], w_ref[:, last])
    g_normed = g_normed_ref[...] + matmul(g_gate, w_ref[:, low], NT)
    g_normed = g_normed + matmul(g_upper, w_ref[:, high], NT)
    e = g_normed * gain
    g_mixed = grad.astype(f32) + scale * (
        e
        - jnp.mean(e, axis=1, keepdims=True)
        - xhat * jnp.mean(e * xhat, axis=1, keepdims=True)
    )
    g_mixed_ref[...] = g_mixed
    g_low = g_mixed.astype(bf16)
    g_att = matmul(g_low, w_out_ref[...], NT).astype(bf16)
    g_att_ref[...] = g_att[:, :HALF]
    g_att_peer_ref[...] = g_att[:, HALF:]
    out_ref[...] = (down_ref[...] + matmul(activ, w_ref[:, last], NT)).astype(bf16)
    g_gain = jnp.broadcast_to(jnp.sum(xhat * g_normed, axis=0, keepdims=True), (128, D))
    row = lax.broadcasted_iota(jnp.int32, (128, D), 0)
    g_gain_ref[...] = jnp.where(row == 1, g_gain, 0.0).T
    buffer_ref[...] = matmul(normed_t, g_gate)
    emit(y_first, 0)
    buffer_ref[...] = matmul(normed_t, g_upper)
    emit(y_first, WIDTH)
    buffer_ref[...] = matmul(grad_t, activ)
    emit(x_first, 3 * WIDTH)
    attended_t = jnp.concatenate([att_ref[...], att_peer_ref[...]], 1).T
    for i in range(2):
        rows_out = matmul(attended_t, g_low[:, WIDTH * i : WIDTH * (i + 1)])
        for half in range(2):
            start = pl.multiple_of((half ^ core) * HALF, HALF)
            buffer_ref[pl.ds(start, HALF), :] = rows_out[HALF * half : HALF * (half + 1), :]
        emit(y_first if i == 0 else x_first, (2 + 2 * i) * WIDTH)


def mlp_second(*args):
    f32, bf16 = jnp.float32, jnp.bfloat16
    outs = [
        ((256, D), bf16),
        ((256, D), f32),
        ((256, HALF), bf16),
        ((256, HALF), bf16),
        ((16, PIECE, 5 * WIDTH), bf16),
        ((16, PIECE, 5 * WIDTH), bf16),
        ((D, 128), f32),
    ]
    scratch = [((D, 3 * WIDTH), bf16), ((D, WIDTH), f32)]
    return kernel_call(mlp_second_kernel, outs, scratch, "mlp_second", 2 * 10**9, 10 * MEGA)(*args)


def attention_back_kernel(
    me_ref,
    g_own_ref,
    g_peer_ref,
    att_ref,
    inv_ref,
    q_ref,
    k_ref,
    v_ref,
    probs_ref,
    cos_ref,
    sin_ref,
    dq_ref,
    dk_ref,
    dv_ref,
    values_ref,
):
    f32, bf16 = jnp.float32, jnp.bfloat16
    low_head = lax.broadcasted_iota(jnp.int32, (1024, 128), 1) < HD
    lane = lax.broadcasted_iota(jnp.int32, (512, 128), 1)
    values_ref[:, 128:] = jnp.ones((1024, 128), bf16)
    for pair in range(3):
        columns = slice(128 * pair, 128 * pair + 128)
        values_ref[:, :128] = v_ref[:, columns]
        queries_t, keys = q_ref[:, columns].T, k_ref[:, columns]
        grad = jnp.concatenate([g_own_ref[:, columns], g_peer_ref[:, columns]]).astype(f32)
        grad = grad * inv_ref[:, columns]
        terms = grad * att_ref[:, columns]
        grad = grad.astype(bf16)
        grad_t = grad.T
        g_queries = jnp.zeros((512, 128), f32)
        g_keys, g_values = [], []
        for head in range(2):
            mine = low_head == (head == 0)
            rows = slice(HD * head, HD * head + HD)
            row = jnp.sum(jnp.where(mine[:512], terms, 0.0), axis=1, keepdims=True)
            high = row.astype(bf16)
            middle = (row - high.astype(f32)).astype(bf16)
            rest = (row - high.astype(f32) - middle.astype(f32)).astype(bf16)
            extra = jnp.where(lane == 0, -high.astype(f32), 0.0)
            extra = jnp.where(lane == 1, -middle.astype(f32), extra)
            extra = jnp.where(lane == 2, -rest.astype(f32), extra).astype(bf16)
            picked = jnp.where(mine[:512], grad, jnp.zeros_like(grad))
            product = matmul(jnp.concatenate([picked, extra], 1), values_ref[...], NT)
            probs = probs_ref[2 * pair + head]
            g_scores = (probs.astype(f32) * product).astype(bf16)
            g_queries = g_queries + matmul(g_scores, jnp.where(mine, keys, jnp.zeros_like(keys)))
            g_keys.append(matmul(queries_t[rows, :], g_scores))
            g_values.append(matmul(grad_t[rows, :], probs))
        g_queries = g_queries * HD**-0.5
        near = slice(0, 512)
        dq_ref[:, columns] = (
            g_queries * cos_ref[near, :] - swap_halves(g_queries) * sin_ref[near, :]
        ).astype(bf16)
        g_keys = jnp.concatenate(g_keys).T
        dk_ref[:, columns] = (
            g_keys * cos_ref[...] - swap_halves(g_keys) * sin_ref[...]
        ).astype(bf16)
        dv_ref[:, columns] = jnp.concatenate(g_values).T.astype(bf16)


def attention_backward(*args):
    bf16 = jnp.bfloat16
    outs = [((512, HALF), bf16), ((1024, HALF), bf16), ((1024, HALF), bf16)]
    scratch = [((1024, 256), bf16)]
    return kernel_call(
        attention_back_kernel, outs, scratch, "attention_bwd", 5 * 10**9, 10 * MEGA
    )(*args)


def qkv_weight_kernel(
    me_ref,
    normed_ref,
    weight_ref,
    g_gain_ref,
    dq_ref,
    dk_ref,
    dv_ref,
    keep_a,
    away_a,
    peer_b,
    buffer_ref,
):
    me = me_ref[0]
    order_a, order_b = masks(1, 6), masks(1, 16, 6)
    normed_t = normed_ref[...].T

    def emit(values_ref, columns):
        put_pieces(me, order_a, values_ref, keep_a, columns)
        put_pieces(me, [m | 16 for m in order_a], values_ref, away_a, columns)
        put_pieces(me, [m | 8 for m in order_b], values_ref, peer_b, columns)

    g_gain = jnp.zeros((D, 1), jnp.float32)
    for i, ref in enumerate((dq_ref, dk_ref, dv_ref)):
        columns = slice(HALF * i, HALF * (i + 1))
        values = matmul(normed_t[:, : ref.shape[0]], ref[...])
        weight = weight_ref[:, columns].astype(jnp.float32)
        g_gain = g_gain + jnp.sum(values * weight, axis=1, keepdims=True)
        buffer_ref[...] = values
        emit(buffer_ref, columns)
    lane = lax.broadcasted_iota(jnp.int32, (D, 128), 1)
    buffer_ref[:, :128] = jnp.where(lane == 0, g_gain, g_gain_ref[...])
    emit(buffer_ref.at[:, :128], slice(3 * HALF, 3 * HALF + 128))


def qkv_weight_gradient(*args):
    outs = [((count, PIECE, 3 * HALF + 128), jnp.bfloat16) for count in (8, 8, 16)]
    scratch = [((D, HALF), jnp.float32)]
    return kernel_call(qkv_weight_kernel, outs, scratch, "qkv_weights", 2 * 10**9, 8 * MEGA)(*args)


def qkv_input_kernel(me_ref, weight_ref, dq_ref, dk_ref, dv_ref, own_ref, across_ref, peer_ref):
    targets = (own_ref, peer_ref.at[0], across_ref, peer_ref.at[1])
    for i, target in enumerate(targets):
        rows = slice(256 * i, 256 * (i + 1))
        grad = matmul(dk_ref[rows, :], weight_ref[:, HALF : 2 * HALF], NT)
        grad = grad + matmul(dv_ref[rows, :], weight_ref[:, 2 * HALF :], NT)
        if i < 2:
            grad = grad + matmul(dq_ref[rows, :], weight_ref[:, :HALF], NT)
        target[...] = grad.astype(target.dtype)


def qkv_input_gradient(*args):
    bf16 = jnp.bfloat16
    outs = [((256, D), bf16), ((256, D), bf16), ((2, 256, D), bf16)]
    return kernel_call(qkv_input_kernel, outs, [], "qkv_inputs", 2 * 10**9, 6 * MEGA)(*args)


def paired_chips(hidden_in, grad_out, segment_ids, w_qkv, w_out, w_in, w_down, gain_attn, gain_mlp):
    bf16, f32 = jnp.bfloat16, jnp.float32
    dp, ctx = lax.axis_index("dp"), lax.axis_index("ctx")
    me = dp * 8 + ctx
    me_ref = me.reshape(1).astype(jnp.int32)
    c, zl, x = dp % 2, (ctx // 2) % 2, ctx % 2
    rows = hidden_in.shape[1]

    def to_chips(values):
        return (
            send_swapped(pick(zl, values[0], values[1]), 0),
            send_swapped(pick(zl, values[1], values[0]), 2),
        )

    def from_chips(values):
        block_a, block_b = send_swapped(values[:rows], 0), send_swapped(values[rows:], 2)
        return jnp.stack([pick(zl, block_a, block_b), pick(zl, block_b, block_a)])

    ids = jnp.pad(segment_ids[:, None, :], ((0, 0), (0, 7), (0, D - rows))).astype(bf16)
    packed = [pick(zl, a, b) for a, b in ((hidden_in, hidden_in[::-1]), (ids, ids[::-1]))]
    packed = jnp.concatenate(packed, 1)

    gains = lax.dynamic_update_slice(
        jnp.zeros((8, 3 * HALF), f32), jnp.stack([gain_attn, gain_mlp]), (0, 192 * dp)
    )

    def my_columns(core):
        columns = [lax.dynamic_slice_in_dim(w_qkv, t * D + core * HALF, HALF, 1) for t in range(3)]
        return jnp.concatenate([jnp.concatenate(columns, 1), gains]).astype(bf16)

    within = jnp.arange(rows, dtype=jnp.int32)
    starts = []
    for far in range(2):
        for core in range(2):
            for low in range(2):
                starts.append((2 * (2 * (c ^ core) + (zl ^ low)) + (x ^ far)) * rows + within)
    cosine, sine = rotary_tables(jnp.concatenate(starts), HD)
    sine = sine * jnp.where(jnp.arange(HD) < HD // 2, -1.0, 1.0)
    cosine, sine = jnp.concatenate([cosine] * 2, 1), jnp.concatenate([sine] * 2, 1)

    pack = jnp.stack([my_columns(c), my_columns(1 - c)])
    pack, packed = stage(pack, packed)
    own = jnp.stack([send_swapped(packed[0], 0), send_swapped(packed[1], 2)])
    up = send(pack, 16)
    w_down = w_down.T
    cut, rest = slice(0, 768), slice(768, FF)
    late = slice(FF + 768, None)
    first = jnp.concatenate([w_out, w_in[:, cut], w_in[:, FF : FF + 768], w_down[:, cut]], 1)
    second = jnp.concatenate([w_in[:, rest], w_in[:, late], w_down[:, rest]], 1)
    own, first, second = stage(own, first.astype(bf16), second.astype(bf16))
    up_first, up_second = send(first, 16), send(second, 16)
    across = send(own, 1)
    across, up, cosine, sine = stage(across, up, cosine, sine)
    by_core = send(jnp.stack([pack[1], up[1]]), 8)
    peer = send(jnp.stack([own, across]), 8)
    grad_low = to_chips(after(grad_out, across))

    normed, queries, keys, values, probs, att_own, att_peer, att, inverse, weight, gains = (
        attention_forward(
            me_ref, own, across, peer, pack, up, by_core, cosine, sine
        )
    )
    grad_a, grad_b, att_peer, first = stage(*grad_low, att_peer, first)
    grad_low = jnp.concatenate([grad_a, grad_b])
    att_peer = send(att_peer, 8)
    core_first = send(first, 8)
    core_second = send(after(second, grad_low), 8)
    up_first, att_peer = stage(up_first, att_peer)
    both_first = send(up_first, 8)
    down, g_norm, xhat, scale, w_out, away_1, stay_1 = mlp_first(
        me_ref, own, att_own, att_peer, grad_low, gains, first, core_first, up_first, both_first
    )
    away_1, up_second, core_second = stage(away_1, up_second, core_second)
    both_second = send(up_second, 8)

    def halves(values, got):
        count = values.shape[0] // 2
        return [
            plus(values[part, :, columns], got[part, :, columns])
            for columns in (slice(0, 3 * WIDTH), slice(3 * WIDTH, None))
            for part in (slice(0, count), slice(count, None))
        ]

    def fold(stay, got):
        return plus(stay[:4], got[:4]), plus(stay[4:], got[4:])

    def fold_near(part):
        return jnp.stack([part[0], part[2]]), jnp.stack([part[1], part[3]])

    def joined(stay_a, got_a, stay_b, got_b):
        return fold_near(jnp.concatenate([plus(stay_a, got_a), plus(stay_b, got_b)], 2))

    got_1 = send(away_1, 8)
    both_second, down = stage(both_second, down)
    layer_out, g_mixed, g_att, g_att_peer, away_2, stay_2, g_gain = mlp_second(
        me_ref,
        *(att_own, att_peer, grad_low, gains),
        *(second, core_second, up_second, both_second),
        *(down, g_norm, xhat, scale, w_out),
    )
    got_1, away_2, g_att_peer, layer_out = stage(got_1, away_2, g_att_peer, layer_out)
    g_att_peer = send(g_att_peer, 8)
    got_2 = send(away_2, 8)
    stay_1a, leave_a, stay_1b, leave_b = halves(stay_1, got_1)
    got_1a, got_1b = send(leave_a, 16), send(leave_b, 1)
    g_att_peer, layer_out = stage(g_att_peer, layer_out)
    layer_out = from_chips(layer_out)
    grads = attention_backward(
        me_ref, g_att, g_att_peer, att, inverse, queries, keys, values, probs, cosine, sine
    )
    got_1a, got_1b, got_2, layer_out, *grads = stage(got_1a, got_1b, got_2, layer_out, *grads)

    stay_1a, leave_1a = fold(stay_1a, got_1a)
    stay_1b, leave_1b = fold(stay_1b, got_1b)
    got_1a, got_1b = send(leave_1a, 1), send(leave_1b, 16)
    stay_2a, leave_a, stay_2b, leave_b = halves(stay_2, got_2)
    got_2a, got_2b = send(leave_a, 16), send(leave_b, 1)
    g_gain, *_ = stage(g_gain, leave_1a, leave_1b, leave_a, leave_b)
    keep_a, away_a, peer_b = qkv_weight_gradient(me_ref, normed, weight, g_gain, *grads)

    got_1a, got_1b, away_a, peer_b, *grads = stage(got_1a, got_1b, away_a, peer_b, *grads)
    got_core, got_a = send(peer_b, 8), send(away_a, 16)
    keep_1, leave_1 = joined(stay_1a, got_1a, stay_1b, got_1b)
    got_1 = send(leave_1, 2)
    weight, _ = stage(weight, leave_1)
    near, across, peer = qkv_input_gradient(me_ref, weight, *grads)

    got_core, near, across, peer = stage(got_core, near, across, peer)
    keep_b, away_b = got_core[:8], got_core[8:]
    got_b = send(away_b, 1)
    peer = send(peer, 8)
    got_2a, got_2b, got_1, _ = stage(got_2a, got_2b, got_1, away_b)
    stay_2a, leave_2a = fold(stay_2a, got_2a)
    stay_2b, leave_2b = fold(stay_2b, got_2b)
    got_2a, got_2b = send(leave_2a, 1), send(leave_2b, 16)
    keep_1 = plus(keep_1, got_1)
    peer, keep_1, *_ = stage(peer, keep_1, leave_2a, leave_2b)
    got_1 = send(keep_1[1], 4)
    across = plus(across, peer[1])
    got_a, got_b, across, _ = stage(got_a, got_b, across, keep_1)

    stay_a, leave_a = fold(keep_a, got_a)
    stay_b, leave_b = fold(keep_b, got_b)
    got_a, got_b = send(leave_a, 1), send(leave_b, 16)
    got_1, got_2a, got_2b, across, *_ = stage(got_1, got_2a, got_2b, across, leave_a, leave_b)
    sum_1 = plus(keep_1[0], got_1)
    far_1 = send(sum_1, 4)
    keep_2, leave_2 = joined(stay_2a, got_2a, stay_2b, got_2b)
    got_2 = send(leave_2, 2)
    got_across = send(across, 1)
    got_a, got_b, *_ = stage(got_a, got_b, sum_1, leave_2, across)

    total = jnp.concatenate([plus(stay_a, got_a), plus(stay_b, got_b)], 2)
    got = [send(total[dz], 2 * dz) for dz in range(1, 4)]
    far_1, got_2, got_across, _ = stage(far_1, got_2, got_across, total)
    sum_1 = jnp.stack([sum_1, far_1])
    far_1 = send(sum_1, 2)
    keep_2 = plus(keep_2, got_2)
    got_2 = send(keep_2[1], 4)
    g_normed = plus(near, peer[0]).astype(f32) + got_across.astype(f32)
    xhat, scale = norm_parts(own[:, :rows].reshape(2 * rows, D).astype(f32))
    grad_in = (g_mixed + norm_back(xhat, scale, g_normed, gains[0])).astype(bf16)
    grad_in, _, _, *got = stage(grad_in, sum_1, keep_2, *got)

    total = sum((part.astype(f32) for part in got), total[0].astype(f32)).astype(bf16)
    got = [send(total, 2 * dz) for dz in range(1, 4)]
    far_1, got_2, _ = stage(far_1, got_2, total)
    sum_1 = jnp.stack([sum_1, far_1], 1).reshape(4, PIECE, -1)
    far_1 = send(sum_1, 1)
    sum_2 = plus(keep_2[0], got_2)
    far_2 = send(sum_2, 4)
    far_2, total, *got = stage(far_2, total, *got)
    total = jnp.stack([total, *got])
    far = send(total, 1)
    sum_2 = jnp.stack([sum_2, far_2])
    far_2 = send(sum_2, 2)
    grad_in, far_1, _ = stage(grad_in, far_1, total)
    grad_in = from_chips(grad_in)
    far_2, total = stage(far_2, total)
    sum_2 = jnp.stack([sum_2, far_2], 1).reshape(4, PIECE, -1)
    far_2 = send(sum_2, 1)
    g_w_qkv, g_gains = finish(
        qkv_result_kernel, me_ref, (total, far), ((192, 3 * D), (8, 192)), (256, 128), "qkv_result"
    )
    g_w_in, g_w_out, g_w_down = finish(
        mlp_result_kernel,
        me_ref,
        (sum_1, far_1, sum_2, far_2),
        ((192, 2 * FF), (192, D), (192, FF)),
        None,
        "mlp_result",
    )
    g_gain_attn = g_gains[0] / gain_attn.astype(bf16).astype(f32)
    return (layer_out, grad_in, g_w_qkv, g_w_out, g_w_in, g_w_down.T, g_gain_attn, g_gains[1])


def solution(mesh):
    whole_fit = mesh.shape["dp"] == 4 and mesh.shape["ctx"] == 8
    return jax.shard_map(
        paired_chips if whole_fit else on_device,
        mesh=mesh,
        in_specs=(
            P("dp", "ctx", None),
            P("dp", "ctx", None),
            P("dp", "ctx"),
            P("dp", None),
            P("dp", None),
            P("dp", None),
            P(None, "dp"),
            P("dp"),
            P("dp"),
        ),
        out_specs=(
            P("dp", "ctx", None),
            P("dp", "ctx", None),
            P("dp", None),
            P("dp", None),
            P("dp", None),
            P(None, "dp"),
            P("dp"),
            P("dp"),
        ),
        check_vma=False,
    )
```

```python
import math

import jax
import jax.numpy as jnp
from jax import lax
from jax.experimental import pallas as pl
from jax.experimental.pallas import tpu as pltpu
from jax.sharding import PartitionSpec as P

D = 768
HEADS = 12
HD = 64
FF = 1152


norm_eps = 1e-05
theta_base = 160000.0


def layer_norm(values, gain):
    mean_val = jnp.mean(values, axis=-1, keepdims=True)
    centred = values - mean_val
    variance = jnp.mean(centred * centred, axis=-1, keepdims=True)
    return centred * lax.rsqrt(variance + norm_eps) * gain


def rotary_tables(positions, head_size):
    half_size = head_size // 2
    exponents = jnp.arange(half_size, dtype=jnp.float32) * (2.0 / head_size)
    inv_freq = 1.0 / theta_base**exponents
    angles = positions.astype(jnp.float32)[:, None] * inv_freq[None, :]
    cosine = jnp.cos(angles)
    sine = jnp.sin(angles)
    return (jnp.concatenate([cosine, cosine], -1), jnp.concatenate([sine, sine], -1))


def rotate(values, cosine, sine):
    half_size = values.shape[-1] // 2
    turned = jnp.concatenate([-values[..., half_size:], values[..., :half_size]], -1)
    return values * cosine[:, None, :] + turned * sine[:, None, :]


def fold_blocks(carry, pieces, piece_segments, work, rows):
    count = piece_segments.shape[0]
    size = math.gcd(count, 4 * rows)
    number = count // size
    blocks = tuple((part.reshape((number, size) + part.shape[1:]) for part in pieces))
    blocks = blocks + (piece_segments.reshape(number, size),)

    def step(acc, block):
        acc = work(acc, block)
        return (acc, None)

    carry, _ = lax.scan(step, carry, blocks)
    return carry


def on_device(hidden_in, grad_out, segment_ids, w_qkv, w_out, w_in, w_down, gain_attn, gain_mlp):
    rows = hidden_in.shape[1]
    local_seqs = hidden_in.shape[0]
    score_scale = HD ** (-0.5)
    bf16 = jnp.bfloat16
    f32 = jnp.float32
    gathered = (
        lax.all_gather(w_qkv.astype(bf16), "dp", axis=0, tiled=True),
        lax.all_gather(w_out.astype(bf16), "dp", axis=0, tiled=True),
        lax.all_gather(w_in.astype(bf16), "dp", axis=0, tiled=True),
        lax.all_gather(w_down.astype(bf16), "dp", axis=1, tiled=True),
        lax.all_gather(gain_attn.astype(bf16), "dp", axis=0, tiled=True),
        lax.all_gather(gain_mlp.astype(bf16), "dp", axis=0, tiled=True),
    )
    weight_qkv, weight_out, weight_in, weight_down, gain_low_a, gain_low_b = gathered
    gain_first = gain_low_a.astype(f32)
    gain_second = gain_low_b.astype(f32)
    whole_segments = lax.all_gather(segment_ids, "ctx", axis=1, tiled=True)
    positions = lax.axis_index("ctx") * rows + jnp.arange(rows, dtype=jnp.int32)
    cosine, sine = rotary_tables(positions, HD)

    def gated(values_in):
        return jax.nn.gelu(values_in[:, :FF], approximate=False) * values_in[:, FF:]

    def turn(pair):
        return (rotate(pair[0], cosine, sine), rotate(pair[1], cosine, sine))

    def one_sequence(seq_index):
        hidden = hidden_in[seq_index].astype(f32)
        own_segments = segment_ids[seq_index]
        all_segments = whole_segments[seq_index]
        normed_first, first_back = jax.vjp(layer_norm, hidden, gain_first)
        normed_attn = normed_first.astype(bf16)
        qkv = jnp.dot(normed_attn, weight_qkv, preferred_element_type=f32)
        q_lin = qkv[:, :D].reshape(rows, HEADS, HD)
        k_lin = qkv[:, D : 2 * D].reshape(rows, HEADS, HD)
        v_lin = qkv[:, 2 * D :].reshape(rows, HEADS, HD)
        turned, turn_back = jax.vjp(turn, (q_lin, k_lin))
        queries = turned[0].astype(bf16)
        keys = turned[1].astype(bf16)
        values = v_lin.astype(bf16)

        def forward_work(acc, block):
            key_blk, value_blk, seg_blk = block
            total, summed = acc
            scores = (
                jnp.einsum("thd,shd->hts", queries, key_blk, preferred_element_type=f32)
                * score_scale
            )
            same = own_segments[:, None] == seg_blk[None, :]
            expo = jnp.where(same[None], jnp.exp(scores), 0.0)
            total = total + jnp.sum(expo, axis=-1)
            summed = summed + jnp.einsum(
                "hts,shd->thd", expo.astype(bf16), value_blk, preferred_element_type=f32
            )
            return (total, summed)

        start_fwd = (jnp.zeros((HEADS, rows), f32), jnp.zeros((rows, HEADS, HD), f32))
        key_piece = lax.all_gather(keys.reshape(rows, D), "ctx", axis=0, tiled=True)
        value_piece = lax.all_gather(values.reshape(rows, D), "ctx", axis=0, tiled=True)
        count = key_piece.shape[0]
        piece_segments = all_segments
        parts = (key_piece.reshape(count, HEADS, HD), value_piece.reshape(count, HEADS, HD))
        total, summed = fold_blocks(start_fwd, parts, piece_segments, forward_work, rows)
        total_rows = jnp.transpose(total)
        attended = (summed / total_rows[:, :, None]).reshape(rows, D).astype(bf16)
        mixed = hidden + jnp.dot(attended, weight_out, preferred_element_type=f32)
        normed_second, second_back = jax.vjp(layer_norm, mixed, gain_second)
        normed_mlp = normed_second.astype(bf16)
        gate_up = jnp.dot(normed_mlp, weight_in, preferred_element_type=f32)
        activ_f, gated_back = jax.vjp(gated, gate_up)
        activ = activ_f.astype(bf16)
        layer_out = (mixed + jnp.dot(activ, weight_down, preferred_element_type=f32)).astype(bf16)
        grad_low = grad_out[seq_index]
        g_w_down = jnp.einsum("tf,td->fd", activ, grad_low, preferred_element_type=f32)
        g_activ = jnp.einsum("td,fd->tf", grad_low, weight_down, preferred_element_type=f32)
        g_gate_up = gated_back(g_activ)[0].astype(bf16)
        g_w_in = jnp.einsum("ti,tj->ij", normed_mlp, g_gate_up, preferred_element_type=f32)
        g_normed_mlp = jnp.einsum("tj,ij->ti", g_gate_up, weight_in, preferred_element_type=f32)
        g_mixed_norm, g_gain_mlp = second_back(g_normed_mlp)
        g_mixed = grad_low.astype(f32) + g_mixed_norm
        g_mixed_low = g_mixed.astype(bf16)
        g_w_out = jnp.einsum("ti,tj->ij", attended, g_mixed_low, preferred_element_type=f32)
        g_att = jnp.einsum(
            "tj,ij->ti", g_mixed_low, weight_out, preferred_element_type=f32
        ).reshape(rows, HEADS, HD)
        g_summed = (g_att / total_rows[:, :, None]).astype(bf16)
        row_term = jnp.sum(g_att * summed, axis=-1) / (total_rows * total_rows)
        own_rows = jnp.transpose(row_term)
        all_rows = lax.all_gather(row_term, "ctx", axis=0, tiled=True)

        def query_work(acc, block):
            key_blk, value_blk, seg_blk = block
            scores = (
                jnp.einsum("thd,shd->hts", queries, key_blk, preferred_element_type=f32)
                * score_scale
            )
            same = own_segments[:, None] == seg_blk[None, :]
            expo = jnp.where(same[None], jnp.exp(scores), 0.0)
            product = jnp.einsum("thd,shd->hts", g_summed, value_blk, preferred_element_type=f32)
            g_scores = (expo * (product - own_rows[:, :, None])).astype(bf16)
            return acc + jnp.einsum("hts,shd->thd", g_scores, key_blk, preferred_element_type=f32)

        key_piece = lax.all_gather(keys.reshape(rows, D), "ctx", axis=0, tiled=True)
        value_piece = lax.all_gather(values.reshape(rows, D), "ctx", axis=0, tiled=True)
        count = key_piece.shape[0]
        piece_segments = all_segments
        parts = (key_piece.reshape(count, HEADS, HD), value_piece.reshape(count, HEADS, HD))
        g_queries = (
            fold_blocks(jnp.zeros((rows, HEADS, HD), f32), parts, piece_segments, query_work, rows)
            * score_scale
        )

        def key_work(acc, block):
            query_blk, gsum_blk, row_blk, seg_blk = block
            g_keys, g_values = acc
            scores = (
                jnp.einsum("shd,thd->hst", query_blk, keys, preferred_element_type=f32)
                * score_scale
            )
            same = seg_blk[:, None] == own_segments[None, :]
            expo = jnp.where(same[None], jnp.exp(scores), 0.0)
            g_values = g_values + jnp.einsum(
                "hst,shd->thd", expo.astype(bf16), gsum_blk, preferred_element_type=f32
            )
            product = jnp.einsum("shd,thd->hst", gsum_blk, values, preferred_element_type=f32)
            g_scores = (expo * (product - jnp.transpose(row_blk)[:, :, None])).astype(bf16)
            g_keys = g_keys + jnp.einsum(
                "hst,shd->thd", g_scores, query_blk, preferred_element_type=f32
            )
            return (g_keys, g_values)

        start_keys = (jnp.zeros((rows, HEADS, HD), f32), jnp.zeros((rows, HEADS, HD), f32))
        query_piece = lax.all_gather(queries.reshape(rows, D), "ctx", axis=0, tiled=True)
        gsum_piece = lax.all_gather(g_summed.reshape(rows, D), "ctx", axis=0, tiled=True)
        count = query_piece.shape[0]
        piece_segments = all_segments
        parts = (
            query_piece.reshape(count, HEADS, HD),
            gsum_piece.reshape(count, HEADS, HD),
            all_rows,
        )
        g_keys, g_values = fold_blocks(start_keys, parts, piece_segments, key_work, rows)
        g_keys = g_keys * score_scale
        unturned = turn_back((g_queries, g_keys))[0]
        g_qkv = jnp.concatenate(
            [unturned[0].reshape(rows, D), unturned[1].reshape(rows, D), g_values.reshape(rows, D)],
            -1,
        ).astype(bf16)
        g_w_qkv = jnp.einsum("ti,tj->ij", normed_attn, g_qkv, preferred_element_type=f32)
        g_normed_attn = jnp.einsum("tj,ij->ti", g_qkv, weight_qkv, preferred_element_type=f32)
        g_hidden_norm, g_gain_attn = first_back(g_normed_attn)
        grad_in = (g_mixed + g_hidden_norm).astype(bf16)
        terms = (g_w_qkv, g_w_out, g_w_in, g_w_down, g_gain_attn, g_gain_mlp)
        return (layer_out, grad_in, terms)

    outputs_fwd = []
    outputs_back = []
    terms = None
    for seq_index in range(local_seqs):
        layer_out, grad_in, seq_terms = one_sequence(seq_index)
        outputs_fwd.append(layer_out)
        outputs_back.append(grad_in)
        if terms is None:
            terms = seq_terms
        else:
            terms = tuple((old + new for old, new in zip(terms, seq_terms)))
    everywhere = lax.psum(terms, "ctx")
    owned = (
        lax.psum_scatter(
            everywhere[0].astype(jnp.bfloat16), "dp", scatter_dimension=0, tiled=True
        ).astype(jnp.float32),
        lax.psum_scatter(
            everywhere[1].astype(jnp.bfloat16), "dp", scatter_dimension=0, tiled=True
        ).astype(jnp.float32),
        lax.psum_scatter(
            everywhere[2].astype(jnp.bfloat16), "dp", scatter_dimension=0, tiled=True
        ).astype(jnp.float32),
        lax.psum_scatter(
            everywhere[3].astype(jnp.bfloat16), "dp", scatter_dimension=1, tiled=True
        ).astype(jnp.float32),
        lax.psum_scatter(
            everywhere[4].astype(jnp.bfloat16), "dp", scatter_dimension=0, tiled=True
        ).astype(jnp.float32),
        lax.psum_scatter(
            everywhere[5].astype(jnp.bfloat16), "dp", scatter_dimension=0, tiled=True
        ).astype(jnp.float32),
    )
    return (
        jnp.stack(outputs_fwd),
        jnp.stack(outputs_back),
        owned[0],
        owned[1],
        owned[2],
        owned[3],
        owned[4],
        owned[5],
    )


HALF = 384
PIECE = 24


def send(values, mask):
    return lax.ppermute(values, ("dp", "ctx"), [(i, i ^ mask) for i in range(32)])


def send_swapped(values, mask):
    def target(i):
        core, high = (i >> 3) & 1, (i >> 2) & 1
        return (i & ~12) | (high << 3) | (core << 2)

    return lax.ppermute(values, ("dp", "ctx"), [(i, target(i) ^ mask) for i in range(32)])


def pick(flag, first, second):
    return jnp.where(flag == 0, first, second)


VM = pl.BlockSpec(memory_space=pltpu.VMEM)
SM = pl.BlockSpec(memory_space=pltpu.SMEM)


def pieces_of(me, near_ref, far_ref):
    for slot, mask in enumerate(XZ):
        start = pl.multiple_of((me % 8 ^ mask) * PIECE, 8)
        yield start, (near_ref, far_ref)[slot // 4][slot % 4].astype(jnp.float32)


def qkv_result_kernel(me_ref, near_ref, far_ref, out_ref, gains_ref, buffer_ref):
    me = me_ref[0]
    core = (me // 8) % 2
    wide = 3 * HALF + 128
    for start, piece in pieces_of(me, near_ref, far_ref):
        rows = pl.ds(start, PIECE)
        for half in range(2):
            for t in range(3):
                column = pl.multiple_of(t * D + (half ^ core) * HALF, 128)
                first = half * wide + t * HALF
                out_ref[rows, pl.ds(column, HALF)] = piece[:, first : first + HALF]
        buffer_ref[rows, :] = piece[:, 3 * HALF : wide] + piece[:, wide + 3 * HALF :]
    gains_ref[...] = buffer_ref[...].T[:8, :192]


def mlp_result_kernel(
    me_ref, near_1, far_1, near_2, far_2, w_in_ref, w_out_ref, w_down_ref
):
    me = me_ref[0]
    for start, piece in pieces_of(me, near_1, far_1):
        rows = pl.ds(start, PIECE)
        w_in_ref[rows, :768] = piece[:, :768]
        w_in_ref[rows, FF : FF + 768] = piece[:, 768:1536]
        w_down_ref[rows, :768] = piece[:, 1536:]
    for start, piece in pieces_of(me, near_2, far_2):
        rows = pl.ds(start, PIECE)
        w_in_ref[rows, 768:FF] = piece[:, :384]
        w_in_ref[rows, FF + 768 :] = piece[:, 384:768]
        w_out_ref[rows, :384] = piece[:, 768:1152]
        w_out_ref[rows, 384:] = piece[:, 1536:]
        w_down_ref[rows, 768:] = piece[:, 1152:1536]


def plus(first, second):
    return (first.astype(jnp.float32) + second.astype(jnp.float32)).astype(jnp.bfloat16)


def finish(body, me, pieces, shapes, scratch, name):
    return pl.pallas_call(
        body,
        out_shape=tuple(jax.ShapeDtypeStruct(shape, jnp.float32) for shape in shapes),
        in_specs=[SM] + [VM] * len(pieces),
        out_specs=(VM,) * len(shapes),
        scratch_shapes=[pltpu.VMEM(scratch, jnp.float32)] if scratch else [],
        compiler_params=pltpu.CompilerParams(vmem_limit_bytes=24 << 20),
        name=name,
    )(me, *pieces)


XZ = [dx | (dz << 1) for dx in range(2) for dz in range(4)]


def masks(*bits):
    order = [0]
    for bit in bits:
        choices = (0, bit) if bit != 6 else (0, 2, 4, 6)
        order = [m | choice for m in order for choice in choices]
    return order


def after(values, *others):
    return lax.optimization_barrier((values,) + others)[0]


def stage(*values):
    return lax.optimization_barrier(values)


def norm_parts(values):
    mean_val = jnp.mean(values, axis=-1, keepdims=True)
    centred = values - mean_val
    variance = jnp.mean(centred * centred, axis=-1, keepdims=True)
    scale = lax.rsqrt(variance + norm_eps)
    return centred * scale, scale


def norm_back(xhat, scale, grad, gain):
    e = grad * gain
    return scale * (
        e
        - jnp.mean(e, axis=-1, keepdims=True)
        - xhat * jnp.mean(e * xhat, axis=-1, keepdims=True)
    )


NT = (((1,), (1,)), ((), ()))
FAR_APART = -1.0e30
MEGA = 1 << 20


def matmul(first, second, dims=None):
    dims = dims or (((1,), (0,)), ((), ()))
    return lax.dot_general(first, second, dims, preferred_element_type=jnp.float32)


def kernel_call(body, outs, scratch, name, flops, moved):
    count = len(outs)
    return lambda *args: pl.pallas_call(
        body,
        out_shape=tuple(jax.ShapeDtypeStruct(shape, kind) for shape, kind in outs),
        in_specs=[SM] + [VM] * (len(args) - 1),
        out_specs=(VM,) * count,
        scratch_shapes=[pltpu.VMEM(shape, kind) for shape, kind in scratch],
        compiler_params=pltpu.CompilerParams(vmem_limit_bytes=32 * MEGA),
        cost_estimate=pl.CostEstimate(flops=flops, bytes_accessed=moved, transcendentals=0),
        name=name,
    )(*args)


def swap_halves(pair):
    lane = lax.broadcasted_iota(jnp.int32, pair.shape, 1) % HD
    return jnp.where(lane < HD // 2, pltpu.roll(pair, 96, 1), pltpu.roll(pair, 32, 1))


def place_rows(me, pieces, whole_ref):
    for mask, piece in pieces:
        start = pl.multiple_of((me // 8 ^ mask) * 192, 16)
        whole_ref[pl.ds(start, 192), :] = piece


def attention_kernel(
    me_ref,
    own_ref,
    across_ref,
    peer_ref,
    pack_ref,
    up_ref,
    core_ref,
    cos_ref,
    sin_ref,
    normed_ref,
    q_ref,
    k_ref,
    v_ref,
    probs_ref,
    att_own_ref,
    att_peer_ref,
    att_ref,
    inv_ref,
    weight_ref,
    gains_ref,
    q_id_ref,
    keys_ref,
    values_ref,
):
    f32, bf16 = jnp.float32, jnp.bfloat16
    me = me_ref[0]
    shards = (pack_ref.at[0], core_ref.at[0], up_ref.at[0], core_ref.at[1])
    place_rows(me, [(mask, ref[:192, :]) for mask, ref in enumerate(shards)], weight_ref)
    gains = sum(ref[192:200, :].astype(f32) for ref in shards)[:, :D]
    gains_ref[...] = gains
    gain = gains[0:1, :]
    row_id = lax.broadcasted_iota(jnp.int32, (128, 128), 0).astype(f32)
    blocks = [own_ref.at[i] for i in range(2)] + [peer_ref.at[0, i] for i in range(2)]
    blocks += [across_ref.at[i] for i in range(2)] + [peer_ref.at[1, i] for i in range(2)]
    for i, block in enumerate(blocks):
        rows = slice(128 * i, 128 * (i + 1))
        hidden = block[:128, :].astype(f32)
        centred = hidden - jnp.mean(hidden, axis=1, keepdims=True)
        variance = jnp.mean(centred * centred, axis=1, keepdims=True)
        normed = (centred * lax.rsqrt(variance + norm_eps) * gain).astype(bf16)
        normed_ref[rows, :] = normed
        ids = block[128:136, :128].astype(f32)[0:1, :]
        hit = jnp.where(row_id == ids, 1.0, 0.0).T
        keys_ref[rows, 128:] = (1.0 - hit).astype(bf16)
        values_ref[rows, 128:] = jnp.ones((128, 128), bf16)
        if i < 4:
            q_id_ref[rows, :] = (hit * FAR_APART).astype(bf16)

    for i in range(4):
        rows = slice(256 * i, 256 * (i + 1))
        normed = normed_ref[rows, :]
        first = 0 if i < 2 else HALF
        qkv = matmul(normed, weight_ref[:, first:])
        for j in range(first // 128, 9):
            part = qkv[:, 128 * j - first : 128 * j - first + 128]
            columns = slice(128 * (j % 3), 128 * (j % 3) + 128)
            if j < 6:
                part = part * cos_ref[rows, :] + swap_halves(part) * sin_ref[rows, :]
            if j < 3:
                q_ref[rows, columns] = (part * HD**-0.5).astype(bf16)
            elif j < 6:
                k_ref[rows, columns] = part.astype(bf16)
            else:
                v_ref[rows, columns] = part.astype(bf16)

    low_head = lax.broadcasted_iota(jnp.int32, (256, 128), 1) < HD
    for pair in range(3):
        columns = slice(128 * pair, 128 * pair + 128)
        keys_ref[:, :128] = k_ref[:, columns]
        values_ref[:, :128] = v_ref[:, columns]
        for i in range(2):
            rows = slice(256 * i, 256 * (i + 1))
            queries = q_ref[rows, columns]
            found = []
            for head in range(2):
                picked = jnp.where(low_head == (head == 0), queries, jnp.zeros_like(queries))
                scores = matmul(
                    jnp.concatenate([picked, q_id_ref[rows, :]], 1), keys_ref[...], NT
                )
                probs = jnp.exp(scores).astype(bf16)
                probs_ref[2 * pair + head, rows, :] = probs
                found.append(matmul(probs, values_ref[...]))
            inverse = 1.0 / jnp.where(low_head, found[0][:, 128:], found[1][:, 128:])
            attended = jnp.where(low_head, found[0][:, :128], found[1][:, :128]) * inverse
            inv_ref[rows, columns] = inverse
            att_ref[rows, columns] = attended
            out_ref = att_own_ref if i == 0 else att_peer_ref
            out_ref[:, columns] = attended.astype(bf16)


def attention_forward(*args):
    f32, bf16 = jnp.float32, jnp.bfloat16
    outs = [
        ((1024, D), bf16),
        ((512, HALF), bf16),
        ((1024, HALF), bf16),
        ((1024, HALF), bf16),
        ((6, 512, 1024), bf16),
        ((256, HALF), bf16),
        ((256, HALF), bf16),
        ((512, HALF), f32),
        ((512, HALF), f32),
        ((D, 3 * HALF), bf16),
        ((8, D), f32),
    ]
    scratch = [((512, 128), bf16), ((1024, 256), bf16), ((1024, 256), bf16)]
    return kernel_call(attention_kernel, outs, scratch, "attention_fwd", 4 * 10**9, 8 * MEGA)(*args)


def put_pieces(me, order, values_ref, out_ref, columns):
    for slot, mask in enumerate(order):
        start = pl.multiple_of((me ^ mask) * PIECE, 8)
        out_ref[slot, :, columns] = values_ref[pl.ds(start, PIECE), :].astype(out_ref.dtype)


def gated_block(normed, grad, gate_rows, upper_rows, down_rows):
    bf16 = jnp.bfloat16
    gate = matmul(normed, gate_rows)
    upper = matmul(normed, upper_rows)
    chance = 0.5 + 0.5 * lax.erf(gate * math.sqrt(0.5))
    bell = jnp.exp(-0.5 * gate * gate) * (1.0 / math.sqrt(2.0 * math.pi))
    gelu = gate * chance
    g_activ = matmul(grad, down_rows)
    g_gate = (g_activ * upper * (chance + gate * bell)).astype(bf16)
    g_upper = (g_activ * gelu).astype(bf16)
    return (gelu * upper).astype(bf16), g_gate, g_upper


WIDTH = 384


def mlp_first_kernel(
    me_ref,
    own_ref,
    att_ref,
    att_peer_ref,
    grad_ref,
    gains_ref,
    shard_ref,
    core_ref,
    up_ref,
    both_ref,
    down_ref,
    g_normed_ref,
    xhat_ref,
    scale_ref,
    w_out_ref,
    away_ref,
    stay_ref,
    w_ref,
    buffer_ref,
):
    f32, bf16 = jnp.float32, jnp.bfloat16
    me = me_ref[0]
    core = (me // 8) % 2
    shards = (shard_ref, core_ref, up_ref, both_ref)
    for mask, ref in enumerate(shards):
        shard = me // 8 ^ mask
        head_row = (shard // 2 ^ core) * HALF + (shard % 2) * 192
        w_out_ref[pl.ds(pl.multiple_of(head_row, 16), 192), :] = ref[:, :D]
    place_rows(me, [(mask, ref[:, D:]) for mask, ref in enumerate(shards)], w_ref)

    attended = jnp.concatenate([att_ref[...], att_peer_ref[...]], 1)
    hidden = jnp.concatenate([own_ref[0, :128, :], own_ref[1, :128, :]]).astype(f32)
    mixed = hidden + matmul(attended, w_out_ref[...])
    centred = mixed - jnp.mean(mixed, axis=1, keepdims=True)
    scale = lax.rsqrt(jnp.mean(centred * centred, axis=1, keepdims=True) + norm_eps)
    xhat = centred * scale
    xhat_ref[...] = xhat
    scale_ref[...] = jnp.broadcast_to(scale, (256, 128))
    normed = (xhat * gains_ref[1:2, :]).astype(bf16)
    grad = grad_ref[...]
    normed_t, grad_t = normed.T, grad.T
    orders = masks(16, 1, 6), masks(1, 16, 6)

    def emit(values, late, first):
        buffer_ref[...] = values
        columns = pl.ds(pl.multiple_of(first, 128), WIDTH)
        for slot, (early_mask, late_mask) in enumerate(zip(*orders)):
            mask = early_mask + late * (late_mask - early_mask)
            for ref, core_mask in ((away_ref, 8), (stay_ref, 0)):
                start = pl.multiple_of((me ^ (mask + core_mask)) * PIECE, 8)
                ref[slot, :, columns] = buffer_ref[pl.ds(start, PIECE), :].astype(bf16)

    down_ref[...] = mixed
    g_normed_ref[...] = jnp.zeros_like(mixed)

    def block(i, carry):
        low, high, last = (
            w_ref[:, pl.ds(pl.multiple_of(first + WIDTH * i, 128), WIDTH)]
            for first in (0, 768, 1536)
        )
        activ, g_gate, g_upper = gated_block(normed, grad, low, high, last)
        down_ref[...] += matmul(activ, last, NT)
        g_normed_ref[...] += matmul(g_gate, low, NT) + matmul(g_upper, high, NT)
        emit(matmul(normed_t, g_gate), 0, WIDTH * i)
        emit(matmul(normed_t, g_upper), i, 768 + WIDTH * i)
        emit(matmul(grad_t, activ), 1, 1536 + WIDTH * i)
        return carry

    lax.fori_loop(0, 2, block, 0)


def mlp_first(*args):
    f32, bf16 = jnp.float32, jnp.bfloat16
    outs = [
        ((256, D), f32),
        ((256, D), f32),
        ((256, D), f32),
        ((256, 128), f32),
        ((D, D), bf16),
        ((16, PIECE, 6 * WIDTH), bf16),
        ((16, PIECE, 6 * WIDTH), bf16),
    ]
    scratch = [((D, 6 * WIDTH), bf16), ((D, WIDTH), f32)]
    return kernel_call(mlp_first_kernel, outs, scratch, "mlp_first", 3 * 10**9, 16 * MEGA)(*args)


def mlp_second_kernel(
    me_ref,
    att_ref,
    att_peer_ref,
    grad_ref,
    gains_ref,
    shard_ref,
    core_ref,
    up_ref,
    both_ref,
    down_ref,
    g_normed_ref,
    xhat_ref,
    scale_ref,
    w_out_ref,
    out_ref,
    g_mixed_ref,
    g_att_ref,
    g_att_peer_ref,
    away_ref,
    stay_ref,
    g_gain_ref,
    w_ref,
    buffer_ref,
):
    f32, bf16 = jnp.float32, jnp.bfloat16
    me = me_ref[0]
    core = (me // 8) % 2
    shards = (shard_ref, core_ref, up_ref, both_ref)
    place_rows(me, [(mask, ref[...]) for mask, ref in enumerate(shards)], w_ref)
    gain = gains_ref[1:2, :]
    xhat = xhat_ref[...]
    scale = scale_ref[:, 0:1]
    normed = (xhat * gain).astype(bf16)
    grad = grad_ref[...]
    normed_t, grad_t = normed.T, grad.T
    y_first, x_first = masks(16, 1, 6), masks(1, 16, 6)

    def emit(order, first):
        columns = slice(first, first + WIDTH)
        put_pieces(me, [m | 8 for m in order], buffer_ref, away_ref, columns)
        put_pieces(me, order, buffer_ref, stay_ref, columns)

    low, high, last = (slice(first, first + WIDTH) for first in (0, 384, 768))
    activ, g_gate, g_upper = gated_block(normed, grad, w_ref[:, low], w_ref[:, high], w_ref[:, last])
    g_normed = g_normed_ref[...] + matmul(g_gate, w_ref[:, low], NT)
    g_normed = g_normed + matmul(g_upper, w_ref[:, high], NT)
    e = g_normed * gain
    g_mixed = grad.astype(f32) + scale * (
        e
        - jnp.mean(e, axis=1, keepdims=True)
        - xhat * jnp.mean(e * xhat, axis=1, keepdims=True)
    )
    g_mixed_ref[...] = g_mixed
    g_low = g_mixed.astype(bf16)
    g_att = matmul(g_low, w_out_ref[...], NT).astype(bf16)
    g_att_ref[...] = g_att[:, :HALF]
    g_att_peer_ref[...] = g_att[:, HALF:]
    out_ref[...] = (down_ref[...] + matmul(activ, w_ref[:, last], NT)).astype(bf16)
    g_gain = jnp.broadcast_to(jnp.sum(xhat * g_normed, axis=0, keepdims=True), (128, D))
    row = lax.broadcasted_iota(jnp.int32, (128, D), 0)
    g_gain_ref[...] = jnp.where(row == 1, g_gain, 0.0).T
    buffer_ref[...] = matmul(normed_t, g_gate)
    emit(y_first, 0)
    buffer_ref[...] = matmul(normed_t, g_upper)
    emit(y_first, WIDTH)
    buffer_ref[...] = matmul(grad_t, activ)
    emit(x_first, 3 * WIDTH)
    attended_t = jnp.concatenate([att_ref[...], att_peer_ref[...]], 1).T
    for i in range(2):
        rows_out = matmul(attended_t, g_low[:, WIDTH * i : WIDTH * (i + 1)])
        for half in range(2):
            start = pl.multiple_of((half ^ core) * HALF, HALF)
            buffer_ref[pl.ds(start, HALF), :] = rows_out[HALF * half : HALF * (half + 1), :]
        emit(y_first if i == 0 else x_first, (2 + 2 * i) * WIDTH)


def mlp_second(*args):
    f32, bf16 = jnp.float32, jnp.bfloat16
    outs = [
        ((256, D), bf16),
        ((256, D), f32),
        ((256, HALF), bf16),
        ((256, HALF), bf16),
        ((16, PIECE, 5 * WIDTH), bf16),
        ((16, PIECE, 5 * WIDTH), bf16),
        ((D, 128), f32),
    ]
    scratch = [((D, 3 * WIDTH), bf16), ((D, WIDTH), f32)]
    return kernel_call(mlp_second_kernel, outs, scratch, "mlp_second", 2 * 10**9, 10 * MEGA)(*args)


def attention_back_kernel(
    me_ref,
    g_own_ref,
    g_peer_ref,
    att_ref,
    inv_ref,
    q_ref,
    k_ref,
    v_ref,
    probs_ref,
    cos_ref,
    sin_ref,
    dq_ref,
    dk_ref,
    dv_ref,
    values_ref,
):
    f32, bf16 = jnp.float32, jnp.bfloat16
    low_head = lax.broadcasted_iota(jnp.int32, (1024, 128), 1) < HD
    lane = lax.broadcasted_iota(jnp.int32, (512, 128), 1)
    values_ref[:, 128:] = jnp.ones((1024, 128), bf16)
    for pair in range(3):
        columns = slice(128 * pair, 128 * pair + 128)
        values_ref[:, :128] = v_ref[:, columns]
        queries_t, keys = q_ref[:, columns].T, k_ref[:, columns]
        grad = jnp.concatenate([g_own_ref[:, columns], g_peer_ref[:, columns]]).astype(f32)
        grad = grad * inv_ref[:, columns]
        terms = grad * att_ref[:, columns]
        grad = grad.astype(bf16)
        grad_t = grad.T
        g_queries = jnp.zeros((512, 128), f32)
        g_keys, g_values = [], []
        for head in range(2):
            mine = low_head == (head == 0)
            rows = slice(HD * head, HD * head + HD)
            row = jnp.sum(jnp.where(mine[:512], terms, 0.0), axis=1, keepdims=True)
            high = row.astype(bf16)
            middle = (row - high.astype(f32)).astype(bf16)
            rest = (row - high.astype(f32) - middle.astype(f32)).astype(bf16)
            extra = jnp.where(lane == 0, -high.astype(f32), 0.0)
            extra = jnp.where(lane == 1, -middle.astype(f32), extra)
            extra = jnp.where(lane == 2, -rest.astype(f32), extra).astype(bf16)
            picked = jnp.where(mine[:512], grad, jnp.zeros_like(grad))
            product = matmul(jnp.concatenate([picked, extra], 1), values_ref[...], NT)
            probs = probs_ref[2 * pair + head]
            g_scores = (probs.astype(f32) * product).astype(bf16)
            g_queries = g_queries + matmul(g_scores, jnp.where(mine, keys, jnp.zeros_like(keys)))
            g_keys.append(matmul(queries_t[rows, :], g_scores))
            g_values.append(matmul(grad_t[rows, :], probs))
        g_queries = g_queries * HD**-0.5
        near = slice(0, 512)
        dq_ref[:, columns] = (
            g_queries * cos_ref[near, :] - swap_halves(g_queries) * sin_ref[near, :]
        ).astype(bf16)
        g_keys = jnp.concatenate(g_keys).T
        dk_ref[:, columns] = (
            g_keys * cos_ref[...] - swap_halves(g_keys) * sin_ref[...]
        ).astype(bf16)
        dv_ref[:, columns] = jnp.concatenate(g_values).T.astype(bf16)


def attention_backward(*args):
    bf16 = jnp.bfloat16
    outs = [((512, HALF), bf16), ((1024, HALF), bf16), ((1024, HALF), bf16)]
    scratch = [((1024, 256), bf16)]
    return kernel_call(
        attention_back_kernel, outs, scratch, "attention_bwd", 5 * 10**9, 10 * MEGA
    )(*args)


def qkv_weight_kernel(
    me_ref,
    normed_ref,
    weight_ref,
    g_gain_ref,
    dq_ref,
    dk_ref,
    dv_ref,
    keep_a,
    away_a,
    peer_b,
    buffer_ref,
):
    me = me_ref[0]
    order_a, order_b = masks(1, 6), masks(1, 16, 6)
    normed_t = normed_ref[...].T

    def emit(values_ref, columns):
        put_pieces(me, order_a, values_ref, keep_a, columns)
        put_pieces(me, [m | 16 for m in order_a], values_ref, away_a, columns)
        put_pieces(me, [m | 8 for m in order_b], values_ref, peer_b, columns)

    g_gain = jnp.zeros((D, 1), jnp.float32)
    for i, ref in enumerate((dq_ref, dk_ref, dv_ref)):
        columns = slice(HALF * i, HALF * (i + 1))
        values = matmul(normed_t[:, : ref.shape[0]], ref[...])
        weight = weight_ref[:, columns].astype(jnp.float32)
        g_gain = g_gain + jnp.sum(values * weight, axis=1, keepdims=True)
        buffer_ref[...] = values
        emit(buffer_ref, columns)
    lane = lax.broadcasted_iota(jnp.int32, (D, 128), 1)
    buffer_ref[:, :128] = jnp.where(lane == 0, g_gain, g_gain_ref[...])
    emit(buffer_ref.at[:, :128], slice(3 * HALF, 3 * HALF + 128))


def qkv_weight_gradient(*args):
    outs = [((count, PIECE, 3 * HALF + 128), jnp.bfloat16) for count in (8, 8, 16)]
    scratch = [((D, HALF), jnp.float32)]
    return kernel_call(qkv_weight_kernel, outs, scratch, "qkv_weights", 2 * 10**9, 8 * MEGA)(*args)


def qkv_input_kernel(me_ref, weight_ref, dq_ref, dk_ref, dv_ref, own_ref, across_ref, peer_ref):
    targets = (own_ref, peer_ref.at[0], across_ref, peer_ref.at[1])
    for i, target in enumerate(targets):
        rows = slice(256 * i, 256 * (i + 1))
        grad = matmul(dk_ref[rows, :], weight_ref[:, HALF : 2 * HALF], NT)
        grad = grad + matmul(dv_ref[rows, :], weight_ref[:, 2 * HALF :], NT)
        if i < 2:
            grad = grad + matmul(dq_ref[rows, :], weight_ref[:, :HALF], NT)
        target[...] = grad.astype(target.dtype)


def qkv_input_gradient(*args):
    bf16 = jnp.bfloat16
    outs = [((256, D), bf16), ((256, D), bf16), ((2, 256, D), bf16)]
    return kernel_call(qkv_input_kernel, outs, [], "qkv_inputs", 2 * 10**9, 6 * MEGA)(*args)


def paired_chips(hidden_in, grad_out, segment_ids, w_qkv, w_out, w_in, w_down, gain_attn, gain_mlp):
    bf16, f32 = jnp.bfloat16, jnp.float32
    dp, ctx = lax.axis_index("dp"), lax.axis_index("ctx")
    me = dp * 8 + ctx
    me_ref = me.reshape(1).astype(jnp.int32)
    c, zl, x = dp % 2, (ctx // 2) % 2, ctx % 2
    rows = hidden_in.shape[1]

    def to_chips(values):
        return (
            send_swapped(pick(zl, values[0], values[1]), 0),
            send_swapped(pick(zl, values[1], values[0]), 2),
        )

    def from_chips(values):
        block_a, block_b = send_swapped(values[:rows], 0), send_swapped(values[rows:], 2)
        return jnp.stack([pick(zl, block_a, block_b), pick(zl, block_b, block_a)])

    ids = jnp.pad(segment_ids[:, None, :], ((0, 0), (0, 7), (0, D - rows))).astype(bf16)
    packed = [pick(zl, a, b) for a, b in ((hidden_in, hidden_in[::-1]), (ids, ids[::-1]))]
    packed = jnp.concatenate(packed, 1)

    gains = lax.dynamic_update_slice(
        jnp.zeros((8, 3 * HALF), f32), jnp.stack([gain_attn, gain_mlp]), (0, 192 * dp)
    )

    def my_columns(core):
        columns = [lax.dynamic_slice_in_dim(w_qkv, t * D + core * HALF, HALF, 1) for t in range(3)]
        return jnp.concatenate([jnp.concatenate(columns, 1), gains]).astype(bf16)

    within = jnp.arange(rows, dtype=jnp.int32)
    starts = []
    for far in range(2):
        for core in range(2):
            for low in range(2):
                starts.append((2 * (2 * (c ^ core) + (zl ^ low)) + (x ^ far)) * rows + within)
    cosine, sine = rotary_tables(jnp.concatenate(starts), HD)
    sine = sine * jnp.where(jnp.arange(HD) < HD // 2, -1.0, 1.0)
    cosine, sine = jnp.concatenate([cosine] * 2, 1), jnp.concatenate([sine] * 2, 1)

    pack = jnp.stack([my_columns(c), my_columns(1 - c)])
    pack, packed = stage(pack, packed)
    own = jnp.stack([send_swapped(packed[0], 0), send_swapped(packed[1], 2)])
    up = send(pack, 16)
    w_down = w_down.T
    cut, rest = slice(0, 768), slice(768, FF)
    late = slice(FF + 768, None)
    first = jnp.concatenate([w_out, w_in[:, cut], w_in[:, FF : FF + 768], w_down[:, cut]], 1)
    second = jnp.concatenate([w_in[:, rest], w_in[:, late], w_down[:, rest]], 1)
    own, first, second = stage(own, first.astype(bf16), second.astype(bf16))
    up_first, up_second = send(first, 16), send(second, 16)
    across = send(own, 1)
    across, up, cosine, sine = stage(across, up, cosine, sine)
    by_core = send(jnp.stack([pack[1], up[1]]), 8)
    peer = send(jnp.stack([own, across]), 8)
    grad_low = to_chips(after(grad_out, across))

    normed, queries, keys, values, probs, att_own, att_peer, att, inverse, weight, gains = (
        attention_forward(
            me_ref, own, across, peer, pack, up, by_core, cosine, sine
        )
    )
    grad_a, grad_b, att_peer, first = stage(*grad_low, att_peer, first)
    grad_low = jnp.concatenate([grad_a, grad_b])
    att_peer = send(att_peer, 8)
    core_first = send(first, 8)
    core_second = send(after(second, grad_low), 8)
    up_first, att_peer = stage(up_first, att_peer)
    both_first = send(up_first, 8)
    down, g_norm, xhat, scale, w_out, away_1, stay_1 = mlp_first(
        me_ref, own, att_own, att_peer, grad_low, gains, first, core_first, up_first, both_first
    )
    away_1, up_second, core_second = stage(away_1, up_second, core_second)
    both_second = send(up_second, 8)

    def halves(values, got):
        count = values.shape[0] // 2
        return [
            plus(values[part, :, columns], got[part, :, columns])
            for columns in (slice(0, 3 * WIDTH), slice(3 * WIDTH, None))
            for part in (slice(0, count), slice(count, None))
        ]

    def fold(stay, got):
        return plus(stay[:4], got[:4]), plus(stay[4:], got[4:])

    def fold_near(part):
        return jnp.stack([part[0], part[2]]), jnp.stack([part[1], part[3]])

    def joined(stay_a, got_a, stay_b, got_b):
        return fold_near(jnp.concatenate([plus(stay_a, got_a), plus(stay_b, got_b)], 2))

    got_1 = send(away_1, 8)
    both_second, down = stage(both_second, down)
    layer_out, g_mixed, g_att, g_att_peer, away_2, stay_2, g_gain = mlp_second(
        me_ref,
        *(att_own, att_peer, grad_low, gains),
        *(second, core_second, up_second, both_second),
        *(down, g_norm, xhat, scale, w_out),
    )
    got_1, away_2, g_att_peer, layer_out = stage(got_1, away_2, g_att_peer, layer_out)
    g_att_peer = send(g_att_peer, 8)
    got_2 = send(away_2, 8)
    stay_1a, leave_a, stay_1b, leave_b = halves(stay_1, got_1)
    got_1a, got_1b = send(leave_a, 16), send(leave_b, 1)
    g_att_peer, layer_out = stage(g_att_peer, layer_out)
    layer_out = from_chips(layer_out)
    grads = attention_backward(
        me_ref, g_att, g_att_peer, att, inverse, queries, keys, values, probs, cosine, sine
    )
    got_1a, got_1b, got_2, layer_out, *grads = stage(got_1a, got_1b, got_2, layer_out, *grads)

    stay_1a, leave_1a = fold(stay_1a, got_1a)
    stay_1b, leave_1b = fold(stay_1b, got_1b)
    got_1a, got_1b = send(leave_1a, 1), send(leave_1b, 16)
    stay_2a, leave_a, stay_2b, leave_b = halves(stay_2, got_2)
    got_2a, got_2b = send(leave_a, 16), send(leave_b, 1)
    g_gain, *_ = stage(g_gain, leave_1a, leave_1b, leave_a, leave_b)
    keep_a, away_a, peer_b = qkv_weight_gradient(me_ref, normed, weight, g_gain, *grads)

    got_1a, got_1b, away_a, peer_b, *grads = stage(got_1a, got_1b, away_a, peer_b, *grads)
    got_core, got_a = send(peer_b, 8), send(away_a, 16)
    keep_1, leave_1 = joined(stay_1a, got_1a, stay_1b, got_1b)
    got_1 = send(leave_1, 2)
    weight, _ = stage(weight, leave_1)
    near, across, peer = qkv_input_gradient(me_ref, weight, *grads)

    got_core, near, across, peer = stage(got_core, near, across, peer)
    keep_b, away_b = got_core[:8], got_core[8:]
    got_b = send(away_b, 1)
    peer = send(peer, 8)
    got_2a, got_2b, got_1, _ = stage(got_2a, got_2b, got_1, away_b)
    stay_2a, leave_2a = fold(stay_2a, got_2a)
    stay_2b, leave_2b = fold(stay_2b, got_2b)
    got_2a, got_2b = send(leave_2a, 1), send(leave_2b, 16)
    keep_1 = plus(keep_1, got_1)
    peer, keep_1, *_ = stage(peer, keep_1, leave_2a, leave_2b)
    got_1 = send(keep_1[1], 4)
    across = plus(across, peer[1])
    got_a, got_b, across, _ = stage(got_a, got_b, across, keep_1)

    stay_a, leave_a = fold(keep_a, got_a)
    stay_b, leave_b = fold(keep_b, got_b)
    got_a, got_b = send(leave_a, 1), send(leave_b, 16)
    got_1, got_2a, got_2b, across, *_ = stage(got_1, got_2a, got_2b, across, leave_a, leave_b)
    sum_1 = plus(keep_1[0], got_1)
    far_1 = send(sum_1, 4)
    keep_2, leave_2 = joined(stay_2a, got_2a, stay_2b, got_2b)
    got_2 = send(leave_2, 2)
    got_across = send(across, 1)
    got_a, got_b, *_ = stage(got_a, got_b, sum_1, leave_2, across)

    total = jnp.concatenate([plus(stay_a, got_a), plus(stay_b, got_b)], 2)
    got = [send(total[dz], 2 * dz) for dz in range(1, 4)]
    far_1, got_2, got_across, _ = stage(far_1, got_2, got_across, total)
    sum_1 = jnp.stack([sum_1, far_1])
    far_1 = send(sum_1, 2)
    keep_2 = plus(keep_2, got_2)
    got_2 = send(keep_2[1], 4)
    g_normed = plus(near, peer[0]).astype(f32) + got_across.astype(f32)
    xhat, scale = norm_parts(own[:, :rows].reshape(2 * rows, D).astype(f32))
    grad_in = (g_mixed + norm_back(xhat, scale, g_normed, gains[0])).astype(bf16)
    grad_in, _, _, *got = stage(grad_in, sum_1, keep_2, *got)

    total = sum((part.astype(f32) for part in got), total[0].astype(f32)).astype(bf16)
    got = [send(total, 2 * dz) for dz in range(1, 4)]
    far_1, got_2, _ = stage(far_1, got_2, total)
    sum_1 = jnp.stack([sum_1, far_1], 1).reshape(4, PIECE, -1)
    far_1 = send(sum_1, 1)
    sum_2 = plus(keep_2[0], got_2)
    far_2 = send(sum_2, 4)
    far_2, total, *got = stage(far_2, total, *got)
    total = jnp.stack([total, *got])
    far = send(total, 1)
    sum_2 = jnp.stack([sum_2, far_2])
    far_2 = send(sum_2, 2)
    grad_in, far_1, _ = stage(grad_in, far_1, total)
    grad_in = from_chips(grad_in)
    far_2, total = stage(far_2, total)
    sum_2 = jnp.stack([sum_2, far_2], 1).reshape(4, PIECE, -1)
    far_2 = send(sum_2, 1)
    g_w_qkv, g_gains = finish(
        qkv_result_kernel, me_ref, (total, far), ((192, 3 * D), (8, 192)), (256, 128), "qkv_result"
    )
    g_w_in, g_w_out, g_w_down = finish(
        mlp_result_kernel,
        me_ref,
        (sum_1, far_1, sum_2, far_2),
        ((192, 2 * FF), (192, D), (192, FF)),
        None,
        "mlp_result",
    )
    g_gain_attn = g_gains[0] / gain_attn.astype(bf16).astype(f32)
    return (layer_out, grad_in, g_w_qkv, g_w_out, g_w_in, g_w_down.T, g_gain_attn, g_gains[1])


def solution(mesh):
    whole_fit = mesh.shape["dp"] == 4 and mesh.shape["ctx"] == 8
    return jax.shard_map(
        paired_chips if whole_fit else on_device,
        mesh=mesh,
        in_specs=(
            P("dp", "ctx", None),
            P("dp", "ctx", None),
            P("dp", "ctx"),
            P("dp", None),
            P("dp", None),
            P("dp", None),
            P(None, "dp"),
            P("dp"),
            P("dp"),
        ),
        out_specs=(
            P("dp", "ctx", None),
            P("dp", "ctx", None),
            P("dp", None),
            P("dp", None),
            P("dp", None),
            P(None, "dp"),
            P("dp"),
            P("dp"),
        ),
        check_vma=False,
    )
```

```python
import math

import jax
import jax.numpy as jnp
from jax import lax
from jax.experimental import pallas as pl
from jax.experimental.pallas import tpu as pltpu
from jax.sharding import PartitionSpec as P

D = 768
HEADS = 12
HD = 64
FF = 1152


norm_eps = 1e-05
theta_base = 160000.0


def layer_norm(values, gain):
    mean_val = jnp.mean(values, axis=-1, keepdims=True)
    centred = values - mean_val
    variance = jnp.mean(centred * centred, axis=-1, keepdims=True)
    return centred * lax.rsqrt(variance + norm_eps) * gain


def rotary_tables(positions, head_size):
    half_size = head_size // 2
    exponents = jnp.arange(half_size, dtype=jnp.float32) * (2.0 / head_size)
    inv_freq = 1.0 / theta_base**exponents
    angles = positions.astype(jnp.float32)[:, None] * inv_freq[None, :]
    cosine = jnp.cos(angles)
    sine = jnp.sin(angles)
    return (jnp.concatenate([cosine, cosine], -1), jnp.concatenate([sine, sine], -1))


def rotate(values, cosine, sine):
    half_size = values.shape[-1] // 2
    turned = jnp.concatenate([-values[..., half_size:], values[..., :half_size]], -1)
    return values * cosine[:, None, :] + turned * sine[:, None, :]


def fold_blocks(carry, pieces, piece_segments, work, rows):
    count = piece_segments.shape[0]
    size = math.gcd(count, 4 * rows)
    number = count // size
    blocks = tuple((part.reshape((number, size) + part.shape[1:]) for part in pieces))
    blocks = blocks + (piece_segments.reshape(number, size),)

    def step(acc, block):
        acc = work(acc, block)
        return (acc, None)

    carry, _ = lax.scan(step, carry, blocks)
    return carry


def on_device(hidden_in, grad_out, segment_ids, w_qkv, w_out, w_in, w_down, gain_attn, gain_mlp):
    rows = hidden_in.shape[1]
    local_seqs = hidden_in.shape[0]
    score_scale = HD ** (-0.5)
    bf16 = jnp.bfloat16
    f32 = jnp.float32
    gathered = (
        lax.all_gather(w_qkv.astype(bf16), "dp", axis=0, tiled=True),
        lax.all_gather(w_out.astype(bf16), "dp", axis=0, tiled=True),
        lax.all_gather(w_in.astype(bf16), "dp", axis=0, tiled=True),
        lax.all_gather(w_down.astype(bf16), "dp", axis=1, tiled=True),
        lax.all_gather(gain_attn.astype(bf16), "dp", axis=0, tiled=True),
        lax.all_gather(gain_mlp.astype(bf16), "dp", axis=0, tiled=True),
    )
    weight_qkv, weight_out, weight_in, weight_down, gain_low_a, gain_low_b = gathered
    gain_first = gain_low_a.astype(f32)
    gain_second = gain_low_b.astype(f32)
    whole_segments = lax.all_gather(segment_ids, "ctx", axis=1, tiled=True)
    positions = lax.axis_index("ctx") * rows + jnp.arange(rows, dtype=jnp.int32)
    cosine, sine = rotary_tables(positions, HD)

    def gated(values_in):
        return jax.nn.gelu(values_in[:, :FF], approximate=False) * values_in[:, FF:]

    def turn(pair):
        return (rotate(pair[0], cosine, sine), rotate(pair[1], cosine, sine))

    def one_sequence(seq_index):
        hidden = hidden_in[seq_index].astype(f32)
        own_segments = segment_ids[seq_index]
        all_segments = whole_segments[seq_index]
        normed_first, first_back = jax.vjp(layer_norm, hidden, gain_first)
        normed_attn = normed_first.astype(bf16)
        qkv = jnp.dot(normed_attn, weight_qkv, preferred_element_type=f32)
        q_lin = qkv[:, :D].reshape(rows, HEADS, HD)
        k_lin = qkv[:, D : 2 * D].reshape(rows, HEADS, HD)
        v_lin = qkv[:, 2 * D :].reshape(rows, HEADS, HD)
        turned, turn_back = jax.vjp(turn, (q_lin, k_lin))
        queries = turned[0].astype(bf16)
        keys = turned[1].astype(bf16)
        values = v_lin.astype(bf16)

        def forward_work(acc, block):
            key_blk, value_blk, seg_blk = block
            total, summed = acc
            scores = (
                jnp.einsum("thd,shd->hts", queries, key_blk, preferred_element_type=f32)
                * score_scale
            )
            same = own_segments[:, None] == seg_blk[None, :]
            expo = jnp.where(same[None], jnp.exp(scores), 0.0)
            total = total + jnp.sum(expo, axis=-1)
            summed = summed + jnp.einsum(
                "hts,shd->thd", expo.astype(bf16), value_blk, preferred_element_type=f32
            )
            return (total, summed)

        start_fwd = (jnp.zeros((HEADS, rows), f32), jnp.zeros((rows, HEADS, HD), f32))
        key_piece = lax.all_gather(keys.reshape(rows, D), "ctx", axis=0, tiled=True)
        value_piece = lax.all_gather(values.reshape(rows, D), "ctx", axis=0, tiled=True)
        count = key_piece.shape[0]
        piece_segments = all_segments
        parts = (key_piece.reshape(count, HEADS, HD), value_piece.reshape(count, HEADS, HD))
        total, summed = fold_blocks(start_fwd, parts, piece_segments, forward_work, rows)
        total_rows = jnp.transpose(total)
        attended = (summed / total_rows[:, :, None]).reshape(rows, D).astype(bf16)
        mixed = hidden + jnp.dot(attended, weight_out, preferred_element_type=f32)
        normed_second, second_back = jax.vjp(layer_norm, mixed, gain_second)
        normed_mlp = normed_second.astype(bf16)
        gate_up = jnp.dot(normed_mlp, weight_in, preferred_element_type=f32)
        activ_f, gated_back = jax.vjp(gated, gate_up)
        activ = activ_f.astype(bf16)
        layer_out = (mixed + jnp.dot(activ, weight_down, preferred_element_type=f32)).astype(bf16)
        grad_low = grad_out[seq_index]
        g_w_down = jnp.einsum("tf,td->fd", activ, grad_low, preferred_element_type=f32)
        g_activ = jnp.einsum("td,fd->tf", grad_low, weight_down, preferred_element_type=f32)
        g_gate_up = gated_back(g_activ)[0].astype(bf16)
        g_w_in = jnp.einsum("ti,tj->ij", normed_mlp, g_gate_up, preferred_element_type=f32)
        g_normed_mlp = jnp.einsum("tj,ij->ti", g_gate_up, weight_in, preferred_element_type=f32)
        g_mixed_norm, g_gain_mlp = second_back(g_normed_mlp)
        g_mixed = grad_low.astype(f32) + g_mixed_norm
        g_mixed_low = g_mixed.astype(bf16)
        g_w_out = jnp.einsum("ti,tj->ij", attended, g_mixed_low, preferred_element_type=f32)
        g_att = jnp.einsum(
            "tj,ij->ti", g_mixed_low, weight_out, preferred_element_type=f32
        ).reshape(rows, HEADS, HD)
        g_summed = (g_att / total_rows[:, :, None]).astype(bf16)
        row_term = jnp.sum(g_att * summed, axis=-1) / (total_rows * total_rows)
        own_rows = jnp.transpose(row_term)
        all_rows = lax.all_gather(row_term, "ctx", axis=0, tiled=True)

        def query_work(acc, block):
            key_blk, value_blk, seg_blk = block
            scores = (
                jnp.einsum("thd,shd->hts", queries, key_blk, preferred_element_type=f32)
                * score_scale
            )
            same = own_segments[:, None] == seg_blk[None, :]
            expo = jnp.where(same[None], jnp.exp(scores), 0.0)
            product = jnp.einsum("thd,shd->hts", g_summed, value_blk, preferred_element_type=f32)
            g_scores = (expo * (product - own_rows[:, :, None])).astype(bf16)
            return acc + jnp.einsum("hts,shd->thd", g_scores, key_blk, preferred_element_type=f32)

        key_piece = lax.all_gather(keys.reshape(rows, D), "ctx", axis=0, tiled=True)
        value_piece = lax.all_gather(values.reshape(rows, D), "ctx", axis=0, tiled=True)
        count = key_piece.shape[0]
        piece_segments = all_segments
        parts = (key_piece.reshape(count, HEADS, HD), value_piece.reshape(count, HEADS, HD))
        g_queries = (
            fold_blocks(jnp.zeros((rows, HEADS, HD), f32), parts, piece_segments, query_work, rows)
            * score_scale
        )

        def key_work(acc, block):
            query_blk, gsum_blk, row_blk, seg_blk = block
            g_keys, g_values = acc
            scores = (
                jnp.einsum("shd,thd->hst", query_blk, keys, preferred_element_type=f32)
                * score_scale
            )
            same = seg_blk[:, None] == own_segments[None, :]
            expo = jnp.where(same[None], jnp.exp(scores), 0.0)
            g_values = g_values + jnp.einsum(
                "hst,shd->thd", expo.astype(bf16), gsum_blk, preferred_element_type=f32
            )
            product = jnp.einsum("shd,thd->hst", gsum_blk, values, preferred_element_type=f32)
            g_scores = (expo * (product - jnp.transpose(row_blk)[:, :, None])).astype(bf16)
            g_keys = g_keys + jnp.einsum(
                "hst,shd->thd", g_scores, query_blk, preferred_element_type=f32
            )
            return (g_keys, g_values)

        start_keys = (jnp.zeros((rows, HEADS, HD), f32), jnp.zeros((rows, HEADS, HD), f32))
        query_piece = lax.all_gather(queries.reshape(rows, D), "ctx", axis=0, tiled=True)
        gsum_piece = lax.all_gather(g_summed.reshape(rows, D), "ctx", axis=0, tiled=True)
        count = query_piece.shape[0]
        piece_segments = all_segments
        parts = (
            query_piece.reshape(count, HEADS, HD),
            gsum_piece.reshape(count, HEADS, HD),
            all_rows,
        )
        g_keys, g_values = fold_blocks(start_keys, parts, piece_segments, key_work, rows)
        g_keys = g_keys * score_scale
        unturned = turn_back((g_queries, g_keys))[0]
        g_qkv = jnp.concatenate(
            [unturned[0].reshape(rows, D), unturned[1].reshape(rows, D), g_values.reshape(rows, D)],
            -1,
        ).astype(bf16)
        g_w_qkv = jnp.einsum("ti,tj->ij", normed_attn, g_qkv, preferred_element_type=f32)
        g_normed_attn = jnp.einsum("tj,ij->ti", g_qkv, weight_qkv, preferred_element_type=f32)
        g_hidden_norm, g_gain_attn = first_back(g_normed_attn)
        grad_in = (g_mixed + g_hidden_norm).astype(bf16)
        terms = (g_w_qkv, g_w_out, g_w_in, g_w_down, g_gain_attn, g_gain_mlp)
        return (layer_out, grad_in, terms)

    outputs_fwd = []
    outputs_back = []
    terms = None
    for seq_index in range(local_seqs):
        layer_out, grad_in, seq_terms = one_sequence(seq_index)
        outputs_fwd.append(layer_out)
        outputs_back.append(grad_in)
        if terms is None:
            terms = seq_terms
        else:
            terms = tuple((old + new for old, new in zip(terms, seq_terms)))
    everywhere = lax.psum(terms, "ctx")
    owned = (
        lax.psum_scatter(
            everywhere[0].astype(jnp.bfloat16), "dp", scatter_dimension=0, tiled=True
        ).astype(jnp.float32),
        lax.psum_scatter(
            everywhere[1].astype(jnp.bfloat16), "dp", scatter_dimension=0, tiled=True
        ).astype(jnp.float32),
        lax.psum_scatter(
            everywhere[2].astype(jnp.bfloat16), "dp", scatter_dimension=0, tiled=True
        ).astype(jnp.float32),
        lax.psum_scatter(
            everywhere[3].astype(jnp.bfloat16), "dp", scatter_dimension=1, tiled=True
        ).astype(jnp.float32),
        lax.psum_scatter(
            everywhere[4].astype(jnp.bfloat16), "dp", scatter_dimension=0, tiled=True
        ).astype(jnp.float32),
        lax.psum_scatter(
            everywhere[5].astype(jnp.bfloat16), "dp", scatter_dimension=0, tiled=True
        ).astype(jnp.float32),
    )
    return (
        jnp.stack(outputs_fwd),
        jnp.stack(outputs_back),
        owned[0],
        owned[1],
        owned[2],
        owned[3],
        owned[4],
        owned[5],
    )


HALF = 384
PIECE = 24


def send(values, mask):
    return lax.ppermute(values, ("dp", "ctx"), [(i, i ^ mask) for i in range(32)])


def send_swapped(values, mask):
    def target(i):
        core, high = (i >> 3) & 1, (i >> 2) & 1
        return (i & ~12) | (high << 3) | (core << 2)

    return lax.ppermute(values, ("dp", "ctx"), [(i, target(i) ^ mask) for i in range(32)])


def pick(flag, first, second):
    return jnp.where(flag == 0, first, second)


VM = pl.BlockSpec(memory_space=pltpu.VMEM)
SM = pl.BlockSpec(memory_space=pltpu.SMEM)


def pieces_of(me, near_ref, far_ref):
    for slot, mask in enumerate(XZ):
        start = pl.multiple_of((me % 8 ^ mask) * PIECE, 8)
        yield start, (near_ref, far_ref)[slot // 4][slot % 4].astype(jnp.float32)


def qkv_result_kernel(me_ref, near_ref, far_ref, out_ref, gains_ref, buffer_ref):
    me = me_ref[0]
    core = (me // 8) % 2
    wide = 3 * HALF + 128
    for start, piece in pieces_of(me, near_ref, far_ref):
        rows = pl.ds(start, PIECE)
        for half in range(2):
            for t in range(3):
                column = pl.multiple_of(t * D + (half ^ core) * HALF, 128)
                first = half * wide + t * HALF
                out_ref[rows, pl.ds(column, HALF)] = piece[:, first : first + HALF]
        buffer_ref[rows, :] = piece[:, 3 * HALF : wide] + piece[:, wide + 3 * HALF :]
    gains_ref[...] = buffer_ref[...].T[:8, :192]


def mlp_result_kernel(
    me_ref, near_1, far_1, near_2, far_2, w_in_ref, w_out_ref, w_down_ref
):
    me = me_ref[0]
    for start, piece in pieces_of(me, near_1, far_1):
        rows = pl.ds(start, PIECE)
        w_in_ref[rows, :768] = piece[:, :768]
        w_in_ref[rows, FF : FF + 768] = piece[:, 768:1536]
        w_down_ref[rows, :768] = piece[:, 1536:]
    for start, piece in pieces_of(me, near_2, far_2):
        rows = pl.ds(start, PIECE)
        w_in_ref[rows, 768:FF] = piece[:, :384]
        w_in_ref[rows, FF + 768 :] = piece[:, 384:768]
        w_out_ref[rows, :384] = piece[:, 768:1152]
        w_out_ref[rows, 384:] = piece[:, 1536:]
        w_down_ref[rows, 768:] = piece[:, 1152:1536]


def plus(first, second):
    return (first.astype(jnp.float32) + second.astype(jnp.float32)).astype(jnp.bfloat16)


def finish(body, me, pieces, shapes, scratch, name):
    return pl.pallas_call(
        body,
        out_shape=tuple(jax.ShapeDtypeStruct(shape, jnp.float32) for shape in shapes),
        in_specs=[SM] + [VM] * len(pieces),
        out_specs=(VM,) * len(shapes),
        scratch_shapes=[pltpu.VMEM(scratch, jnp.float32)] if scratch else [],
        compiler_params=pltpu.CompilerParams(vmem_limit_bytes=24 << 20),
        name=name,
    )(me, *pieces)


XZ = [dx | (dz << 1) for dx in range(2) for dz in range(4)]


def masks(*bits):
    order = [0]
    for bit in bits:
        choices = (0, bit) if bit != 6 else (0, 2, 4, 6)
        order = [m | choice for m in order for choice in choices]
    return order


def after(values, *others):
    return lax.optimization_barrier((values,) + others)[0]


def stage(*values):
    return lax.optimization_barrier(values)


def norm_parts(values):
    mean_val = jnp.mean(values, axis=-1, keepdims=True)
    centred = values - mean_val
    variance = jnp.mean(centred * centred, axis=-1, keepdims=True)
    scale = lax.rsqrt(variance + norm_eps)
    return centred * scale, scale


def norm_back(xhat, scale, grad, gain):
    e = grad * gain
    return scale * (
        e
        - jnp.mean(e, axis=-1, keepdims=True)
        - xhat * jnp.mean(e * xhat, axis=-1, keepdims=True)
    )


NT = (((1,), (1,)), ((), ()))
FAR_APART = -1.0e30
MEGA = 1 << 20


def matmul(first, second, dims=None):
    dims = dims or (((1,), (0,)), ((), ()))
    return lax.dot_general(first, second, dims, preferred_element_type=jnp.float32)


def kernel_call(body, outs, scratch, name, flops, moved):
    count = len(outs)
    return lambda *args: pl.pallas_call(
        body,
        out_shape=tuple(jax.ShapeDtypeStruct(shape, kind) for shape, kind in outs),
        in_specs=[SM] + [VM] * (len(args) - 1),
        out_specs=(VM,) * count,
        scratch_shapes=[pltpu.VMEM(shape, kind) for shape, kind in scratch],
        compiler_params=pltpu.CompilerParams(vmem_limit_bytes=32 * MEGA),
        cost_estimate=pl.CostEstimate(flops=flops, bytes_accessed=moved, transcendentals=0),
        name=name,
    )(*args)


def swap_halves(pair):
    lane = lax.broadcasted_iota(jnp.int32, pair.shape, 1) % HD
    return jnp.where(lane < HD // 2, pltpu.roll(pair, 96, 1), pltpu.roll(pair, 32, 1))


def place_rows(me, pieces, whole_ref):
    for mask, piece in pieces:
        start = pl.multiple_of((me // 8 ^ mask) * 192, 16)
        whole_ref[pl.ds(start, 192), :] = piece


def attention_kernel(
    me_ref,
    own_ref,
    across_ref,
    peer_ref,
    beyond_ref,
    mine_ref,
    core_ref,
    up_ref,
    both_ref,
    cos_ref,
    sin_ref,
    normed_ref,
    q_ref,
    k_ref,
    v_ref,
    probs_ref,
    att_own_ref,
    att_peer_ref,
    att_ref,
    inv_ref,
    weight_ref,
    gains_ref,
    q_id_ref,
    keys_ref,
    values_ref,
):
    f32, bf16 = jnp.float32, jnp.bfloat16
    me = me_ref[0]
    shards = (mine_ref, core_ref, up_ref, both_ref)
    place_rows(me, [(mask, ref[:192, :]) for mask, ref in enumerate(shards)], weight_ref)
    gains = sum(ref[192:200, :].astype(f32) for ref in shards)[:, :D]
    gains_ref[...] = gains
    gain = gains[0:1, :]
    row_id = lax.broadcasted_iota(jnp.int32, (128, 128), 0).astype(f32)
    blocks = [own_ref.at[i] for i in range(2)] + [peer_ref.at[i] for i in range(2)]
    blocks += [across_ref.at[i] for i in range(2)] + [beyond_ref.at[i] for i in range(2)]
    for i, block in enumerate(blocks):
        rows = slice(128 * i, 128 * (i + 1))
        hidden = block[:128, :].astype(f32)
        centred = hidden - jnp.mean(hidden, axis=1, keepdims=True)
        variance = jnp.mean(centred * centred, axis=1, keepdims=True)
        normed = (centred * lax.rsqrt(variance + norm_eps) * gain).astype(bf16)
        normed_ref[rows, :] = normed
        ids = block[128:136, :128].astype(f32)[0:1, :]
        hit = jnp.where(row_id == ids, 1.0, 0.0).T
        keys_ref[rows, 128:] = (1.0 - hit).astype(bf16)
        values_ref[rows, 128:] = jnp.ones((128, 128), bf16)
        if i < 4:
            q_id_ref[rows, :] = (hit * FAR_APART).astype(bf16)

    for i in range(4):
        rows = slice(256 * i, 256 * (i + 1))
        normed = normed_ref[rows, :]
        first = 0 if i < 2 else HALF
        qkv = matmul(normed, weight_ref[:, first:])
        for j in range(first // 128, 9):
            part = qkv[:, 128 * j - first : 128 * j - first + 128]
            columns = slice(128 * (j % 3), 128 * (j % 3) + 128)
            if j < 6:
                part = part * cos_ref[rows, :] + swap_halves(part) * sin_ref[rows, :]
            if j < 3:
                q_ref[rows, columns] = (part * HD**-0.5).astype(bf16)
            elif j < 6:
                k_ref[rows, columns] = part.astype(bf16)
            else:
                v_ref[rows, columns] = part.astype(bf16)

    low_head = lax.broadcasted_iota(jnp.int32, (256, 128), 1) < HD
    for pair in range(3):
        columns = slice(128 * pair, 128 * pair + 128)
        keys_ref[:, :128] = k_ref[:, columns]
        values_ref[:, :128] = v_ref[:, columns]
        for i in range(2):
            rows = slice(256 * i, 256 * (i + 1))
            queries = q_ref[rows, columns]
            found = []
            for head in range(2):
                picked = jnp.where(low_head == (head == 0), queries, jnp.zeros_like(queries))
                scores = matmul(
                    jnp.concatenate([picked, q_id_ref[rows, :]], 1), keys_ref[...], NT
                )
                probs = jnp.exp(scores).astype(bf16)
                probs_ref[2 * pair + head, rows, :] = probs
                found.append(matmul(probs, values_ref[...]))
            inverse = 1.0 / jnp.where(low_head, found[0][:, 128:], found[1][:, 128:])
            attended = jnp.where(low_head, found[0][:, :128], found[1][:, :128]) * inverse
            inv_ref[rows, columns] = inverse
            att_ref[rows, columns] = attended
            out_ref = att_own_ref if i == 0 else att_peer_ref
            out_ref[:, columns] = attended.astype(bf16)


def attention_forward(*args):
    f32, bf16 = jnp.float32, jnp.bfloat16
    outs = [
        ((1024, D), bf16),
        ((512, HALF), bf16),
        ((1024, HALF), bf16),
        ((1024, HALF), bf16),
        ((6, 512, 1024), bf16),
        ((256, HALF), bf16),
        ((256, HALF), bf16),
        ((512, HALF), f32),
        ((512, HALF), f32),
        ((D, 3 * HALF), bf16),
        ((8, D), f32),
    ]
    scratch = [((512, 128), bf16), ((1024, 256), bf16), ((1024, 256), bf16)]
    return kernel_call(attention_kernel, outs, scratch, "attention_fwd", 4 * 10**9, 8 * MEGA)(*args)


def put_pieces(me, order, values_ref, out_ref, columns):
    for slot, mask in enumerate(order):
        start = pl.multiple_of((me ^ mask) * PIECE, 8)
        out_ref[slot, :, columns] = values_ref[pl.ds(start, PIECE), :].astype(out_ref.dtype)


def gated_block(normed, grad, gate_rows, upper_rows, down_rows):
    bf16 = jnp.bfloat16
    gate = matmul(normed, gate_rows)
    upper = matmul(normed, upper_rows)
    chance = 0.5 + 0.5 * lax.erf(gate * math.sqrt(0.5))
    bell = jnp.exp(-0.5 * gate * gate) * (1.0 / math.sqrt(2.0 * math.pi))
    gelu = gate * chance
    g_activ = matmul(grad, down_rows)
    g_gate = (g_activ * upper * (chance + gate * bell)).astype(bf16)
    g_upper = (g_activ * gelu).astype(bf16)
    return (gelu * upper).astype(bf16), g_gate, g_upper


WIDTH = 384


def mlp_first_kernel(
    me_ref,
    own_ref,
    att_ref,
    att_peer_ref,
    grad_ref,
    gains_ref,
    shard_ref,
    core_ref,
    up_ref,
    both_ref,
    down_ref,
    g_normed_ref,
    xhat_ref,
    scale_ref,
    w_out_ref,
    away_ref,
    stay_ref,
    w_ref,
    buffer_ref,
):
    f32, bf16 = jnp.float32, jnp.bfloat16
    me = me_ref[0]
    core = (me // 8) % 2
    shards = (shard_ref, core_ref, up_ref, both_ref)
    for mask, ref in enumerate(shards):
        shard = me // 8 ^ mask
        head_row = (shard // 2 ^ core) * HALF + (shard % 2) * 192
        w_out_ref[pl.ds(pl.multiple_of(head_row, 16), 192), :] = ref[:, :D]
    place_rows(me, [(mask, ref[:, D:]) for mask, ref in enumerate(shards)], w_ref)

    attended = jnp.concatenate([att_ref[...], att_peer_ref[...]], 1)
    hidden = jnp.concatenate([own_ref[0, :128, :], own_ref[1, :128, :]]).astype(f32)
    mixed = hidden + matmul(attended, w_out_ref[...])
    centred = mixed - jnp.mean(mixed, axis=1, keepdims=True)
    scale = lax.rsqrt(jnp.mean(centred * centred, axis=1, keepdims=True) + norm_eps)
    xhat = centred * scale
    xhat_ref[...] = xhat
    scale_ref[...] = jnp.broadcast_to(scale, (256, 128))
    normed = (xhat * gains_ref[1:2, :]).astype(bf16)
    grad = grad_ref[...]
    normed_t, grad_t = normed.T, grad.T
    orders = masks(16, 1, 6), masks(1, 16, 6)

    def emit(values, late, first):
        buffer_ref[...] = values
        columns = pl.ds(pl.multiple_of(first, 128), WIDTH)
        for slot, (early_mask, late_mask) in enumerate(zip(*orders)):
            mask = early_mask + late * (late_mask - early_mask)
            for ref, core_mask in ((away_ref, 8), (stay_ref, 0)):
                start = pl.multiple_of((me ^ (mask + core_mask)) * PIECE, 8)
                ref[slot, :, columns] = buffer_ref[pl.ds(start, PIECE), :].astype(bf16)

    down_ref[...] = mixed
    g_normed_ref[...] = jnp.zeros_like(mixed)

    def block(i, carry):
        low, high, last = (
            w_ref[:, pl.ds(pl.multiple_of(first + WIDTH * i, 128), WIDTH)]
            for first in (0, 768, 1536)
        )
        activ, g_gate, g_upper = gated_block(normed, grad, low, high, last)
        down_ref[...] += matmul(activ, last, NT)
        g_normed_ref[...] += matmul(g_gate, low, NT) + matmul(g_upper, high, NT)
        emit(matmul(normed_t, g_gate), 0, WIDTH * i)
        emit(matmul(normed_t, g_upper), i, 768 + WIDTH * i)
        emit(matmul(grad_t, activ), 1, 1536 + WIDTH * i)
        return carry

    lax.fori_loop(0, 2, block, 0)


def mlp_first(*args):
    f32, bf16 = jnp.float32, jnp.bfloat16
    outs = [
        ((256, D), f32),
        ((256, D), f32),
        ((256, D), f32),
        ((256, 128), f32),
        ((D, D), bf16),
        ((16, PIECE, 6 * WIDTH), bf16),
        ((16, PIECE, 6 * WIDTH), bf16),
    ]
    scratch = [((D, 6 * WIDTH), bf16), ((D, WIDTH), f32)]
    return kernel_call(mlp_first_kernel, outs, scratch, "mlp_first", 3 * 10**9, 16 * MEGA)(*args)


def mlp_second_kernel(
    me_ref,
    att_ref,
    att_peer_ref,
    grad_ref,
    gains_ref,
    shard_ref,
    core_ref,
    up_ref,
    both_ref,
    down_ref,
    g_normed_ref,
    xhat_ref,
    scale_ref,
    w_out_ref,
    out_ref,
    g_mixed_ref,
    g_att_ref,
    g_att_peer_ref,
    away_ref,
    stay_ref,
    g_gain_ref,
    w_ref,
    buffer_ref,
):
    f32, bf16 = jnp.float32, jnp.bfloat16
    me = me_ref[0]
    core = (me // 8) % 2
    shards = (shard_ref, core_ref, up_ref, both_ref)
    place_rows(me, [(mask, ref[...]) for mask, ref in enumerate(shards)], w_ref)
    gain = gains_ref[1:2, :]
    xhat = xhat_ref[...]
    scale = scale_ref[:, 0:1]
    normed = (xhat * gain).astype(bf16)
    grad = grad_ref[...]
    normed_t, grad_t = normed.T, grad.T
    y_first, x_first = masks(16, 1, 6), masks(1, 16, 6)

    def emit(order, first):
        columns = slice(first, first + WIDTH)
        put_pieces(me, [m | 8 for m in order], buffer_ref, away_ref, columns)
        put_pieces(me, order, buffer_ref, stay_ref, columns)

    low, high, last = (slice(first, first + WIDTH) for first in (0, 384, 768))
    activ, g_gate, g_upper = gated_block(normed, grad, w_ref[:, low], w_ref[:, high], w_ref[:, last])
    g_normed = g_normed_ref[...] + matmul(g_gate, w_ref[:, low], NT)
    g_normed = g_normed + matmul(g_upper, w_ref[:, high], NT)
    e = g_normed * gain
    g_mixed = grad.astype(f32) + scale * (
        e
        - jnp.mean(e, axis=1, keepdims=True)
        - xhat * jnp.mean(e * xhat, axis=1, keepdims=True)
    )
    g_mixed_ref[...] = g_mixed
    g_low = g_mixed.astype(bf16)
    g_att = matmul(g_low, w_out_ref[...], NT).astype(bf16)
    g_att_ref[...] = g_att[:, :HALF]
    g_att_peer_ref[...] = g_att[:, HALF:]
    out_ref[...] = (down_ref[...] + matmul(activ, w_ref[:, last], NT)).astype(bf16)
    g_gain = jnp.broadcast_to(jnp.sum(xhat * g_normed, axis=0, keepdims=True), (128, D))
    row = lax.broadcasted_iota(jnp.int32, (128, D), 0)
    g_gain_ref[...] = jnp.where(row == 1, g_gain, 0.0).T
    buffer_ref[...] = matmul(normed_t, g_gate)
    emit(y_first, 0)
    buffer_ref[...] = matmul(normed_t, g_upper)
    emit(y_first, WIDTH)
    buffer_ref[...] = matmul(grad_t, activ)
    emit(x_first, 3 * WIDTH)
    attended_t = jnp.concatenate([att_ref[...], att_peer_ref[...]], 1).T
    for i in range(2):
        rows_out = matmul(attended_t, g_low[:, WIDTH * i : WIDTH * (i + 1)])
        for half in range(2):
            start = pl.multiple_of((half ^ core) * HALF, HALF)
            buffer_ref[pl.ds(start, HALF), :] = rows_out[HALF * half : HALF * (half + 1), :]
        emit(y_first if i == 0 else x_first, (2 + 2 * i) * WIDTH)


def mlp_second(*args):
    f32, bf16 = jnp.float32, jnp.bfloat16
    outs = [
        ((256, D), bf16),
        ((256, D), f32),
        ((256, HALF), bf16),
        ((256, HALF), bf16),
        ((16, PIECE, 5 * WIDTH), bf16),
        ((16, PIECE, 5 * WIDTH), bf16),
        ((D, 128), f32),
    ]
    scratch = [((D, 3 * WIDTH), bf16), ((D, WIDTH), f32)]
    return kernel_call(mlp_second_kernel, outs, scratch, "mlp_second", 2 * 10**9, 10 * MEGA)(*args)


def attention_back_kernel(
    me_ref,
    g_own_ref,
    g_peer_ref,
    att_ref,
    inv_ref,
    q_ref,
    k_ref,
    v_ref,
    probs_ref,
    cos_ref,
    sin_ref,
    dq_ref,
    dk_ref,
    dv_ref,
    values_ref,
):
    f32, bf16 = jnp.float32, jnp.bfloat16
    low_head = lax.broadcasted_iota(jnp.int32, (1024, 128), 1) < HD
    lane = lax.broadcasted_iota(jnp.int32, (512, 128), 1)
    values_ref[:, 128:] = jnp.ones((1024, 128), bf16)
    for pair in range(3):
        columns = slice(128 * pair, 128 * pair + 128)
        values_ref[:, :128] = v_ref[:, columns]
        queries_t, keys = q_ref[:, columns].T, k_ref[:, columns]
        grad = jnp.concatenate([g_own_ref[:, columns], g_peer_ref[:, columns]]).astype(f32)
        grad = grad * inv_ref[:, columns]
        terms = grad * att_ref[:, columns]
        grad = grad.astype(bf16)
        grad_t = grad.T
        g_queries = jnp.zeros((512, 128), f32)
        g_keys, g_values = [], []
        for head in range(2):
            mine = low_head == (head == 0)
            rows = slice(HD * head, HD * head + HD)
            row = jnp.sum(jnp.where(mine[:512], terms, 0.0), axis=1, keepdims=True)
            high = row.astype(bf16)
            middle = (row - high.astype(f32)).astype(bf16)
            rest = (row - high.astype(f32) - middle.astype(f32)).astype(bf16)
            extra = jnp.where(lane == 0, -high.astype(f32), 0.0)
            extra = jnp.where(lane == 1, -middle.astype(f32), extra)
            extra = jnp.where(lane == 2, -rest.astype(f32), extra).astype(bf16)
            picked = jnp.where(mine[:512], grad, jnp.zeros_like(grad))
            product = matmul(jnp.concatenate([picked, extra], 1), values_ref[...], NT)
            probs = probs_ref[2 * pair + head]
            g_scores = (probs.astype(f32) * product).astype(bf16)
            g_queries = g_queries + matmul(g_scores, jnp.where(mine, keys, jnp.zeros_like(keys)))
            g_keys.append(matmul(queries_t[rows, :], g_scores))
            g_values.append(matmul(grad_t[rows, :], probs))
        g_queries = g_queries * HD**-0.5
        near = slice(0, 512)
        dq_ref[:, columns] = (
            g_queries * cos_ref[near, :] - swap_halves(g_queries) * sin_ref[near, :]
        ).astype(bf16)
        g_keys = jnp.concatenate(g_keys).T
        dk_ref[:, columns] = (
            g_keys * cos_ref[...] - swap_halves(g_keys) * sin_ref[...]
        ).astype(bf16)
        dv_ref[:, columns] = jnp.concatenate(g_values).T.astype(bf16)


def attention_backward(*args):
    bf16 = jnp.bfloat16
    outs = [((512, HALF), bf16), ((1024, HALF), bf16), ((1024, HALF), bf16)]
    scratch = [((1024, 256), bf16)]
    return kernel_call(
        attention_back_kernel, outs, scratch, "attention_bwd", 5 * 10**9, 10 * MEGA
    )(*args)


def qkv_weight_kernel(
    me_ref,
    normed_ref,
    weight_ref,
    g_gain_ref,
    dq_ref,
    dk_ref,
    dv_ref,
    keep_a,
    away_a,
    peer_b,
    buffer_ref,
):
    me = me_ref[0]
    order_a, order_b = masks(1, 6), masks(1, 16, 6)
    normed_t = normed_ref[...].T

    def emit(values_ref, columns):
        put_pieces(me, order_a, values_ref, keep_a, columns)
        put_pieces(me, [m | 16 for m in order_a], values_ref, away_a, columns)
        put_pieces(me, [m | 8 for m in order_b], values_ref, peer_b, columns)

    g_gain = jnp.zeros((D, 1), jnp.float32)
    for i, ref in enumerate((dq_ref, dk_ref, dv_ref)):
        columns = slice(HALF * i, HALF * (i + 1))
        values = matmul(normed_t[:, : ref.shape[0]], ref[...])
        weight = weight_ref[:, columns].astype(jnp.float32)
        g_gain = g_gain + jnp.sum(values * weight, axis=1, keepdims=True)
        buffer_ref[...] = values
        emit(buffer_ref, columns)
    lane = lax.broadcasted_iota(jnp.int32, (D, 128), 1)
    buffer_ref[:, :128] = jnp.where(lane == 0, g_gain, g_gain_ref[...])
    emit(buffer_ref.at[:, :128], slice(3 * HALF, 3 * HALF + 128))


def qkv_weight_gradient(*args):
    outs = [((count, PIECE, 3 * HALF + 128), jnp.bfloat16) for count in (8, 8, 16)]
    scratch = [((D, HALF), jnp.float32)]
    return kernel_call(qkv_weight_kernel, outs, scratch, "qkv_weights", 2 * 10**9, 8 * MEGA)(*args)


def qkv_input_kernel(me_ref, weight_ref, dq_ref, dk_ref, dv_ref, own_ref, across_ref, peer_ref):
    targets = (own_ref, peer_ref.at[0], across_ref, peer_ref.at[1])
    for i, target in enumerate(targets):
        rows = slice(256 * i, 256 * (i + 1))
        grad = matmul(dk_ref[rows, :], weight_ref[:, HALF : 2 * HALF], NT)
        grad = grad + matmul(dv_ref[rows, :], weight_ref[:, 2 * HALF :], NT)
        if i < 2:
            grad = grad + matmul(dq_ref[rows, :], weight_ref[:, :HALF], NT)
        target[...] = grad.astype(target.dtype)


def qkv_input_gradient(*args):
    bf16 = jnp.bfloat16
    outs = [((256, D), bf16), ((256, D), bf16), ((2, 256, D), bf16)]
    return kernel_call(qkv_input_kernel, outs, [], "qkv_inputs", 2 * 10**9, 6 * MEGA)(*args)


def paired_chips(hidden_in, grad_out, segment_ids, w_qkv, w_out, w_in, w_down, gain_attn, gain_mlp):
    bf16, f32 = jnp.bfloat16, jnp.float32
    dp, ctx = lax.axis_index("dp"), lax.axis_index("ctx")
    me = dp * 8 + ctx
    me_ref = me.reshape(1).astype(jnp.int32)
    c, zl, x = dp % 2, (ctx // 2) % 2, ctx % 2
    rows = hidden_in.shape[1]

    def to_chips(values):
        return (
            send_swapped(pick(zl, values[0], values[1]), 0),
            send_swapped(pick(zl, values[1], values[0]), 2),
        )

    def from_chips(values):
        block_a, block_b = send_swapped(values[:rows], 0), send_swapped(values[rows:], 2)
        return jnp.stack([pick(zl, block_a, block_b), pick(zl, block_b, block_a)])

    ids = jnp.pad(segment_ids[:, None, :], ((0, 0), (0, 7), (0, D - rows))).astype(bf16)
    packed = [pick(zl, a, b) for a, b in ((hidden_in, hidden_in[::-1]), (ids, ids[::-1]))]
    packed = jnp.concatenate(packed, 1)

    gains = lax.dynamic_update_slice(
        jnp.zeros((8, 3 * HALF), f32), jnp.stack([gain_attn, gain_mlp]), (0, 192 * dp)
    )

    def my_columns(core):
        columns = [lax.dynamic_slice_in_dim(w_qkv, t * D + core * HALF, HALF, 1) for t in range(3)]
        return jnp.concatenate([jnp.concatenate(columns, 1), gains]).astype(bf16)

    within = jnp.arange(rows, dtype=jnp.int32)
    starts = []
    for far in range(2):
        for core in range(2):
            for low in range(2):
                starts.append((2 * (2 * (c ^ core) + (zl ^ low)) + (x ^ far)) * rows + within)
    cosine, sine = rotary_tables(jnp.concatenate(starts), HD)
    sine = sine * jnp.where(jnp.arange(HD) < HD // 2, -1.0, 1.0)
    cosine, sine = jnp.concatenate([cosine] * 2, 1), jnp.concatenate([sine] * 2, 1)

    mine, other, packed = stage(my_columns(c), my_columns(1 - c), packed)
    own = jnp.stack([send_swapped(packed[0], 0), send_swapped(packed[1], 2)])
    up, up_other = send(mine, 16), send(other, 16)
    by_core = send(other, 8)
    w_down = w_down.T
    cut, rest = slice(0, 768), slice(768, FF)
    late = slice(FF + 768, None)
    first = jnp.concatenate([w_out, w_in[:, cut], w_in[:, FF : FF + 768], w_down[:, cut]], 1)
    second = jnp.concatenate([w_in[:, rest], w_in[:, late], w_down[:, rest]], 1)
    own, by_core, first, second = stage(own, by_core, first.astype(bf16), second.astype(bf16))
    up_first, up_second = send(first, 16), send(second, 16)
    across, peer = send(own, 1), send(own, 8)
    across, peer, up, up_other, cosine, sine = stage(across, peer, up, up_other, cosine, sine)
    by_both, beyond = send(up_other, 8), send(across, 8)
    grad_low = to_chips(after(grad_out, across))

    normed, queries, keys, values, probs, att_own, att_peer, att, inverse, weight, gains = (
        attention_forward(
            *(me_ref, own, across, peer, beyond),
            *(mine, by_core, up, by_both, cosine, sine),
        )
    )
    grad_a, grad_b, att_peer, first = stage(*grad_low, att_peer, first)
    grad_low = jnp.concatenate([grad_a, grad_b])
    att_peer = send(att_peer, 8)
    core_first = send(first, 8)
    core_second = send(after(second, grad_low), 8)
    up_first, att_peer = stage(up_first, att_peer)
    both_first = send(up_first, 8)
    down, g_norm, xhat, scale, w_out, away_1, stay_1 = mlp_first(
        me_ref, own, att_own, att_peer, grad_low, gains, first, core_first, up_first, both_first
    )
    away_1, up_second, core_second = stage(away_1, up_second, core_second)
    both_second = send(up_second, 8)

    def halves(values, got):
        count = values.shape[0] // 2
        return [
            plus(values[part, :, columns], got[part, :, columns])
            for columns in (slice(0, 3 * WIDTH), slice(3 * WIDTH, None))
            for part in (slice(0, count), slice(count, None))
        ]

    def fold(stay, got):
        return plus(stay[:4], got[:4]), plus(stay[4:], got[4:])

    def fold_near(part):
        return jnp.stack([part[0], part[2]]), jnp.stack([part[1], part[3]])

    def joined(stay_a, got_a, stay_b, got_b):
        return fold_near(jnp.concatenate([plus(stay_a, got_a), plus(stay_b, got_b)], 2))

    got_1 = send(away_1, 8)
    both_second, down = stage(both_second, down)
    layer_out, g_mixed, g_att, g_att_peer, away_2, stay_2, g_gain = mlp_second(
        me_ref,
        *(att_own, att_peer, grad_low, gains),
        *(second, core_second, up_second, both_second),
        *(down, g_norm, xhat, scale, w_out),
    )
    got_1, away_2, g_att_peer, layer_out = stage(got_1, away_2, g_att_peer, layer_out)
    g_att_peer = send(g_att_peer, 8)
    got_2 = send(away_2, 8)
    stay_1a, leave_a, stay_1b, leave_b = halves(stay_1, got_1)
    got_1a, got_1b = send(leave_a, 16), send(leave_b, 1)
    g_att_peer, layer_out = stage(g_att_peer, layer_out)
    layer_out = from_chips(layer_out)
    grads = attention_backward(
        me_ref, g_att, g_att_peer, att, inverse, queries, keys, values, probs, cosine, sine
    )
    got_1a, got_1b, got_2, layer_out, *grads = stage(got_1a, got_1b, got_2, layer_out, *grads)

    stay_1a, leave_1a = fold(stay_1a, got_1a)
    stay_1b, leave_1b = fold(stay_1b, got_1b)
    got_1a, got_1b = send(leave_1a, 1), send(leave_1b, 16)
    stay_2a, leave_a, stay_2b, leave_b = halves(stay_2, got_2)
    got_2a, got_2b = send(leave_a, 16), send(leave_b, 1)
    g_gain, *_ = stage(g_gain, leave_1a, leave_1b, leave_a, leave_b)
    keep_a, away_a, peer_b = qkv_weight_gradient(me_ref, normed, weight, g_gain, *grads)

    got_1a, got_1b, away_a, peer_b, *grads = stage(got_1a, got_1b, away_a, peer_b, *grads)
    got_core, got_a = send(peer_b, 8), send(away_a, 16)
    keep_1, leave_1 = joined(stay_1a, got_1a, stay_1b, got_1b)
    got_1 = send(leave_1, 2)
    weight, _ = stage(weight, leave_1)
    near, across, peer = qkv_input_gradient(me_ref, weight, *grads)

    got_core, near, across, peer = stage(got_core, near, across, peer)
    keep_b, away_b = got_core[:8], got_core[8:]
    got_b = send(away_b, 1)
    peer = send(peer, 8)
    got_2a, got_2b, got_1, _ = stage(got_2a, got_2b, got_1, away_b)
    stay_2a, leave_2a = fold(stay_2a, got_2a)
    stay_2b, leave_2b = fold(stay_2b, got_2b)
    got_2a, got_2b = send(leave_2a, 1), send(leave_2b, 16)
    keep_1 = plus(keep_1, got_1)
    peer, keep_1, *_ = stage(peer, keep_1, leave_2a, leave_2b)
    got_1 = send(keep_1[1], 4)
    across = plus(across, peer[1])
    got_a, got_b, across, _ = stage(got_a, got_b, across, keep_1)

    stay_a, leave_a = fold(keep_a, got_a)
    stay_b, leave_b = fold(keep_b, got_b)
    got_a, got_b = send(leave_a, 1), send(leave_b, 16)
    got_1, got_2a, got_2b, across, *_ = stage(got_1, got_2a, got_2b, across, leave_a, leave_b)
    sum_1 = plus(keep_1[0], got_1)
    far_1 = send(sum_1, 4)
    keep_2, leave_2 = joined(stay_2a, got_2a, stay_2b, got_2b)
    got_2 = send(leave_2, 2)
    got_across = send(across, 1)
    got_a, got_b, *_ = stage(got_a, got_b, sum_1, leave_2, across)

    total = jnp.concatenate([plus(stay_a, got_a), plus(stay_b, got_b)], 2)
    got = [send(total[dz], 2 * dz) for dz in range(1, 4)]
    far_1, got_2, got_across, _ = stage(far_1, got_2, got_across, total)
    sum_1 = jnp.stack([sum_1, far_1])
    far_1 = send(sum_1, 2)
    keep_2 = plus(keep_2, got_2)
    got_2 = send(keep_2[1], 4)
    g_normed = plus(near, peer[0]).astype(f32) + got_across.astype(f32)
    xhat, scale = norm_parts(own[:, :rows].reshape(2 * rows, D).astype(f32))
    grad_in = (g_mixed + norm_back(xhat, scale, g_normed, gains[0])).astype(bf16)
    grad_in, _, _, *got = stage(grad_in, sum_1, keep_2, *got)

    total = sum((part.astype(f32) for part in got), total[0].astype(f32)).astype(bf16)
    got = [send(total, 2 * dz) for dz in range(1, 4)]
    far_1, got_2, _ = stage(far_1, got_2, total)
    sum_1 = jnp.stack([sum_1, far_1], 1).reshape(4, PIECE, -1)
    far_1 = send(sum_1, 1)
    sum_2 = plus(keep_2[0], got_2)
    far_2 = send(sum_2, 4)
    far_2, total, *got = stage(far_2, total, *got)
    total = jnp.stack([total, *got])
    far = send(total, 1)
    sum_2 = jnp.stack([sum_2, far_2])
    far_2 = send(sum_2, 2)
    grad_in, far_1, _ = stage(grad_in, far_1, total)
    grad_in = from_chips(grad_in)
    far_2, total = stage(far_2, total)
    sum_2 = jnp.stack([sum_2, far_2], 1).reshape(4, PIECE, -1)
    far_2 = send(sum_2, 1)
    g_w_qkv, g_gains = finish(
        qkv_result_kernel, me_ref, (total, far), ((192, 3 * D), (8, 192)), (256, 128), "qkv_result"
    )
    g_w_in, g_w_out, g_w_down = finish(
        mlp_result_kernel,
        me_ref,
        (sum_1, far_1, sum_2, far_2),
        ((192, 2 * FF), (192, D), (192, FF)),
        None,
        "mlp_result",
    )
    g_gain_attn = g_gains[0] / gain_attn.astype(bf16).astype(f32)
    return (layer_out, grad_in, g_w_qkv, g_w_out, g_w_in, g_w_down.T, g_gain_attn, g_gains[1])


def solution(mesh):
    whole_fit = mesh.shape["dp"] == 4 and mesh.shape["ctx"] == 8
    return jax.shard_map(
        paired_chips if whole_fit else on_device,
        mesh=mesh,
        in_specs=(
            P("dp", "ctx", None),
            P("dp", "ctx", None),
            P("dp", "ctx"),
            P("dp", None),
            P("dp", None),
            P("dp", None),
            P(None, "dp"),
            P("dp"),
            P("dp"),
        ),
        out_specs=(
            P("dp", "ctx", None),
            P("dp", "ctx", None),
            P("dp", None),
            P("dp", None),
            P("dp", None),
            P(None, "dp"),
            P("dp"),
            P("dp"),
        ),
        check_vma=False,
    )
```

```python
import math

import jax
import jax.numpy as jnp
from jax import lax
from jax.experimental import pallas as pl
from jax.experimental.pallas import tpu as pltpu
from jax.sharding import PartitionSpec as P

D = 768
HEADS = 12
HD = 64
FF = 1152


norm_eps = 1e-05
theta_base = 160000.0


def layer_norm(values, gain):
    mean_val = jnp.mean(values, axis=-1, keepdims=True)
    centred = values - mean_val
    variance = jnp.mean(centred * centred, axis=-1, keepdims=True)
    return centred * lax.rsqrt(variance + norm_eps) * gain


def rotary_tables(positions, head_size):
    half_size = head_size // 2
    exponents = jnp.arange(half_size, dtype=jnp.float32) * (2.0 / head_size)
    inv_freq = 1.0 / theta_base**exponents
    angles = positions.astype(jnp.float32)[:, None] * inv_freq[None, :]
    cosine = jnp.cos(angles)
    sine = jnp.sin(angles)
    return (jnp.concatenate([cosine, cosine], -1), jnp.concatenate([sine, sine], -1))


def rotate(values, cosine, sine):
    half_size = values.shape[-1] // 2
    turned = jnp.concatenate([-values[..., half_size:], values[..., :half_size]], -1)
    return values * cosine[:, None, :] + turned * sine[:, None, :]


def fold_blocks(carry, pieces, piece_segments, work, rows):
    count = piece_segments.shape[0]
    size = math.gcd(count, 4 * rows)
    number = count // size
    blocks = tuple((part.reshape((number, size) + part.shape[1:]) for part in pieces))
    blocks = blocks + (piece_segments.reshape(number, size),)

    def step(acc, block):
        acc = work(acc, block)
        return (acc, None)

    carry, _ = lax.scan(step, carry, blocks)
    return carry


def on_device(hidden_in, grad_out, segment_ids, w_qkv, w_out, w_in, w_down, gain_attn, gain_mlp):
    rows = hidden_in.shape[1]
    local_seqs = hidden_in.shape[0]
    score_scale = HD ** (-0.5)
    bf16 = jnp.bfloat16
    f32 = jnp.float32
    gathered = (
        lax.all_gather(w_qkv.astype(bf16), "dp", axis=0, tiled=True),
        lax.all_gather(w_out.astype(bf16), "dp", axis=0, tiled=True),
        lax.all_gather(w_in.astype(bf16), "dp", axis=0, tiled=True),
        lax.all_gather(w_down.astype(bf16), "dp", axis=1, tiled=True),
        lax.all_gather(gain_attn.astype(bf16), "dp", axis=0, tiled=True),
        lax.all_gather(gain_mlp.astype(bf16), "dp", axis=0, tiled=True),
    )
    weight_qkv, weight_out, weight_in, weight_down, gain_low_a, gain_low_b = gathered
    gain_first = gain_low_a.astype(f32)
    gain_second = gain_low_b.astype(f32)
    whole_segments = lax.all_gather(segment_ids, "ctx", axis=1, tiled=True)
    positions = lax.axis_index("ctx") * rows + jnp.arange(rows, dtype=jnp.int32)
    cosine, sine = rotary_tables(positions, HD)

    def gated(values_in):
        return jax.nn.gelu(values_in[:, :FF], approximate=False) * values_in[:, FF:]

    def turn(pair):
        return (rotate(pair[0], cosine, sine), rotate(pair[1], cosine, sine))

    def one_sequence(seq_index):
        hidden = hidden_in[seq_index].astype(f32)
        own_segments = segment_ids[seq_index]
        all_segments = whole_segments[seq_index]
        normed_first, first_back = jax.vjp(layer_norm, hidden, gain_first)
        normed_attn = normed_first.astype(bf16)
        qkv = jnp.dot(normed_attn, weight_qkv, preferred_element_type=f32)
        q_lin = qkv[:, :D].reshape(rows, HEADS, HD)
        k_lin = qkv[:, D : 2 * D].reshape(rows, HEADS, HD)
        v_lin = qkv[:, 2 * D :].reshape(rows, HEADS, HD)
        turned, turn_back = jax.vjp(turn, (q_lin, k_lin))
        queries = turned[0].astype(bf16)
        keys = turned[1].astype(bf16)
        values = v_lin.astype(bf16)

        def forward_work(acc, block):
            key_blk, value_blk, seg_blk = block
            total, summed = acc
            scores = (
                jnp.einsum("thd,shd->hts", queries, key_blk, preferred_element_type=f32)
                * score_scale
            )
            same = own_segments[:, None] == seg_blk[None, :]
            expo = jnp.where(same[None], jnp.exp(scores), 0.0)
            total = total + jnp.sum(expo, axis=-1)
            summed = summed + jnp.einsum(
                "hts,shd->thd", expo.astype(bf16), value_blk, preferred_element_type=f32
            )
            return (total, summed)

        start_fwd = (jnp.zeros((HEADS, rows), f32), jnp.zeros((rows, HEADS, HD), f32))
        key_piece = lax.all_gather(keys.reshape(rows, D), "ctx", axis=0, tiled=True)
        value_piece = lax.all_gather(values.reshape(rows, D), "ctx", axis=0, tiled=True)
        count = key_piece.shape[0]
        piece_segments = all_segments
        parts = (key_piece.reshape(count, HEADS, HD), value_piece.reshape(count, HEADS, HD))
        total, summed = fold_blocks(start_fwd, parts, piece_segments, forward_work, rows)
        total_rows = jnp.transpose(total)
        attended = (summed / total_rows[:, :, None]).reshape(rows, D).astype(bf16)
        mixed = hidden + jnp.dot(attended, weight_out, preferred_element_type=f32)
        normed_second, second_back = jax.vjp(layer_norm, mixed, gain_second)
        normed_mlp = normed_second.astype(bf16)
        gate_up = jnp.dot(normed_mlp, weight_in, preferred_element_type=f32)
        activ_f, gated_back = jax.vjp(gated, gate_up)
        activ = activ_f.astype(bf16)
        layer_out = (mixed + jnp.dot(activ, weight_down, preferred_element_type=f32)).astype(bf16)
        grad_low = grad_out[seq_index]
        g_w_down = jnp.einsum("tf,td->fd", activ, grad_low, preferred_element_type=f32)
        g_activ = jnp.einsum("td,fd->tf", grad_low, weight_down, preferred_element_type=f32)
        g_gate_up = gated_back(g_activ)[0].astype(bf16)
        g_w_in = jnp.einsum("ti,tj->ij", normed_mlp, g_gate_up, preferred_element_type=f32)
        g_normed_mlp = jnp.einsum("tj,ij->ti", g_gate_up, weight_in, preferred_element_type=f32)
        g_mixed_norm, g_gain_mlp = second_back(g_normed_mlp)
        g_mixed = grad_low.astype(f32) + g_mixed_norm
        g_mixed_low = g_mixed.astype(bf16)
        g_w_out = jnp.einsum("ti,tj->ij", attended, g_mixed_low, preferred_element_type=f32)
        g_att = jnp.einsum(
            "tj,ij->ti", g_mixed_low, weight_out, preferred_element_type=f32
        ).reshape(rows, HEADS, HD)
        g_summed = (g_att / total_rows[:, :, None]).astype(bf16)
        row_term = jnp.sum(g_att * summed, axis=-1) / (total_rows * total_rows)
        own_rows = jnp.transpose(row_term)
        all_rows = lax.all_gather(row_term, "ctx", axis=0, tiled=True)

        def query_work(acc, block):
            key_blk, value_blk, seg_blk = block
            scores = (
                jnp.einsum("thd,shd->hts", queries, key_blk, preferred_element_type=f32)
                * score_scale
            )
            same = own_segments[:, None] == seg_blk[None, :]
            expo = jnp.where(same[None], jnp.exp(scores), 0.0)
            product = jnp.einsum("thd,shd->hts", g_summed, value_blk, preferred_element_type=f32)
            g_scores = (expo * (product - own_rows[:, :, None])).astype(bf16)
            return acc + jnp.einsum("hts,shd->thd", g_scores, key_blk, preferred_element_type=f32)

        key_piece = lax.all_gather(keys.reshape(rows, D), "ctx", axis=0, tiled=True)
        value_piece = lax.all_gather(values.reshape(rows, D), "ctx", axis=0, tiled=True)
        count = key_piece.shape[0]
        piece_segments = all_segments
        parts = (key_piece.reshape(count, HEADS, HD), value_piece.reshape(count, HEADS, HD))
        g_queries = (
            fold_blocks(jnp.zeros((rows, HEADS, HD), f32), parts, piece_segments, query_work, rows)
            * score_scale
        )

        def key_work(acc, block):
            query_blk, gsum_blk, row_blk, seg_blk = block
            g_keys, g_values = acc
            scores = (
                jnp.einsum("shd,thd->hst", query_blk, keys, preferred_element_type=f32)
                * score_scale
            )
            same = seg_blk[:, None] == own_segments[None, :]
            expo = jnp.where(same[None], jnp.exp(scores), 0.0)
            g_values = g_values + jnp.einsum(
                "hst,shd->thd", expo.astype(bf16), gsum_blk, preferred_element_type=f32
            )
            product = jnp.einsum("shd,thd->hst", gsum_blk, values, preferred_element_type=f32)
            g_scores = (expo * (product - jnp.transpose(row_blk)[:, :, None])).astype(bf16)
            g_keys = g_keys + jnp.einsum(
                "hst,shd->thd", g_scores, query_blk, preferred_element_type=f32
            )
            return (g_keys, g_values)

        start_keys = (jnp.zeros((rows, HEADS, HD), f32), jnp.zeros((rows, HEADS, HD), f32))
        query_piece = lax.all_gather(queries.reshape(rows, D), "ctx", axis=0, tiled=True)
        gsum_piece = lax.all_gather(g_summed.reshape(rows, D), "ctx", axis=0, tiled=True)
        count = query_piece.shape[0]
        piece_segments = all_segments
        parts = (
            query_piece.reshape(count, HEADS, HD),
            gsum_piece.reshape(count, HEADS, HD),
            all_rows,
        )
        g_keys, g_values = fold_blocks(start_keys, parts, piece_segments, key_work, rows)
        g_keys = g_keys * score_scale
        unturned = turn_back((g_queries, g_keys))[0]
        g_qkv = jnp.concatenate(
            [unturned[0].reshape(rows, D), unturned[1].reshape(rows, D), g_values.reshape(rows, D)],
            -1,
        ).astype(bf16)
        g_w_qkv = jnp.einsum("ti,tj->ij", normed_attn, g_qkv, preferred_element_type=f32)
        g_normed_attn = jnp.einsum("tj,ij->ti", g_qkv, weight_qkv, preferred_element_type=f32)
        g_hidden_norm, g_gain_attn = first_back(g_normed_attn)
        grad_in = (g_mixed + g_hidden_norm).astype(bf16)
        terms = (g_w_qkv, g_w_out, g_w_in, g_w_down, g_gain_attn, g_gain_mlp)
        return (layer_out, grad_in, terms)

    outputs_fwd = []
    outputs_back = []
    terms = None
    for seq_index in range(local_seqs):
        layer_out, grad_in, seq_terms = one_sequence(seq_index)
        outputs_fwd.append(layer_out)
        outputs_back.append(grad_in)
        if terms is None:
            terms = seq_terms
        else:
            terms = tuple((old + new for old, new in zip(terms, seq_terms)))
    everywhere = lax.psum(terms, "ctx")
    owned = (
        lax.psum_scatter(
            everywhere[0].astype(jnp.bfloat16), "dp", scatter_dimension=0, tiled=True
        ).astype(jnp.float32),
        lax.psum_scatter(
            everywhere[1].astype(jnp.bfloat16), "dp", scatter_dimension=0, tiled=True
        ).astype(jnp.float32),
        lax.psum_scatter(
            everywhere[2].astype(jnp.bfloat16), "dp", scatter_dimension=0, tiled=True
        ).astype(jnp.float32),
        lax.psum_scatter(
            everywhere[3].astype(jnp.bfloat16), "dp", scatter_dimension=1, tiled=True
        ).astype(jnp.float32),
        lax.psum_scatter(
            everywhere[4].astype(jnp.bfloat16), "dp", scatter_dimension=0, tiled=True
        ).astype(jnp.float32),
        lax.psum_scatter(
            everywhere[5].astype(jnp.bfloat16), "dp", scatter_dimension=0, tiled=True
        ).astype(jnp.float32),
    )
    return (
        jnp.stack(outputs_fwd),
        jnp.stack(outputs_back),
        owned[0],
        owned[1],
        owned[2],
        owned[3],
        owned[4],
        owned[5],
    )


HALF = 384
PIECE = 24


def send(values, mask):
    return lax.ppermute(values, ("dp", "ctx"), [(i, i ^ mask) for i in range(32)])


def send_swapped(values, mask):
    def target(i):
        core, high = (i >> 3) & 1, (i >> 2) & 1
        return (i & ~12) | (high << 3) | (core << 2)

    return lax.ppermute(values, ("dp", "ctx"), [(i, target(i) ^ mask) for i in range(32)])


def pick(flag, first, second):
    return jnp.where(flag == 0, first, second)


VM = pl.BlockSpec(memory_space=pltpu.VMEM)
SM = pl.BlockSpec(memory_space=pltpu.SMEM)


def pieces_of(me, near_ref, far_ref):
    for slot, mask in enumerate(XZ):
        start = pl.multiple_of((me % 8 ^ mask) * PIECE, 8)
        yield start, (near_ref, far_ref)[slot // 4][slot % 4].astype(jnp.float32)


def qkv_result_kernel(me_ref, near_ref, far_ref, out_ref, gains_ref, buffer_ref):
    me = me_ref[0]
    core = (me // 8) % 2
    wide = 3 * HALF + 128
    for start, piece in pieces_of(me, near_ref, far_ref):
        rows = pl.ds(start, PIECE)
        for half in range(2):
            for t in range(3):
                column = pl.multiple_of(t * D + (half ^ core) * HALF, 128)
                first = half * wide + t * HALF
                out_ref[rows, pl.ds(column, HALF)] = piece[:, first : first + HALF]
        buffer_ref[rows, :] = piece[:, 3 * HALF : wide] + piece[:, wide + 3 * HALF :]
    gains_ref[...] = buffer_ref[...].T[:8, :192]


def mlp_result_kernel(
    me_ref, near_1, far_1, near_2, far_2, w_in_ref, w_out_ref, w_down_ref
):
    me = me_ref[0]
    for start, piece in pieces_of(me, near_1, far_1):
        rows = pl.ds(start, PIECE)
        w_in_ref[rows, :768] = piece[:, :768]
        w_in_ref[rows, FF : FF + 768] = piece[:, 768:1536]
        w_down_ref[rows, :768] = piece[:, 1536:]
    for start, piece in pieces_of(me, near_2, far_2):
        rows = pl.ds(start, PIECE)
        w_in_ref[rows, 768:FF] = piece[:, :384]
        w_in_ref[rows, FF + 768 :] = piece[:, 384:768]
        w_out_ref[rows, :384] = piece[:, 768:1152]
        w_out_ref[rows, 384:] = piece[:, 1536:]
        w_down_ref[rows, 768:] = piece[:, 1152:1536]


def plus(first, second):
    return (first.astype(jnp.float32) + second.astype(jnp.float32)).astype(jnp.bfloat16)


def finish(body, me, pieces, shapes, scratch, name):
    return pl.pallas_call(
        body,
        out_shape=tuple(jax.ShapeDtypeStruct(shape, jnp.float32) for shape in shapes),
        in_specs=[SM] + [VM] * len(pieces),
        out_specs=(VM,) * len(shapes),
        scratch_shapes=[pltpu.VMEM(scratch, jnp.float32)] if scratch else [],
        compiler_params=pltpu.CompilerParams(vmem_limit_bytes=24 << 20),
        name=name,
    )(me, *pieces)


XZ = [dx | (dz << 1) for dx in range(2) for dz in range(4)]


def masks(*bits):
    order = [0]
    for bit in bits:
        choices = (0, bit) if bit != 6 else (0, 2, 4, 6)
        order = [m | choice for m in order for choice in choices]
    return order


def after(values, *others):
    return lax.optimization_barrier((values,) + others)[0]


def stage(*values):
    return lax.optimization_barrier(values)


def norm_parts(values):
    mean_val = jnp.mean(values, axis=-1, keepdims=True)
    centred = values - mean_val
    variance = jnp.mean(centred * centred, axis=-1, keepdims=True)
    scale = lax.rsqrt(variance + norm_eps)
    return centred * scale, scale


def norm_back(xhat, scale, grad, gain):
    e = grad * gain
    return scale * (
        e
        - jnp.mean(e, axis=-1, keepdims=True)
        - xhat * jnp.mean(e * xhat, axis=-1, keepdims=True)
    )


NT = (((1,), (1,)), ((), ()))
FAR_APART = -1.0e30
MEGA = 1 << 20


def matmul(first, second, dims=None):
    dims = dims or (((1,), (0,)), ((), ()))
    return lax.dot_general(first, second, dims, preferred_element_type=jnp.float32)


def kernel_call(body, outs, scratch, name, flops, moved):
    count = len(outs)
    return lambda *args: pl.pallas_call(
        body,
        out_shape=tuple(jax.ShapeDtypeStruct(shape, kind) for shape, kind in outs),
        in_specs=[SM] + [VM] * (len(args) - 1),
        out_specs=(VM,) * count,
        scratch_shapes=[pltpu.VMEM(shape, kind) for shape, kind in scratch],
        compiler_params=pltpu.CompilerParams(vmem_limit_bytes=32 * MEGA),
        cost_estimate=pl.CostEstimate(flops=flops, bytes_accessed=moved, transcendentals=0),
        name=name,
    )(*args)


def swap_halves(pair):
    lane = lax.broadcasted_iota(jnp.int32, pair.shape, 1) % HD
    return jnp.where(lane < HD // 2, pltpu.roll(pair, 96, 1), pltpu.roll(pair, 32, 1))


def place_rows(me, pieces, whole_ref):
    for mask, piece in pieces:
        start = pl.multiple_of((me // 8 ^ mask) * 192, 16)
        whole_ref[pl.ds(start, 192), :] = piece


def attention_kernel(
    me_ref,
    own_ref,
    across_ref,
    peer_ref,
    beyond_ref,
    mine_ref,
    core_ref,
    up_ref,
    both_ref,
    cos_ref,
    sin_ref,
    normed_ref,
    q_ref,
    k_ref,
    v_ref,
    probs_ref,
    att_own_ref,
    att_peer_ref,
    att_ref,
    inv_ref,
    weight_ref,
    gains_ref,
    q_id_ref,
    keys_ref,
    values_ref,
):
    f32, bf16 = jnp.float32, jnp.bfloat16
    me = me_ref[0]
    shards = (mine_ref, core_ref, up_ref, both_ref)
    place_rows(me, [(mask, ref[:192, :]) for mask, ref in enumerate(shards)], weight_ref)
    gains = sum(ref[192:200, :].astype(f32) for ref in shards)[:, :D]
    gains_ref[...] = gains
    gain = gains[0:1, :]
    row_id = lax.broadcasted_iota(jnp.int32, (128, 128), 0).astype(f32)
    blocks = [own_ref.at[i] for i in range(2)] + [peer_ref.at[i] for i in range(2)]
    blocks += [across_ref.at[i] for i in range(2)] + [beyond_ref.at[i] for i in range(2)]
    for i, block in enumerate(blocks):
        rows = slice(128 * i, 128 * (i + 1))
        hidden = block[:128, :].astype(f32)
        centred = hidden - jnp.mean(hidden, axis=1, keepdims=True)
        variance = jnp.mean(centred * centred, axis=1, keepdims=True)
        normed = (centred * lax.rsqrt(variance + norm_eps) * gain).astype(bf16)
        normed_ref[rows, :] = normed
        ids = block[128:136, :128].astype(f32)[0:1, :]
        hit = jnp.where(row_id == ids, 1.0, 0.0).T
        keys_ref[rows, 128:] = (1.0 - hit).astype(bf16)
        values_ref[rows, 128:] = jnp.ones((128, 128), bf16)
        if i < 4:
            q_id_ref[rows, :] = (hit * FAR_APART).astype(bf16)

    for i in range(4):
        rows = slice(256 * i, 256 * (i + 1))
        normed = normed_ref[rows, :]
        first = 0 if i < 2 else HALF
        qkv = matmul(normed, weight_ref[:, first:])
        for j in range(first // 128, 9):
            part = qkv[:, 128 * j - first : 128 * j - first + 128]
            columns = slice(128 * (j % 3), 128 * (j % 3) + 128)
            if j < 6:
                part = part * cos_ref[rows, :] + swap_halves(part) * sin_ref[rows, :]
            if j < 3:
                q_ref[rows, columns] = (part * HD**-0.5).astype(bf16)
            elif j < 6:
                k_ref[rows, columns] = part.astype(bf16)
            else:
                v_ref[rows, columns] = part.astype(bf16)

    low_head = lax.broadcasted_iota(jnp.int32, (256, 128), 1) < HD
    for pair in range(3):
        columns = slice(128 * pair, 128 * pair + 128)
        keys_ref[:, :128] = k_ref[:, columns]
        values_ref[:, :128] = v_ref[:, columns]
        for i in range(2):
            rows = slice(256 * i, 256 * (i + 1))
            queries = q_ref[rows, columns]
            found = []
            for head in range(2):
                picked = jnp.where(low_head == (head == 0), queries, jnp.zeros_like(queries))
                scores = matmul(
                    jnp.concatenate([picked, q_id_ref[rows, :]], 1), keys_ref[...], NT
                )
                probs = jnp.exp(scores).astype(bf16)
                probs_ref[2 * pair + head, rows, :] = probs
                found.append(matmul(probs, values_ref[...]))
            inverse = 1.0 / jnp.where(low_head, found[0][:, 128:], found[1][:, 128:])
            attended = jnp.where(low_head, found[0][:, :128], found[1][:, :128]) * inverse
            inv_ref[rows, columns] = inverse
            att_ref[rows, columns] = attended
            out_ref = att_own_ref if i == 0 else att_peer_ref
            out_ref[:, columns] = attended.astype(bf16)


def attention_forward(*args):
    f32, bf16 = jnp.float32, jnp.bfloat16
    outs = [
        ((1024, D), bf16),
        ((512, HALF), bf16),
        ((1024, HALF), bf16),
        ((1024, HALF), bf16),
        ((6, 512, 1024), bf16),
        ((256, HALF), bf16),
        ((256, HALF), bf16),
        ((512, HALF), f32),
        ((512, HALF), f32),
        ((D, 3 * HALF), bf16),
        ((8, D), f32),
    ]
    scratch = [((512, 128), bf16), ((1024, 256), bf16), ((1024, 256), bf16)]
    return kernel_call(attention_kernel, outs, scratch, "attention_fwd", 4 * 10**9, 8 * MEGA)(*args)


def put_pieces(me, order, values_ref, out_ref, columns):
    for slot, mask in enumerate(order):
        start = pl.multiple_of((me ^ mask) * PIECE, 8)
        out_ref[slot, :, columns] = values_ref[pl.ds(start, PIECE), :].astype(out_ref.dtype)


def gated_block(normed, grad, gate_rows, upper_rows, down_rows):
    bf16 = jnp.bfloat16
    gate = matmul(normed, gate_rows)
    upper = matmul(normed, upper_rows)
    chance = 0.5 + 0.5 * lax.erf(gate * math.sqrt(0.5))
    bell = jnp.exp(-0.5 * gate * gate) * (1.0 / math.sqrt(2.0 * math.pi))
    gelu = gate * chance
    g_activ = matmul(grad, down_rows)
    g_gate = (g_activ * upper * (chance + gate * bell)).astype(bf16)
    g_upper = (g_activ * gelu).astype(bf16)
    return (gelu * upper).astype(bf16), g_gate, g_upper


WIDTH = 384


def mlp_first_kernel(
    me_ref,
    own_ref,
    att_ref,
    att_peer_ref,
    grad_ref,
    gains_ref,
    shard_ref,
    core_ref,
    up_ref,
    both_ref,
    down_ref,
    g_normed_ref,
    xhat_ref,
    scale_ref,
    w_out_ref,
    away_ref,
    stay_ref,
    w_ref,
    buffer_ref,
):
    f32, bf16 = jnp.float32, jnp.bfloat16
    me = me_ref[0]
    core = (me // 8) % 2
    shards = (shard_ref, core_ref, up_ref, both_ref)
    for mask, ref in enumerate(shards):
        shard = me // 8 ^ mask
        head_row = (shard // 2 ^ core) * HALF + (shard % 2) * 192
        w_out_ref[pl.ds(pl.multiple_of(head_row, 16), 192), :] = ref[:, :D]
    place_rows(me, [(mask, ref[:, D:]) for mask, ref in enumerate(shards)], w_ref)

    attended = jnp.concatenate([att_ref[...], att_peer_ref[...]], 1)
    hidden = jnp.concatenate([own_ref[0, :128, :], own_ref[1, :128, :]]).astype(f32)
    mixed = hidden + matmul(attended, w_out_ref[...])
    centred = mixed - jnp.mean(mixed, axis=1, keepdims=True)
    scale = lax.rsqrt(jnp.mean(centred * centred, axis=1, keepdims=True) + norm_eps)
    xhat = centred * scale
    xhat_ref[...] = xhat
    scale_ref[...] = jnp.broadcast_to(scale, (256, 128))
    normed = (xhat * gains_ref[1:2, :]).astype(bf16)
    grad = grad_ref[...]
    normed_t, grad_t = normed.T, grad.T
    orders = masks(16, 1, 6), masks(1, 16, 6)

    def emit(values, late, first):
        buffer_ref[...] = values
        columns = pl.ds(pl.multiple_of(first, 128), WIDTH)
        for slot, (early_mask, late_mask) in enumerate(zip(*orders)):
            mask = early_mask + late * (late_mask - early_mask)
            for ref, core_mask in ((away_ref, 8), (stay_ref, 0)):
                start = pl.multiple_of((me ^ (mask + core_mask)) * PIECE, 8)
                ref[slot, :, columns] = buffer_ref[pl.ds(start, PIECE), :].astype(bf16)

    down_ref[...] = mixed
    g_normed_ref[...] = jnp.zeros_like(mixed)

    def block(i, carry):
        low, high, last = (
            w_ref[:, pl.ds(pl.multiple_of(first + WIDTH * i, 128), WIDTH)]
            for first in (0, 768, 1536)
        )
        activ, g_gate, g_upper = gated_block(normed, grad, low, high, last)
        down_ref[...] += matmul(activ, last, NT)
        g_normed_ref[...] += matmul(g_gate, low, NT) + matmul(g_upper, high, NT)
        emit(matmul(normed_t, g_gate), 0, WIDTH * i)
        emit(matmul(normed_t, g_upper), i, 768 + WIDTH * i)
        emit(matmul(grad_t, activ), 1, 1536 + WIDTH * i)
        return carry

    lax.fori_loop(0, 2, block, 0)


def mlp_first(*args):
    f32, bf16 = jnp.float32, jnp.bfloat16
    outs = [
        ((256, D), f32),
        ((256, D), f32),
        ((256, D), f32),
        ((256, 128), f32),
        ((D, D), bf16),
        ((16, PIECE, 6 * WIDTH), bf16),
        ((16, PIECE, 6 * WIDTH), bf16),
    ]
    scratch = [((D, 6 * WIDTH), bf16), ((D, WIDTH), f32)]
    return kernel_call(mlp_first_kernel, outs, scratch, "mlp_first", 3 * 10**9, 16 * MEGA)(*args)


def mlp_second_kernel(
    me_ref,
    att_ref,
    att_peer_ref,
    grad_ref,
    gains_ref,
    shard_ref,
    core_ref,
    up_ref,
    both_ref,
    down_ref,
    g_normed_ref,
    xhat_ref,
    scale_ref,
    w_out_ref,
    out_ref,
    g_mixed_ref,
    g_att_ref,
    g_att_peer_ref,
    away_ref,
    stay_ref,
    g_gain_ref,
    w_ref,
    buffer_ref,
):
    f32, bf16 = jnp.float32, jnp.bfloat16
    me = me_ref[0]
    core = (me // 8) % 2
    shards = (shard_ref, core_ref, up_ref, both_ref)
    place_rows(me, [(mask, ref[...]) for mask, ref in enumerate(shards)], w_ref)
    gain = gains_ref[1:2, :]
    xhat = xhat_ref[...]
    scale = scale_ref[:, 0:1]
    normed = (xhat * gain).astype(bf16)
    grad = grad_ref[...]
    normed_t, grad_t = normed.T, grad.T
    y_first, x_first = masks(16, 1, 6), masks(1, 16, 6)

    def emit(order, first):
        columns = slice(first, first + WIDTH)
        put_pieces(me, [m | 8 for m in order], buffer_ref, away_ref, columns)
        put_pieces(me, order, buffer_ref, stay_ref, columns)

    low, high, last = (slice(first, first + WIDTH) for first in (0, 384, 768))
    activ, g_gate, g_upper = gated_block(normed, grad, w_ref[:, low], w_ref[:, high], w_ref[:, last])
    g_normed = g_normed_ref[...] + matmul(g_gate, w_ref[:, low], NT)
    g_normed = g_normed + matmul(g_upper, w_ref[:, high], NT)
    e = g_normed * gain
    g_mixed = grad.astype(f32) + scale * (
        e
        - jnp.mean(e, axis=1, keepdims=True)
        - xhat * jnp.mean(e * xhat, axis=1, keepdims=True)
    )
    g_mixed_ref[...] = g_mixed
    g_low = g_mixed.astype(bf16)
    g_att = matmul(g_low, w_out_ref[...], NT).astype(bf16)
    g_att_ref[...] = g_att[:, :HALF]
    g_att_peer_ref[...] = g_att[:, HALF:]
    out_ref[...] = (down_ref[...] + matmul(activ, w_ref[:, last], NT)).astype(bf16)
    g_gain = jnp.broadcast_to(jnp.sum(xhat * g_normed, axis=0, keepdims=True), (128, D))
    row = lax.broadcasted_iota(jnp.int32, (128, D), 0)
    g_gain_ref[...] = jnp.where(row == 1, g_gain, 0.0).T
    buffer_ref[...] = matmul(normed_t, g_gate)
    emit(y_first, 0)
    buffer_ref[...] = matmul(normed_t, g_upper)
    emit(y_first, WIDTH)
    buffer_ref[...] = matmul(grad_t, activ)
    emit(x_first, 3 * WIDTH)
    attended_t = jnp.concatenate([att_ref[...], att_peer_ref[...]], 1).T
    for i in range(2):
        rows_out = matmul(attended_t, g_low[:, WIDTH * i : WIDTH * (i + 1)])
        for half in range(2):
            start = pl.multiple_of((half ^ core) * HALF, HALF)
            buffer_ref[pl.ds(start, HALF), :] = rows_out[HALF * half : HALF * (half + 1), :]
        emit(y_first if i == 0 else x_first, (2 + 2 * i) * WIDTH)


def mlp_second(*args):
    f32, bf16 = jnp.float32, jnp.bfloat16
    outs = [
        ((256, D), bf16),
        ((256, D), f32),
        ((256, HALF), bf16),
        ((256, HALF), bf16),
        ((16, PIECE, 5 * WIDTH), bf16),
        ((16, PIECE, 5 * WIDTH), bf16),
        ((D, 128), f32),
    ]
    scratch = [((D, 3 * WIDTH), bf16), ((D, WIDTH), f32)]
    return kernel_call(mlp_second_kernel, outs, scratch, "mlp_second", 2 * 10**9, 10 * MEGA)(*args)


def attention_back_kernel(
    me_ref,
    g_own_ref,
    g_peer_ref,
    att_ref,
    inv_ref,
    q_ref,
    k_ref,
    v_ref,
    probs_ref,
    cos_ref,
    sin_ref,
    dq_ref,
    dk_ref,
    dv_ref,
    values_ref,
):
    f32, bf16 = jnp.float32, jnp.bfloat16
    low_head = lax.broadcasted_iota(jnp.int32, (1024, 128), 1) < HD
    lane = lax.broadcasted_iota(jnp.int32, (512, 128), 1)
    values_ref[:, 128:] = jnp.ones((1024, 128), bf16)
    for pair in range(3):
        columns = slice(128 * pair, 128 * pair + 128)
        values_ref[:, :128] = v_ref[:, columns]
        queries_t, keys = q_ref[:, columns].T, k_ref[:, columns]
        grad = jnp.concatenate([g_own_ref[:, columns], g_peer_ref[:, columns]]).astype(f32)
        grad = grad * inv_ref[:, columns]
        terms = grad * att_ref[:, columns]
        grad = grad.astype(bf16)
        grad_t = grad.T
        g_queries = jnp.zeros((512, 128), f32)
        g_keys, g_values = [], []
        for head in range(2):
            mine = low_head == (head == 0)
            rows = slice(HD * head, HD * head + HD)
            row = jnp.sum(jnp.where(mine[:512], terms, 0.0), axis=1, keepdims=True)
            high = row.astype(bf16)
            middle = (row - high.astype(f32)).astype(bf16)
            rest = (row - high.astype(f32) - middle.astype(f32)).astype(bf16)
            extra = jnp.where(lane == 0, -high.astype(f32), 0.0)
            extra = jnp.where(lane == 1, -middle.astype(f32), extra)
            extra = jnp.where(lane == 2, -rest.astype(f32), extra).astype(bf16)
            picked = jnp.where(mine[:512], grad, jnp.zeros_like(grad))
            product = matmul(jnp.concatenate([picked, extra], 1), values_ref[...], NT)
            probs = probs_ref[2 * pair + head]
            g_scores = (probs.astype(f32) * product).astype(bf16)
            g_queries = g_queries + matmul(g_scores, jnp.where(mine, keys, jnp.zeros_like(keys)))
            g_keys.append(matmul(queries_t[rows, :], g_scores))
            g_values.append(matmul(grad_t[rows, :], probs))
        g_queries = g_queries * HD**-0.5
        near = slice(0, 512)
        dq_ref[:, columns] = (
            g_queries * cos_ref[near, :] - swap_halves(g_queries) * sin_ref[near, :]
        ).astype(bf16)
        g_keys = jnp.concatenate(g_keys).T
        dk_ref[:, columns] = (
            g_keys * cos_ref[...] - swap_halves(g_keys) * sin_ref[...]
        ).astype(bf16)
        dv_ref[:, columns] = jnp.concatenate(g_values).T.astype(bf16)


def attention_backward(*args):
    bf16 = jnp.bfloat16
    outs = [((512, HALF), bf16), ((1024, HALF), bf16), ((1024, HALF), bf16)]
    scratch = [((1024, 256), bf16)]
    return kernel_call(
        attention_back_kernel, outs, scratch, "attention_bwd", 5 * 10**9, 10 * MEGA
    )(*args)


def qkv_weight_kernel(
    me_ref,
    normed_ref,
    weight_ref,
    g_gain_ref,
    dq_ref,
    dk_ref,
    dv_ref,
    keep_a,
    away_a,
    peer_b,
    buffer_ref,
):
    me = me_ref[0]
    order_a, order_b = masks(1, 6), masks(1, 16, 6)
    normed_t = normed_ref[...].T

    def emit(values_ref, columns):
        put_pieces(me, order_a, values_ref, keep_a, columns)
        put_pieces(me, [m | 16 for m in order_a], values_ref, away_a, columns)
        put_pieces(me, [m | 8 for m in order_b], values_ref, peer_b, columns)

    g_gain = jnp.zeros((D, 1), jnp.float32)
    for i, ref in enumerate((dq_ref, dk_ref, dv_ref)):
        columns = slice(HALF * i, HALF * (i + 1))
        values = matmul(normed_t[:, : ref.shape[0]], ref[...])
        weight = weight_ref[:, columns].astype(jnp.float32)
        g_gain = g_gain + jnp.sum(values * weight, axis=1, keepdims=True)
        buffer_ref[...] = values
        emit(buffer_ref, columns)
    lane = lax.broadcasted_iota(jnp.int32, (D, 128), 1)
    buffer_ref[:, :128] = jnp.where(lane == 0, g_gain, g_gain_ref[...])
    emit(buffer_ref.at[:, :128], slice(3 * HALF, 3 * HALF + 128))


def qkv_weight_gradient(*args):
    outs = [((count, PIECE, 3 * HALF + 128), jnp.bfloat16) for count in (8, 8, 16)]
    scratch = [((D, HALF), jnp.float32)]
    return kernel_call(qkv_weight_kernel, outs, scratch, "qkv_weights", 2 * 10**9, 8 * MEGA)(*args)


def qkv_input_kernel(me_ref, weight_ref, dq_ref, dk_ref, dv_ref, own_ref, across_ref, peer_ref):
    targets = (own_ref, peer_ref.at[0], across_ref, peer_ref.at[1])
    for i, target in enumerate(targets):
        rows = slice(256 * i, 256 * (i + 1))
        grad = matmul(dk_ref[rows, :], weight_ref[:, HALF : 2 * HALF], NT)
        grad = grad + matmul(dv_ref[rows, :], weight_ref[:, 2 * HALF :], NT)
        if i < 2:
            grad = grad + matmul(dq_ref[rows, :], weight_ref[:, :HALF], NT)
        target[...] = grad.astype(target.dtype)


def qkv_input_gradient(*args):
    bf16 = jnp.bfloat16
    outs = [((256, D), bf16), ((256, D), bf16), ((2, 256, D), bf16)]
    return kernel_call(qkv_input_kernel, outs, [], "qkv_inputs", 2 * 10**9, 6 * MEGA)(*args)


def paired_chips(hidden_in, grad_out, segment_ids, w_qkv, w_out, w_in, w_down, gain_attn, gain_mlp):
    bf16, f32 = jnp.bfloat16, jnp.float32
    dp, ctx = lax.axis_index("dp"), lax.axis_index("ctx")
    me = dp * 8 + ctx
    me_ref = me.reshape(1).astype(jnp.int32)
    c, zl, x = dp % 2, (ctx // 2) % 2, ctx % 2
    rows = hidden_in.shape[1]

    def to_chips(values):
        return (
            send_swapped(pick(zl, values[0], values[1]), 0),
            send_swapped(pick(zl, values[1], values[0]), 2),
        )

    def from_chips(values):
        block_a, block_b = send_swapped(values[:rows], 0), send_swapped(values[rows:], 2)
        return jnp.stack([pick(zl, block_a, block_b), pick(zl, block_b, block_a)])

    ids = jnp.pad(segment_ids[:, None, :], ((0, 0), (0, 7), (0, D - rows))).astype(bf16)
    packed = [pick(zl, a, b) for a, b in ((hidden_in, hidden_in[::-1]), (ids, ids[::-1]))]
    packed = jnp.concatenate(packed, 1)

    gains = lax.dynamic_update_slice(
        jnp.zeros((8, 3 * HALF), f32), jnp.stack([gain_attn, gain_mlp]), (0, 192 * dp)
    )

    def my_columns(core):
        columns = [lax.dynamic_slice_in_dim(w_qkv, t * D + core * HALF, HALF, 1) for t in range(3)]
        return jnp.concatenate([jnp.concatenate(columns, 1), gains]).astype(bf16)

    within = jnp.arange(rows, dtype=jnp.int32)
    starts = []
    for far in range(2):
        for core in range(2):
            for low in range(2):
                starts.append((2 * (2 * (c ^ core) + (zl ^ low)) + (x ^ far)) * rows + within)
    cosine, sine = rotary_tables(jnp.concatenate(starts), HD)
    sine = sine * jnp.where(jnp.arange(HD) < HD // 2, -1.0, 1.0)
    cosine, sine = jnp.concatenate([cosine] * 2, 1), jnp.concatenate([sine] * 2, 1)

    mine, other, packed = stage(my_columns(c), my_columns(1 - c), packed)
    own = jnp.stack([send_swapped(packed[0], 0), send_swapped(packed[1], 2)])
    up, up_other = send(mine, 16), send(other, 16)
    by_core = send(other, 8)
    w_down = w_down.T
    cut, rest = slice(0, 768), slice(768, FF)
    late = slice(FF + 768, None)
    first = jnp.concatenate([w_out, w_in[:, cut], w_in[:, FF : FF + 768], w_down[:, cut]], 1)
    second = jnp.concatenate([w_in[:, rest], w_in[:, late], w_down[:, rest]], 1)
    own, by_core, first, second = stage(own, by_core, first.astype(bf16), second.astype(bf16))
    up_first, up_second = send(first, 16), send(second, 16)
    across, peer = send(own, 1), send(own, 8)
    across, peer, up, up_other, cosine, sine = stage(across, peer, up, up_other, cosine, sine)
    by_both, beyond = send(up_other, 8), send(across, 8)
    grad_low = to_chips(after(grad_out, across))

    normed, queries, keys, values, probs, att_own, att_peer, att, inverse, weight, gains = (
        attention_forward(
            *(me_ref, own, across, peer, beyond),
            *(mine, by_core, up, by_both, cosine, sine),
        )
    )
    grad_a, grad_b, att_peer, first = stage(*grad_low, att_peer, first)
    grad_low = jnp.concatenate([grad_a, grad_b])
    att_peer = send(att_peer, 8)
    core_first = send(first, 8)
    core_second = send(after(second, grad_low), 8)
    up_first, att_peer = stage(up_first, att_peer)
    both_first = send(up_first, 8)
    down, g_norm, xhat, scale, w_out, away_1, stay_1 = mlp_first(
        me_ref, own, att_own, att_peer, grad_low, gains, first, core_first, up_first, both_first
    )
    away_1, up_second, core_second = stage(away_1, up_second, core_second)
    both_second = send(up_second, 8)

    def halves(values, got):
        count = values.shape[0] // 2
        return [
            plus(values[part, :, columns], got[part, :, columns])
            for columns in (slice(0, 3 * WIDTH), slice(3 * WIDTH, None))
            for part in (slice(0, count), slice(count, None))
        ]

    def fold(stay, got):
        return plus(stay[:4], got[:4]), plus(stay[4:], got[4:])

    def fold_near(part):
        return jnp.stack([part[0], part[2]]), jnp.stack([part[1], part[3]])

    def joined(stay_a, got_a, stay_b, got_b):
        return fold_near(jnp.concatenate([plus(stay_a, got_a), plus(stay_b, got_b)], 2))

    got_1 = send(away_1, 8)
    both_second, down = stage(both_second, down)
    layer_out, g_mixed, g_att, g_att_peer, away_2, stay_2, g_gain = mlp_second(
        me_ref,
        *(att_own, att_peer, grad_low, gains),
        *(second, core_second, up_second, both_second),
        *(down, g_norm, xhat, scale, w_out),
    )
    got_1, away_2, g_att_peer, layer_out = stage(got_1, away_2, g_att_peer, layer_out)
    g_att_peer = send(g_att_peer, 8)
    got_2 = send(away_2, 8)
    stay_1a, leave_a, stay_1b, leave_b = halves(stay_1, got_1)
    got_1a, got_1b = send(leave_a, 16), send(leave_b, 1)
    g_att_peer, layer_out = stage(g_att_peer, layer_out)
    layer_out = from_chips(layer_out)
    grads = attention_backward(
        me_ref, g_att, g_att_peer, att, inverse, queries, keys, values, probs, cosine, sine
    )
    got_1a, got_1b, got_2, layer_out, *grads = stage(got_1a, got_1b, got_2, layer_out, *grads)

    stay_1a, leave_1a = fold(stay_1a, got_1a)
    stay_1b, leave_1b = fold(stay_1b, got_1b)
    got_1a, got_1b = send(leave_1a, 1), send(leave_1b, 16)
    stay_2a, leave_a, stay_2b, leave_b = halves(stay_2, got_2)
    got_2a, got_2b = send(leave_a, 16), send(leave_b, 1)
    g_gain, *_ = stage(g_gain, leave_1a, leave_1b, leave_a, leave_b)
    keep_a, away_a, peer_b = qkv_weight_gradient(me_ref, normed, weight, g_gain, *grads)

    got_1a, got_1b, away_a, peer_b, *grads = stage(got_1a, got_1b, away_a, peer_b, *grads)
    got_core, got_a = send(peer_b, 8), send(away_a, 16)
    keep_1, leave_1 = joined(stay_1a, got_1a, stay_1b, got_1b)
    got_1 = send(leave_1, 2)
    got_core, _ = stage(got_core, leave_1)
    keep_b, away_b = got_core[:8], got_core[8:]
    got_b = send(away_b, 1)
    weight, *_ = stage(weight, leave_1, away_b)
    near, across, peer = qkv_input_gradient(me_ref, weight, *grads)

    peer = send(peer, 8)
    got_2a, got_2b, got_1, _ = stage(got_2a, got_2b, got_1, away_b)
    stay_2a, leave_2a = fold(stay_2a, got_2a)
    stay_2b, leave_2b = fold(stay_2b, got_2b)
    got_2a, got_2b = send(leave_2a, 1), send(leave_2b, 16)
    keep_1 = plus(keep_1, got_1)
    peer, keep_1, *_ = stage(peer, keep_1, leave_2a, leave_2b)
    got_1 = send(keep_1[1], 4)
    across = plus(across, peer[1])
    got_a, got_b, across, _ = stage(got_a, got_b, across, keep_1)

    stay_a, leave_a = fold(keep_a, got_a)
    stay_b, leave_b = fold(keep_b, got_b)
    got_a, got_b = send(leave_a, 1), send(leave_b, 16)
    got_1, got_2a, got_2b, across, *_ = stage(got_1, got_2a, got_2b, across, leave_a, leave_b)
    sum_1 = plus(keep_1[0], got_1)
    far_1 = send(sum_1, 4)
    keep_2, leave_2 = joined(stay_2a, got_2a, stay_2b, got_2b)
    got_2 = send(leave_2, 2)
    got_across = send(across, 1)
    got_a, got_b, *_ = stage(got_a, got_b, sum_1, leave_2, across)

    total = jnp.concatenate([plus(stay_a, got_a), plus(stay_b, got_b)], 2)
    got = [send(total[dz], 2 * dz) for dz in range(1, 4)]
    far_1, got_2, got_across, _ = stage(far_1, got_2, got_across, total)
    sum_1 = jnp.stack([sum_1, far_1])
    far_1 = send(sum_1, 2)
    keep_2 = plus(keep_2, got_2)
    got_2 = send(keep_2[1], 4)
    g_normed = plus(near, peer[0]).astype(f32) + got_across.astype(f32)
    xhat, scale = norm_parts(own[:, :rows].reshape(2 * rows, D).astype(f32))
    grad_in = (g_mixed + norm_back(xhat, scale, g_normed, gains[0])).astype(bf16)
    grad_in, _, _, *got = stage(grad_in, sum_1, keep_2, *got)

    total = sum((part.astype(f32) for part in got), total[0].astype(f32)).astype(bf16)
    got = [send(total, 2 * dz) for dz in range(1, 4)]
    far_1, got_2, _ = stage(far_1, got_2, total)
    sum_1 = jnp.stack([sum_1, far_1], 1).reshape(4, PIECE, -1)
    far_1 = send(sum_1, 1)
    sum_2 = plus(keep_2[0], got_2)
    far_2 = send(sum_2, 4)
    far_2, total, *got = stage(far_2, total, *got)
    total = jnp.stack([total, *got])
    far = send(total, 1)
    sum_2 = jnp.stack([sum_2, far_2])
    far_2 = send(sum_2, 2)
    grad_in, far_1, _ = stage(grad_in, far_1, total)
    grad_in = from_chips(grad_in)
    far_2, total = stage(far_2, total)
    sum_2 = jnp.stack([sum_2, far_2], 1).reshape(4, PIECE, -1)
    far_2 = send(sum_2, 1)
    g_w_qkv, g_gains = finish(
        qkv_result_kernel, me_ref, (total, far), ((192, 3 * D), (8, 192)), (256, 128), "qkv_result"
    )
    g_w_in, g_w_out, g_w_down = finish(
        mlp_result_kernel,
        me_ref,
        (sum_1, far_1, sum_2, far_2),
        ((192, 2 * FF), (192, D), (192, FF)),
        None,
        "mlp_result",
    )
    g_gain_attn = g_gains[0] / gain_attn.astype(bf16).astype(f32)
    return (layer_out, grad_in, g_w_qkv, g_w_out, g_w_in, g_w_down.T, g_gain_attn, g_gains[1])


def solution(mesh):
    whole_fit = mesh.shape["dp"] == 4 and mesh.shape["ctx"] == 8
    return jax.shard_map(
        paired_chips if whole_fit else on_device,
        mesh=mesh,
        in_specs=(
            P("dp", "ctx", None),
            P("dp", "ctx", None),
            P("dp", "ctx"),
            P("dp", None),
            P("dp", None),
            P("dp", None),
            P(None, "dp"),
            P("dp"),
            P("dp"),
        ),
        out_specs=(
            P("dp", "ctx", None),
            P("dp", "ctx", None),
            P("dp", None),
            P("dp", None),
            P("dp", None),
            P(None, "dp"),
            P("dp"),
            P("dp"),
        ),
        check_vma=False,
    )
```
